32 devices in a mesh: dp: 2 (over x), ctx: 4 (over y, core), tp: 4 (over z).
Axes of the slice: x: 2, y: 2, z: 4, core: 2. Of those that a mesh axis runs over, the one named last changes fastest.
Arguments:
- inputs: bfloat16 [2, 2048, 768], P('dp', 'ctx'), may hold values from -6 to 6
- teacher_states: bfloat16 [2, 2048, 768], P('dp', 'ctx'), may hold values from -6 to 6
- lengths: int32 [2], P('dp'), may hold values from 512 to 2048, as said below
- prev_logits: bfloat16 [2, 12, 2048, 2048], P('dp', 'tp', 'ctx'), may hold values from -6 to 6
- w_query: bfloat16 [768, 768], P('dp', 'tp'), may hold values from -0.21875 to 0.21875
- w_key: bfloat16 [768, 768], P('dp', 'tp'), may hold values from -0.21875 to 0.21875
- w_value: bfloat16 [768, 768], P('dp', 'tp'), may hold values from -0.21875 to 0.21875
- w_output: bfloat16 [768, 768], P('tp', 'dp'), may hold values from -2.5 to 2.5
- w_inner: bfloat16 [768, 3072], P('dp', 'tp'), may hold values from -0.21875 to 0.21875
- w_outer: bfloat16 [3072, 768], P('tp', 'dp'), may hold values from -0.15625 to 0.15625
- bias_query: float32 [768], P('tp'), may hold values from -3 to 3
- bias_value: float32 [768], P('tp'), may hold values from -3 to 3
- bias_output: float32 [768], replicated, may hold values from -2 to 2
- bias_inner: float32 [3072], P('tp'), may hold values from -3 to 3
- bias_outer: float32 [768], replicated, may hold values from -2 to 2
- gain_first: float32 [768], replicated, may hold values from 0.5 to 1.5
- shift_first: float32 [768], replicated, may hold values from -2 to 2
- gain_second: float32 [768], replicated, may hold values from 0.5 to 1.5
- shift_second: float32 [768], replicated, may hold values from -2 to 2
Outputs:
- outputs: float32 [2, 2048, 768], P('dp', 'ctx')
- logits: bfloat16 [2, 12, 2048, 2048], P('dp', 'tp', 'ctx')
- loss_value: float32 [], replicated
- grad_inputs: float32 [2, 2048, 768], P('dp', 'ctx')
- grad_logits_in: bfloat16 [2, 12, 2048, 2048], P('dp', 'tp', 'ctx')
- grad_w_query: float32 [768, 768], P('dp', 'tp')
- grad_w_key: float32 [768, 768], P('dp', 'tp')
- grad_w_value: float32 [768, 768], P('dp', 'tp')
- grad_w_output: float32 [768, 768], P('tp', 'dp')
- grad_w_inner: float32 [768, 3072], P('dp', 'tp')
- grad_w_outer: float32 [3072, 768], P('tp', 'dp')
- grad_bias_query: float32 [768], P('tp')
- grad_bias_value: float32 [768], P('tp')
- grad_bias_output: float32 [768], replicated
- grad_bias_inner: float32 [3072], P('tp')
- grad_bias_outer: float32 [768], replicated
- grad_gain_first: float32 [768], replicated
- grad_shift_first: float32 [768], replicated
- grad_gain_second: float32 [768], replicated
- grad_shift_second: float32 [768], replicated
The draws below stay inside these ranges and needn't reach their ends.
Inputs may be any that keep to these rules, and one draw needn't show every extreme that they name: lengths[s] counts the leading valid tokens of sequence s; in every draw some sequence is full, with 2048 valid tokens.
All inputs are finite; a program needn't handle non-finite values.
Results may differ from the reference program's by a relative error of at most 0.018.
Values may be sent and summed in bfloat16 or wider, within the bound.
No kernel may reach another device: no remote copies, remote signals or barrier semaphores. Data moves between devices by JAX's collectives and lax.ppermute only.
A program may use at most 128 MiB of HBM per device.

```python
import math
from functools import partial
import jax
import jax.numpy as jnp
from jax import lax

D = 768
H = 12
DH = 64
FF = 3072
BLK = 256
SEQ_LEN = 2048
SEQS = 2
TOKENS = 4096


def draw_lengths(key, part):
    first, second = jax.random.split(jax.random.fold_in(key, 11))
    base = jax.random.randint(first, (SEQS,), SEQ_LEN // 4, SEQ_LEN + 1)
    chosen = jax.random.randint(second, (), 0, SEQS)
    return jnp.where(jnp.arange(SEQS) == chosen, SEQ_LEN, base).astype(jnp.int32)


def block_levels(stream_key, extent, cuts, low, high):
    loudness, own = 1.0, jax.random.fold_in(stream_key, 6)
    for dim, parts in cuts:
        steps = jnp.exp(jax.random.uniform(jax.random.fold_in(own, dim), (parts,), jnp.float32, low / len(cuts), high / len(cuts)))
        loudness = loudness * jnp.repeat(steps, extent[dim] // parts).reshape([-1 if axis == dim else 1 for axis in range(len(extent))])
    return loudness


def noise(rng, dims, width, most, shards=(), held_as=jnp.bfloat16):
    drawn = jax.random.normal(rng, dims, jnp.float32) * width
    if len(shards) > 0:
        drawn = block_levels(rng, dims, shards, -0.22, 0.18) * drawn
    return jnp.clip(drawn, min=-most, max=most).astype(held_as)


def setup_inputs(seed: int = 0) -> dict:
    seeds = jax.random.split(jax.random.key(seed), 20)
    return {
        "inputs": noise(seeds[0], (SEQS, SEQ_LEN, D), 1.0, 6.0, ((0, 2), (1, 4))),
        "teacher_states": noise(seeds[1], (SEQS, SEQ_LEN, D), 1.0, 6.0, ((0, 2), (1, 4))),
        "lengths": draw_lengths(jax.random.fold_in(seeds[19], 71), 0),
        "prev_logits": noise(seeds[3], (SEQS, H, SEQ_LEN, SEQ_LEN), 1.0, 6.0, ((0, 2), (1, 4), (2, 4))),
        "w_query": noise(seeds[4], (D, D), D ** -0.5, 0.21875, ((0, 2), (1, 4))),
        "w_key": noise(seeds[5], (D, D), D ** -0.5, 0.21875, ((0, 2), (1, 4))),
        "w_value": noise(seeds[6], (D, D), D ** -0.5, 0.21875, ((0, 2), (1, 4))),
        "w_output": noise(seeds[7], (D, D), (max(4, D // 128)) ** -0.5, 2.5, ((0, 4), (1, 2))),
        "w_inner": noise(seeds[8], (D, FF), D ** -0.5, 0.21875, ((0, 2), (1, 4))),
        "w_outer": noise(seeds[9], (FF, D), (FF // 2) ** -0.5, 0.15625, ((0, 4), (1, 2))),
        "bias_query": noise(seeds[10], (D,), 0.5, 3.0, ((0, 4),), jnp.float32),
        "bias_value": noise(seeds[11], (D,), 0.5, 3.0, ((0, 4),), jnp.float32),
        "bias_output": noise(seeds[12], (D,), 0.3, 2.0, (), jnp.float32),
        "bias_inner": noise(seeds[13], (FF,), 0.5, 3.0, ((0, 4),), jnp.float32),
        "bias_outer": noise(seeds[14], (D,), 0.3, 2.0, (), jnp.float32),
        "gain_first": jnp.clip(1.0 + 0.1 * jax.random.normal(seeds[15], (D,), jnp.float32), 0.5, 1.5),
        "shift_first": noise(seeds[16], (D,), 0.3, 2.0, (), jnp.float32),
        "gain_second": jnp.clip(1.0 + 0.1 * jax.random.normal(seeds[17], (D,), jnp.float32), 0.5, 1.5),
        "shift_second": noise(seeds[18], (D,), 0.3, 2.0, (), jnp.float32),
    }


EPS = 1e-06
MASKED = -1e+30
HIGH = lax.Precision.HIGHEST

@jax.custom_vjp
def low(v):
    return lax.optimization_barrier(v.astype(jnp.bfloat16)).astype(jnp.float32)

@jax.custom_vjp
def low_back(v):
    return v

def low_keep(v):
    return (low(v), None)

def low_pass(kept, grad):
    return (grad,)

def back_keep(v):
    return (v, None)

def back_low(kept, grad):
    return (low(grad),)
low.defvjp(low_keep, low_pass)
low_back.defvjp(back_keep, back_low)

def product(left, right):
    return jnp.dot(left, right, precision=HIGH, preferred_element_type=jnp.float32)

def layer_norm(total, gain_vec, shift_vec):
    center = total - lax.optimization_barrier(jnp.mean(total, -1, keepdims=True))
    spread = lax.rsqrt(lax.optimization_barrier(jnp.mean(center * center, -1, keepdims=True)) + EPS)
    return center * spread * gain_vec + shift_vec

def attend_block(keys_head, values_head, seq_length, items):
    query_block, prior_block, start = items
    block_rows = query_block.shape[1]
    score_scale = 1.0 / math.sqrt(DH)
    raw_scores = jnp.einsum('hrd,hkd->hrk', query_block, keys_head, precision=HIGH)
    scores = low_back(prior_block.astype(jnp.float32) + raw_scores * score_scale)
    row_pos = start + jnp.arange(block_rows, dtype=jnp.int32)
    key_pos = jnp.arange(SEQ_LEN, dtype=jnp.int32)
    allowed = (key_pos[None, :] // BLK <= row_pos[:, None] // BLK) & (key_pos[None, :] < seq_length)
    masked = jnp.where(allowed[None], scores, MASKED)
    row_top = lax.optimization_barrier(jnp.max(masked, -1, keepdims=True))
    exponent = jnp.exp(masked - row_top)
    probs = exponent / lax.optimization_barrier(jnp.sum(exponent, -1, keepdims=True))
    context = jnp.einsum('hrk,hkd->rhd', low(probs), values_head, precision=HIGH)
    return context.reshape(block_rows, D)

def one_sequence(tokens, prior_logits, seq_length, target, parameters):
    w_query, w_key, w_value, w_output, w_inner, w_outer, bias_query, bias_value, bias_output, bias_inner, bias_outer, gain_first, shift_first, gain_second, shift_second = parameters
    block_rows = min(512, SEQ_LEN)
    block_count = SEQ_LEN // block_rows
    query_all = low(low_back(product(tokens, w_query)) + bias_query)
    key_all = low(low_back(product(tokens, w_key)))
    value_all = low(low_back(product(tokens, w_value)) + bias_value)
    query_head = query_all.reshape(SEQ_LEN, H, DH).transpose(1, 0, 2)
    keys_head = key_all.reshape(SEQ_LEN, H, DH).transpose(1, 0, 2)
    values_head = value_all.reshape(SEQ_LEN, H, DH).transpose(1, 0, 2)
    query_blocks = query_head.reshape(H, block_count, block_rows, DH).transpose(1, 0, 2, 3)
    prior_blocks = prior_logits.reshape(H, block_count, block_rows, SEQ_LEN).transpose(1, 0, 2, 3)
    starts = jnp.arange(block_count, dtype=jnp.int32) * block_rows
    block_fn = jax.checkpoint(partial(attend_block, keys_head, values_head, seq_length))
    context_blocks = lax.map(block_fn, (query_blocks, prior_blocks, starts))
    context = low(low_back(context_blocks.reshape(SEQ_LEN, D)))
    attended = low_back(product(context, w_output)) + bias_output
    hidden = layer_norm(tokens + attended, gain_first, shift_first)
    pre_act = low_back(product(low(hidden), w_inner)) + bias_inner
    act = low(jax.nn.gelu(pre_act, approximate=False))
    fed = low_back(product(act, w_outer)) + bias_outer
    result = layer_norm(hidden + fed, gain_second, shift_second)
    valid_rows = (jnp.arange(SEQ_LEN, dtype=jnp.int32) < seq_length).astype(jnp.float32)
    deviation = result - target
    squared = jnp.sum(valid_rows[:, None] * deviation * deviation)
    return (result, squared)

def sequence_logits(w_query, w_key, bias_query, items):
    tokens, prior_logits = items
    block_rows = min(512, SEQ_LEN)
    block_count = SEQ_LEN // block_rows
    score_scale = 1.0 / math.sqrt(DH)
    query_all = low(product(tokens, w_query) + bias_query)
    key_all = low(product(tokens, w_key))
    query_head = query_all.reshape(SEQ_LEN, H, DH).transpose(1, 0, 2)
    keys_head = key_all.reshape(SEQ_LEN, H, DH).transpose(1, 0, 2)
    query_blocks = query_head.reshape(H, block_count, block_rows, DH).transpose(1, 0, 2, 3)
    prior_blocks = prior_logits.reshape(H, block_count, block_rows, SEQ_LEN).transpose(1, 0, 2, 3)

    def block_logits(pair):
        query_block, prior_block = pair
        raw_scores = jnp.einsum('hrd,hkd->hrk', query_block, keys_head, precision=HIGH)
        return (prior_block.astype(jnp.float32) + raw_scores * score_scale).astype(jnp.bfloat16)
    blocks = lax.map(block_logits, (query_blocks, prior_blocks))
    return blocks.transpose(1, 0, 2, 3).reshape(H, SEQ_LEN, SEQ_LEN)

def reference(inputs, teacher_states, lengths, prev_logits, w_query, w_key, w_value, w_output, w_inner, w_outer, bias_query, bias_value, bias_output, bias_inner, bias_outer, gain_first, shift_first, gain_second, shift_second):
    parameters = (w_query.astype(jnp.float32), w_key.astype(jnp.float32), w_value.astype(jnp.float32), w_output.astype(jnp.float32), w_inner.astype(jnp.float32), w_outer.astype(jnp.float32), bias_query, bias_value, bias_output, bias_inner, bias_outer, gain_first, shift_first, gain_second, shift_second)
    inputs_wide = inputs.astype(jnp.float32)
    targets_wide = teacher_states.astype(jnp.float32)
    count = jnp.sum(lengths).astype(jnp.float32)

    def objective(parameters, inputs_wide, prev_logits):

        def advance(running, items):
            tokens, prior_logits, seq_length, target = items
            result, squared = jax.checkpoint(one_sequence)(tokens, prior_logits, seq_length, target, parameters)
            return (running + squared, result)
        running, results = lax.scan(advance, jnp.float32(0.0), (inputs_wide, prev_logits, lengths, targets_wide))
        loss_value = running / (count * D)
        return (loss_value * (TOKENS * D), (results, loss_value))
    scaled, backward, (results, loss_value) = jax.vjp(objective, parameters, inputs_wide, prev_logits, has_aux=True)
    grad_params, grad_inputs, grad_logits_in = backward(jnp.ones_like(scaled))
    logits = lax.map(partial(sequence_logits, parameters[0], parameters[1], parameters[6]), (inputs_wide, prev_logits))
    return (results, logits, loss_value, grad_inputs, grad_logits_in.astype(jnp.bfloat16), grad_params[0], grad_params[1], grad_params[2], grad_params[3], grad_params[4], grad_params[5], grad_params[6], grad_params[7], grad_params[8], grad_params[9], grad_params[10], grad_params[11], grad_params[12], grad_params[13], grad_params[14])
```

```python
from functools import partial
import math

import jax
import jax.numpy as jnp
from jax import lax
from jax.sharding import PartitionSpec as P

BLK = 256


EPS = 1e-06
MASKED = -1e30


def norm_forward(total, gain_vec, shift_vec):
    center = total - jnp.mean(total, -1, keepdims=True)
    spread = lax.rsqrt(jnp.mean(center * center, -1, keepdims=True) + EPS)
    normed = center * spread
    return (normed, spread, normed * gain_vec + shift_vec)


def norm_backward(gradient, normed, spread, gain_vec):
    scaled = gradient * gain_vec
    inner_term = (
        scaled
        - jnp.mean(scaled, -1, keepdims=True)
        - normed * jnp.mean(scaled * normed, -1, keepdims=True)
    )
    return (inner_term * spread, jnp.sum(gradient * normed, 0), jnp.sum(gradient, 0))


F32, BF16 = jnp.float32, jnp.bfloat16


def dot32(left, right, dims):
    return lax.dot_general(left, right, (dims, ((), ())), preferred_element_type=F32)


def shifted(block, axis, step):
    size = lax.axis_size(axis)
    return lax.ppermute(block, axis, [(i, (i + step) % size) for i in range(size)])


def flipped(block, axis, bit):
    size = lax.axis_size(axis)
    return lax.ppermute(block, axis, [(i, i ^ bit) for i in range(size)])


def sum_all(vector, axes):
    for axis in axes:
        bit = 1
        while bit < lax.axis_size(axis):
            vector = vector + flipped(vector, axis, bit)
            bit *= 2
    return vector


def gather_weight(shard, dim):
    if lax.axis_size("dp") != 2:
        return lax.all_gather(shard, "dp", axis=dim, tiled=True)
    half = shard.shape[0] // 2
    side = lax.rem(lax.axis_index("ctx"), 2)
    mine = lax.dynamic_slice_in_dim(shard, side * half, half, 0)
    near = flipped(mine, "dp", 1)
    far = flipped(near, "ctx", 1)
    other = jnp.where(side == 0, jnp.concatenate([near, far], 0), jnp.concatenate([far, near], 0))
    first = lax.axis_index("dp") == 0
    return jnp.where(
        first, jnp.concatenate([shard, other], dim), jnp.concatenate([other, shard], dim)
    )


def reduce_weight(gradient, dim):
    if lax.axis_size("dp") != 2:
        summed = lax.psum(gradient.astype(BF16), "ctx")
        return lax.psum_scatter(summed, "dp", scatter_dimension=dim, tiled=True).astype(F32)
    side = lax.rem(lax.axis_index("ctx"), 2)
    place = lax.axis_index("dp")
    half = gradient.shape[0] // 2
    if dim == 0:
        half //= 2
        parts = gradient.reshape((2, 2, half) + gradient.shape[1:])
        parts = parts.transpose((1, 0, 2, 3))
    else:
        width = gradient.shape[1] // 2
        parts = jnp.stack(
            [
                jnp.stack([gradient[s * half : (s + 1) * half, p * width : (p + 1) * width] for p in (0, 1)])
                for s in (0, 1)
            ]
        )
    keep = lax.dynamic_index_in_dim(parts, side, 0, False)
    give = lax.dynamic_index_in_dim(parts, 1 - side, 0, False).astype(BF16)
    chip = keep + flipped(give, "ctx", 1).astype(F32)
    keep = lax.dynamic_index_in_dim(chip, place, 0, False)
    give = lax.dynamic_index_in_dim(chip, 1 - place, 0, False).astype(BF16)
    total = keep + flipped(give, "dp", 1).astype(F32)
    bit = 2
    while bit < lax.axis_size("ctx"):
        rounded = total.astype(BF16)
        total = rounded.astype(F32) + flipped(rounded, "ctx", bit).astype(F32)
        bit *= 2
    total = total.astype(BF16)
    far = flipped(total, "ctx", 1)
    return jnp.where(
        side == 0, jnp.concatenate([total, far], 0), jnp.concatenate([far, total], 0)
    ).astype(F32)


def gather_parts(block):
    size = lax.axis_size("ctx")
    place = lax.axis_index("ctx")
    held, order, bit = block[None], [0], size // 2
    while bit:
        held = jnp.concatenate([held, flipped(held, "ctx", bit)], 0)
        order = order + [e ^ bit for e in order]
        bit //= 2
    where_of = {e: i for i, e in enumerate(order)}
    lookup = jnp.asarray([where_of[e] for e in range(size)], jnp.int32)
    return jnp.concatenate(
        [lax.dynamic_index_in_dim(held, lookup[place ^ p], 0, False) for p in range(size)], 0
    )


def scatter_parts(total):
    size = lax.axis_size("ctx")
    place = lax.axis_index("ctx")
    blocks = total.reshape((size, total.shape[0] // size) + total.shape[1:])
    held = {e: lax.dynamic_index_in_dim(blocks, place ^ e, 0, False) for e in range(size)}
    bit = 1
    while bit < size:
        sent = [e for e in held if e & bit]
        moved = flipped(jnp.stack([held[e].astype(BF16) for e in sent]), "ctx", bit)
        for i, e in enumerate(sent):
            held[e ^ bit] = held[e ^ bit] + moved[i].astype(F32)
            del held[e]
        bit *= 2
    return held[0]


def rows_sum(total):
    size = lax.axis_size("tp")
    place = lax.axis_index("tp")
    rows = total.shape[0] // size
    low = total.astype(BF16)
    kept = lax.dynamic_slice_in_dim(total, place * rows, rows, 0)
    for step in range(1, size):
        target = lax.rem(place + step, size)
        moved = shifted(lax.dynamic_slice_in_dim(low, target * rows, rows, 0), "tp", step)
        kept = kept + moved.astype(F32)
    return kept


def rows_gather(block):
    size = lax.axis_size("tp")
    place = lax.axis_index("tp")
    rows = block.shape[0]
    held = lax.dynamic_update_slice_in_dim(
        jnp.zeros((size * rows,) + block.shape[1:], block.dtype), block, place * rows, 0
    )
    for step in range(1, size):
        source = lax.rem(place - step + size, size)
        held = lax.dynamic_update_slice_in_dim(held, shifted(block, "tp", step), source * rows, 0)
    return held


def per_device(
    inputs,
    teacher_states,
    lengths,
    prev_logits,
    w_query,
    w_key,
    w_value,
    w_output,
    w_inner,
    w_outer,
    bias_query,
    bias_value,
    bias_output,
    bias_inner,
    bias_outer,
    gain_first,
    shift_first,
    gain_second,
    shift_second,
):
    tokens = inputs[0]
    row_count, model_width = tokens.shape
    heads_local = prev_logits.shape[1]
    key_count = prev_logits.shape[3]
    width_local = w_query.shape[1]
    head_width = width_local // heads_local
    score_scale = 1.0 / math.sqrt(head_width)
    seq_length = lengths[0]
    ctx_place, tp_place = lax.axis_index("ctx"), lax.axis_index("tp")
    tp_size = lax.axis_size("tp")
    part_rows = row_count // tp_size
    all_count = sum_all(seq_length.astype(F32), ("dp",))

    full_qkv = gather_weight(jnp.concatenate([w_query, w_key, w_value], 1), 0)
    full_output = gather_weight(w_output, 1)
    full_inner = gather_weight(w_inner, 0)
    full_outer = gather_weight(w_outer, 1)

    row_pos = ctx_place * row_count + jnp.arange(row_count, dtype=jnp.int32)
    key_pos = jnp.arange(key_count, dtype=jnp.int32)
    allowed = (key_pos[None, :] // BLK <= row_pos[:, None] // BLK) & (key_pos[None, :] < seq_length)

    def own_rows(array):
        return lax.dynamic_slice_in_dim(array, tp_place * part_rows, part_rows, 0)

    projected = dot32(tokens, full_qkv, ((1,), (0,)))
    query_local = (projected[:, :width_local] + bias_query).astype(BF16)
    kv_local = jnp.concatenate(
        [projected[:, width_local : 2 * width_local], projected[:, 2 * width_local :] + bias_value], 1
    ).astype(BF16)
    kv_all = gather_parts(kv_local)
    query_heads = query_local.reshape(row_count, heads_local, head_width)
    key_heads = kv_all[:, :width_local].reshape(key_count, heads_local, head_width)
    value_heads = kv_all[:, width_local:].reshape(key_count, heads_local, head_width)
    prior_logits = prev_logits[0]

    def score_block():
        raw_scores = jnp.einsum(
            "rhd,khd->hrk", query_heads, key_heads, preferred_element_type=F32
        )
        return prior_logits.astype(F32) + raw_scores * score_scale

    scores = score_block()
    masked = jnp.where(allowed[None], scores, MASKED)
    row_top = jnp.max(masked, -1, keepdims=True)
    exponent = jnp.exp(masked - row_top)
    row_total = jnp.sum(exponent, -1, keepdims=True)
    probs = exponent / row_total
    log_total = row_top + jnp.log(row_total)
    context = (
        jnp.einsum("hrk,khd->rhd", probs.astype(BF16), value_heads, preferred_element_type=F32)
        .reshape(row_count, width_local)
        .astype(BF16)
    )
    attended = rows_sum(dot32(context, full_output, ((1,), (0,))))
    first_sum = own_rows(tokens).astype(F32) + attended + bias_output
    normed_first, spread_first, hidden = norm_forward(first_sum, gain_first, shift_first)
    hidden_low = rows_gather(hidden.astype(BF16))
    pre_act = dot32(hidden_low, full_inner, ((1,), (0,))) + bias_inner
    act_low = jax.nn.gelu(pre_act, approximate=False).astype(BF16)
    fed = rows_sum(dot32(act_low, full_outer, ((1,), (0,))))
    second_sum = hidden + fed + bias_outer
    normed_second, spread_second, result = norm_forward(second_sum, gain_second, shift_second)
    valid_rows = (own_rows(row_pos) < seq_length).astype(F32)
    deviation = result - own_rows(teacher_states[0]).astype(F32)
    local_squared = jnp.sum(valid_rows[:, None] * deviation * deviation)
    token_total = row_count * lax.axis_size("ctx") * lax.axis_size("dp")
    d_out = 2.0 * token_total / all_count * valid_rows[:, None] * deviation
    d_second, grad_gain_second, grad_shift_second = norm_backward(
        d_out, normed_second, spread_second, gain_second
    )
    grad_bias_outer = jnp.sum(d_second, 0)
    d_second_low = rows_gather(d_second.astype(BF16))
    result_all = rows_gather(result.astype(BF16)).astype(F32)
    d_act = dot32(d_second_low, full_outer, ((1,), (1,)))
    gelu_back = jax.vjp(partial(jax.nn.gelu, approximate=False), pre_act)[1]
    d_pre = gelu_back(d_act)[0]
    grad_bias_inner = jnp.sum(d_pre, 0)
    d_pre_low = d_pre.astype(BF16)
    d_hidden = d_second + rows_sum(dot32(d_pre_low, full_inner, ((1,), (1,))))
    d_first, grad_gain_first, grad_shift_first = norm_backward(
        d_hidden, normed_first, spread_first, gain_first
    )
    grad_bias_output = jnp.sum(d_first, 0)
    d_first_low = rows_gather(d_first.astype(BF16))
    shard_outer = reduce_weight(dot32(act_low, d_second_low, ((0,), (0,))), 1)
    shard_inner = reduce_weight(dot32(hidden_low, d_pre_low, ((0,), (0,))), 0)
    d_context = dot32(d_first_low, full_output, ((1,), (1,))).astype(BF16)
    shard_output = reduce_weight(dot32(context, d_first_low, ((0,), (0,))), 1)
    d_context_heads = d_context.reshape(row_count, heads_local, head_width)
    probs_again = jnp.where(allowed[None], jnp.exp(score_block() - log_total), 0.0)
    d_probs = jnp.einsum(
        "rhd,khd->hrk", d_context_heads, value_heads, preferred_element_type=F32
    )
    d_scores = probs_again * (d_probs - jnp.sum(probs_again * d_probs, -1, keepdims=True))
    d_scores_low = d_scores.astype(BF16)
    d_query = score_scale * jnp.einsum(
        "hrk,khd->rhd", d_scores_low, key_heads, preferred_element_type=F32
    ).reshape(row_count, width_local)
    key_part = score_scale * jnp.einsum(
        "hrk,rhd->khd", d_scores_low, query_heads, preferred_element_type=F32
    ).reshape(key_count, width_local)
    value_part = jnp.einsum(
        "hrk,rhd->khd", probs_again.astype(BF16), d_context_heads, preferred_element_type=F32
    ).reshape(key_count, width_local)
    d_kv = scatter_parts(jnp.concatenate([key_part, value_part], 1))
    d_qkv_low = jnp.concatenate([d_query, d_kv], 1).astype(BF16)
    tokens_part = rows_sum(dot32(d_qkv_low, full_qkv, ((1,), (1,))))
    grad_inputs = rows_gather((d_first + tokens_part).astype(BF16)).astype(F32)
    shard_qkv = reduce_weight(dot32(tokens, d_qkv_low, ((0,), (0,))), 0)

    places = jnp.arange(tp_size)[:, None] == tp_place
    placed_bias = jnp.where(places, grad_bias_inner[None], 0.0).reshape(-1)
    early = jnp.concatenate(
        [
            grad_bias_output,
            grad_bias_outer,
            grad_gain_first,
            grad_shift_first,
            grad_gain_second,
            grad_shift_second,
            jnp.full((128,), local_squared),
            placed_bias,
        ]
    )
    early = sum_all(early, ("dp", "ctx", "tp"))
    width = model_width
    sums = [early[i * width : (i + 1) * width] for i in range(6)]
    loss_value = early[6 * width] / (all_count * width)
    sum_bias_inner = lax.dynamic_slice_in_dim(
        early, 6 * width + 128 + tp_place * grad_bias_inner.shape[0], grad_bias_inner.shape[0], 0
    )
    late = sum_all(
        jnp.concatenate([jnp.sum(d_query, 0), jnp.sum(d_kv[:, width_local:], 0)]), ("dp", "ctx")
    )
    return (
        result_all[None],
        scores.astype(BF16)[None],
        loss_value,
        grad_inputs[None],
        d_scores_low[None],
        shard_qkv[:, :width_local],
        shard_qkv[:, width_local : 2 * width_local],
        shard_qkv[:, 2 * width_local :],
        shard_output,
        shard_inner,
        shard_outer,
        late[:width_local],
        late[width_local:],
        sums[0],
        sum_bias_inner,
        sums[1],
        sums[2],
        sums[3],
        sums[4],
        sums[5],
    )


def solution(mesh):
    placed = (
        P("dp", "ctx", None),
        P("dp", "ctx", None),
        P("dp"),
        P("dp", "tp", "ctx", None),
        P("dp", "tp"),
        P("dp", "tp"),
        P("dp", "tp"),
        P("tp", "dp"),
        P("dp", "tp"),
        P("tp", "dp"),
        P("tp"),
        P("tp"),
        P(),
        P("tp"),
        P(),
        P(),
        P(),
        P(),
        P(),
    )
    return jax.shard_map(
        per_device,
        mesh=mesh,
        in_specs=placed,
        out_specs=(
            P("dp", "ctx", None),
            P("dp", "tp", "ctx", None),
            P(),
            P("dp", "ctx", None),
            P("dp", "tp", "ctx", None),
            P("dp", "tp"),
            P("dp", "tp"),
            P("dp", "tp"),
            P("tp", "dp"),
            P("dp", "tp"),
            P("tp", "dp"),
            P("tp"),
            P("tp"),
            P(),
            P("tp"),
            P(),
            P(),
            P(),
            P(),
            P(),
        ),
        check_vma=False,
    )
```

```python
from functools import partial
import math

import jax
import jax.numpy as jnp
from jax import lax
from jax.experimental import pallas as pl
from jax.experimental.pallas import tpu as pltpu
from jax.sharding import PartitionSpec as P

BLK = 256


EPS = 1e-06
MASKED = -1e30


def norm_forward(total, gain_vec, shift_vec):
    center = total - jnp.mean(total, -1, keepdims=True)
    spread = lax.rsqrt(jnp.mean(center * center, -1, keepdims=True) + EPS)
    normed = center * spread
    return (normed, spread, normed * gain_vec + shift_vec)


def norm_backward(gradient, normed, spread, gain_vec):
    scaled = gradient * gain_vec
    inner_term = (
        scaled
        - jnp.mean(scaled, -1, keepdims=True)
        - normed * jnp.mean(scaled * normed, -1, keepdims=True)
    )
    return (inner_term * spread, jnp.sum(gradient * normed, 0), jnp.sum(gradient, 0))


F32, BF16 = jnp.float32, jnp.bfloat16


def dot32(left, right, dims):
    return lax.dot_general(left, right, (dims, ((), ())), preferred_element_type=F32)


def shifted(block, axis, step):
    size = lax.axis_size(axis)
    return lax.ppermute(block, axis, [(i, (i + step) % size) for i in range(size)])


def flipped(block, axis, bit):
    size = lax.axis_size(axis)
    return lax.ppermute(block, axis, [(i, i ^ bit) for i in range(size)])


def sum_all(vector, axes):
    for axis in axes:
        bit = 1
        while bit < lax.axis_size(axis):
            vector = vector + flipped(vector, axis, bit)
            bit *= 2
    return vector


def gather_weight(shard, dim):
    if lax.axis_size("dp") != 2:
        return lax.all_gather(shard, "dp", axis=dim, tiled=True)
    half = shard.shape[0] // 2
    side = lax.rem(lax.axis_index("ctx"), 2)
    mine = lax.dynamic_slice_in_dim(shard, side * half, half, 0)
    near = flipped(mine, "dp", 1)
    far = flipped(near, "ctx", 1)
    other = jnp.where(side == 0, jnp.concatenate([near, far], 0), jnp.concatenate([far, near], 0))
    first = lax.axis_index("dp") == 0
    return jnp.where(
        first, jnp.concatenate([shard, other], dim), jnp.concatenate([other, shard], dim)
    )


def reduce_weight(gradient, dim):
    if lax.axis_size("dp") != 2:
        summed = lax.psum(gradient.astype(BF16), "ctx")
        return lax.psum_scatter(summed, "dp", scatter_dimension=dim, tiled=True).astype(F32)
    side = lax.rem(lax.axis_index("ctx"), 2)
    place = lax.axis_index("dp")
    half = gradient.shape[0] // 2
    if dim == 0:
        half //= 2
        parts = gradient.reshape((2, 2, half) + gradient.shape[1:])
        parts = parts.transpose((1, 0, 2, 3))
    else:
        width = gradient.shape[1] // 2
        parts = jnp.stack(
            [
                jnp.stack([gradient[s * half : (s + 1) * half, p * width : (p + 1) * width] for p in (0, 1)])
                for s in (0, 1)
            ]
        )
    keep = lax.dynamic_index_in_dim(parts, side, 0, False)
    give = lax.dynamic_index_in_dim(parts, 1 - side, 0, False).astype(BF16)
    chip = keep + flipped(give, "ctx", 1).astype(F32)
    keep = lax.dynamic_index_in_dim(chip, place, 0, False)
    give = lax.dynamic_index_in_dim(chip, 1 - place, 0, False).astype(BF16)
    total = keep + flipped(give, "dp", 1).astype(F32)
    bit = 2
    while bit < lax.axis_size("ctx"):
        rounded = total.astype(BF16)
        total = rounded.astype(F32) + flipped(rounded, "ctx", bit).astype(F32)
        bit *= 2
    total = total.astype(BF16)
    far = flipped(total, "ctx", 1)
    return jnp.where(
        side == 0, jnp.concatenate([total, far], 0), jnp.concatenate([far, total], 0)
    ).astype(F32)


def gather_parts(block):
    size = lax.axis_size("ctx")
    place = lax.axis_index("ctx")
    held, order, bit = block[None], [0], size // 2
    while bit:
        held = jnp.concatenate([held, flipped(held, "ctx", bit)], 0)
        order = order + [e ^ bit for e in order]
        bit //= 2
    where_of = {e: i for i, e in enumerate(order)}
    lookup = jnp.asarray([where_of[e] for e in range(size)], jnp.int32)
    return jnp.concatenate(
        [lax.dynamic_index_in_dim(held, lookup[place ^ p], 0, False) for p in range(size)], 0
    )


def scatter_parts(blocks):
    size = lax.axis_size("ctx")
    place = lax.axis_index("ctx")
    held = {e: lax.dynamic_index_in_dim(blocks, place ^ e, 0, False).astype(F32) for e in range(size)}
    bit = 1
    while bit < size:
        sent = [e for e in held if e & bit]
        moved = flipped(jnp.stack([held[e].astype(BF16) for e in sent]), "ctx", bit)
        for i, e in enumerate(sent):
            held[e ^ bit] = held[e ^ bit] + moved[i].astype(F32)
            del held[e]
        bit *= 2
    return held[0]


def rows_turn(block):
    size = lax.axis_size("tp")
    place = lax.axis_index("tp")
    blocks = block.reshape((size, block.shape[0] // size) + block.shape[1:])
    return jnp.concatenate(
        [
            lax.dynamic_index_in_dim(blocks, lax.rem(place - e + size, size), 0, False)
            for e in range(size)
        ],
        0,
    )


def rows_sum(total):
    size = lax.axis_size("tp")
    rows = total.shape[0] // size
    low = total.astype(BF16)
    moved = [shifted(low[e * rows : (e + 1) * rows], "tp", size - e) for e in range(1, size)]
    kept = total[:rows]
    for block in moved:
        kept = kept + block.astype(F32)
    return kept


def rows_gather(block):
    size = lax.axis_size("tp")
    return jnp.concatenate([block] + [shifted(block, "tp", e) for e in range(1, size)], 0)


TILE = 128


def attend_kernel(heads, limits, query, kv, prior, logits, weights, context, inverse):
    limit = limits[pl.program_id(0)]
    width = query.shape[1]
    size = width // heads
    keys = kv.shape[0]
    column = lax.broadcasted_iota(jnp.int32, (query.shape[0], keys), 1)
    for h in range(heads):
        own = slice(h * size, (h + 1) * size)
        raw = lax.dot_general(
            query[:, own], kv[:, own], (((1,), (1,)), ((), ())), preferred_element_type=F32
        )
        score = prior[0, h].astype(F32) + raw
        logits[0, h] = score.astype(BF16)
        masked = jnp.where(column < limit, score, MASKED)
        exponent = jnp.exp(masked - jnp.max(masked, -1, keepdims=True))
        scale = 1.0 / jnp.sum(exponent, -1, keepdims=True)
        low = exponent.astype(BF16)
        weights[h] = low
        mixed = jnp.dot(low, kv[:, width + h * size : width + (h + 1) * size], preferred_element_type=F32)
        context[:, own] = (mixed * scale).astype(BF16)
        inverse[:, own] = jnp.broadcast_to(scale, (query.shape[0], size))


def attend(query, kv, prior, limits, heads):
    rows, width = query.shape
    keys = kv.shape[0]
    tile = lambda i, lim: (i, 0)
    whole = lambda i, lim: (0, 0)
    cube = lambda i, lim: (0, i, 0)
    quad = lambda i, lim: (0, 0, i, 0)
    return pl.pallas_call(
        partial(attend_kernel, heads),
        grid_spec=pltpu.PrefetchScalarGridSpec(
            num_scalar_prefetch=1,
            grid=(rows // TILE,),
            in_specs=[
                pl.BlockSpec((TILE, width), tile),
                pl.BlockSpec((keys, 2 * width), whole),
                pl.BlockSpec((1, heads, TILE, keys), quad),
            ],
            out_specs=[
                pl.BlockSpec((1, heads, TILE, keys), quad),
                pl.BlockSpec((heads, TILE, keys), cube),
                pl.BlockSpec((TILE, width), tile),
                pl.BlockSpec((TILE, width), tile),
            ],
        ),
        out_shape=[
            jax.ShapeDtypeStruct((1, heads, rows, keys), BF16),
            jax.ShapeDtypeStruct((heads, rows, keys), BF16),
            jax.ShapeDtypeStruct((rows, width), BF16),
            jax.ShapeDtypeStruct((rows, width), F32),
        ],
        name="attend",
    )(limits, query, kv, prior)


def attend_back_kernel(
    heads, scale, weights, kv, context, d_context, d_context_t, query_t, d_scores, d_query, d_kv, total
):
    width = context.shape[1]
    size = width // heads
    step = pl.program_id(0)

    @pl.when(step == 0)
    def _():
        total[...] = jnp.zeros_like(total)

    for h in range(heads):
        own = slice(h * size, (h + 1) * size)
        other = slice(width + h * size, width + (h + 1) * size)
        low = weights[h]
        d_weights = lax.dot_general(
            d_context[:, own], kv[:, other], (((1,), (1,)), ((), ())), preferred_element_type=F32
        )
        mean = jnp.sum(
            d_context[:, own].astype(F32) * context[:, own].astype(F32), -1, keepdims=True
        )
        change = (low.astype(F32) * (d_weights - mean)).astype(BF16)
        d_scores[0, h] = change
        d_query[:, own] = scale * jnp.dot(change, kv[:, own], preferred_element_type=F32)
        total[own, :] += jnp.dot(query_t[own, :], change, preferred_element_type=F32)
        total[other, :] += jnp.dot(d_context_t[own, :], low, preferred_element_type=F32)

    @pl.when(step == pl.num_programs(0) - 1)
    def _():
        columns = d_kv.shape[2]
        for p in range(d_kv.shape[0]):
            d_kv[p] = total[:, p * columns : (p + 1) * columns].astype(BF16)


def attend_back(weights, kv, context, d_context, query, scale, places):
    heads, rows, keys = weights.shape
    width = context.shape[1]
    tile = lambda i: (i, 0)
    turned = lambda i: (0, i)
    whole = lambda i: (0, 0)
    return pl.pallas_call(
        partial(attend_back_kernel, heads, scale),
        grid=(rows // TILE,),
        in_specs=[
            pl.BlockSpec((heads, TILE, keys), lambda i: (0, i, 0)),
            pl.BlockSpec((keys, 2 * width), whole),
            pl.BlockSpec((TILE, width), tile),
            pl.BlockSpec((TILE, width), tile),
            pl.BlockSpec((width, TILE), turned),
            pl.BlockSpec((width, TILE), turned),
        ],
        out_specs=[
            pl.BlockSpec((1, heads, TILE, keys), lambda i: (0, 0, i, 0)),
            pl.BlockSpec((TILE, width), tile),
            pl.BlockSpec((places, 2 * width, keys // places), lambda i: (0, 0, 0)),
        ],
        out_shape=[
            jax.ShapeDtypeStruct((1, heads, rows, keys), BF16),
            jax.ShapeDtypeStruct((rows, width), F32),
            jax.ShapeDtypeStruct((places, 2 * width, keys // places), BF16),
        ],
        scratch_shapes=[pltpu.VMEM((2 * width, keys), F32)],
        name="attend_back",
    )(weights, kv, context, d_context, d_context.T, query.T)


def per_device(
    inputs,
    teacher_states,
    lengths,
    prev_logits,
    w_query,
    w_key,
    w_value,
    w_output,
    w_inner,
    w_outer,
    bias_query,
    bias_value,
    bias_output,
    bias_inner,
    bias_outer,
    gain_first,
    shift_first,
    gain_second,
    shift_second,
):
    tokens = inputs[0]
    row_count, model_width = tokens.shape
    heads_local = prev_logits.shape[1]
    width_local = w_query.shape[1]
    head_width = width_local // heads_local
    score_scale = 1.0 / math.sqrt(head_width)
    seq_length = lengths[0]
    ctx_place, tp_place = lax.axis_index("ctx"), lax.axis_index("tp")
    tp_size = lax.axis_size("tp")
    part_rows = row_count // tp_size
    all_count = sum_all(seq_length.astype(F32), ("dp",))

    full_qkv = gather_weight(jnp.concatenate([w_query, w_key, w_value], 1), 0)
    full_output = gather_weight(w_output, 1)
    full_inner = gather_weight(w_inner, 0)
    full_outer = gather_weight(w_outer, 1)

    row_pos = ctx_place * row_count + jnp.arange(row_count, dtype=jnp.int32)
    tile_pos = row_pos[::TILE]
    limits = jnp.minimum((tile_pos // BLK + 1) * BLK, seq_length)

    def own_rows(array):
        return lax.dynamic_slice_in_dim(array, tp_place * part_rows, part_rows, 0)

    projected = dot32(tokens, full_qkv, ((1,), (0,)))
    query_local = (projected[:, :width_local] + bias_query).astype(BF16)
    kv_local = jnp.concatenate(
        [projected[:, width_local : 2 * width_local], projected[:, 2 * width_local :] + bias_value], 1
    ).astype(BF16)
    kv_all = gather_parts(kv_local)
    query_scaled = (query_local.astype(F32) * score_scale).astype(BF16)
    logits, weights, context, inverse = attend(query_scaled, kv_all, prev_logits, limits, heads_local)
    context_turned = rows_turn(context)
    attended = rows_sum(dot32(context_turned, full_output, ((1,), (0,))))
    first_sum = own_rows(tokens).astype(F32) + attended + bias_output
    normed_first, spread_first, hidden = norm_forward(first_sum, gain_first, shift_first)
    hidden_low = rows_gather(hidden.astype(BF16))
    pre_act = dot32(hidden_low, full_inner, ((1,), (0,))) + bias_inner
    act_low = jax.nn.gelu(pre_act, approximate=False).astype(BF16)
    fed = rows_sum(dot32(act_low, full_outer, ((1,), (0,))))
    second_sum = hidden + fed + bias_outer
    normed_second, spread_second, result = norm_forward(second_sum, gain_second, shift_second)
    valid_rows = (own_rows(row_pos) < seq_length).astype(F32)
    deviation = result - own_rows(teacher_states[0]).astype(F32)
    local_squared = jnp.sum(valid_rows[:, None] * deviation * deviation)
    token_total = row_count * lax.axis_size("ctx") * lax.axis_size("dp")
    d_out = 2.0 * token_total / all_count * valid_rows[:, None] * deviation
    d_second, grad_gain_second, grad_shift_second = norm_backward(
        d_out, normed_second, spread_second, gain_second
    )
    grad_bias_outer = jnp.sum(d_second, 0)
    d_second_low = rows_gather(d_second.astype(BF16))
    result_all = rows_turn(rows_gather(result.astype(BF16))).astype(F32)
    d_act = dot32(d_second_low, full_outer, ((1,), (1,)))
    gelu_back = jax.vjp(partial(jax.nn.gelu, approximate=False), pre_act)[1]
    d_pre = gelu_back(d_act)[0]
    grad_bias_inner = jnp.sum(d_pre, 0)
    d_pre_low = d_pre.astype(BF16)
    d_hidden = d_second + rows_sum(dot32(d_pre_low, full_inner, ((1,), (1,))))
    d_first, grad_gain_first, grad_shift_first = norm_backward(
        d_hidden, normed_first, spread_first, gain_first
    )
    grad_bias_output = jnp.sum(d_first, 0)
    d_first_low = rows_gather(d_first.astype(BF16))
    shard_outer = reduce_weight(dot32(act_low, d_second_low, ((0,), (0,))), 1)
    shard_inner = reduce_weight(dot32(hidden_low, d_pre_low, ((0,), (0,))), 0)
    d_context = rows_turn(dot32(d_first_low, full_output, ((1,), (1,)))) * inverse
    shard_output = reduce_weight(dot32(context_turned, d_first_low, ((0,), (0,))), 1)
    d_scores, d_query, d_kv_parts = attend_back(
        weights, kv_all, context, d_context.astype(BF16), query_scaled, score_scale, lax.axis_size("ctx")
    )
    d_kv = scatter_parts(d_kv_parts)
    d_query_low, d_kv_low = d_query.astype(BF16), d_kv.astype(BF16)
    tokens_part = rows_sum(
        rows_turn(
            dot32(d_query_low, full_qkv[:, :width_local], ((1,), (1,)))
            + dot32(d_kv_low, full_qkv[:, width_local:], ((0,), (1,)))
        )
    )
    grad_inputs = rows_turn(rows_gather((d_first + tokens_part).astype(BF16))).astype(F32)
    shard_qkv = reduce_weight(
        jnp.concatenate(
            [dot32(tokens, d_query_low, ((0,), (0,))), dot32(tokens, d_kv_low, ((0,), (1,)))], 1
        ), 0)

    places = jnp.arange(tp_size)[:, None] == tp_place
    placed_bias = jnp.where(places, grad_bias_inner[None], 0.0).reshape(-1)
    early = jnp.concatenate(
        [
            grad_bias_output,
            grad_bias_outer,
            grad_gain_first,
            grad_shift_first,
            grad_gain_second,
            grad_shift_second,
            jnp.full((128,), local_squared),
            placed_bias,
        ]
    )
    early = sum_all(early, ("dp", "ctx", "tp"))
    width = model_width
    sums = [early[i * width : (i + 1) * width] for i in range(6)]
    loss_value = early[6 * width] / (all_count * width)
    sum_bias_inner = lax.dynamic_slice_in_dim(
        early, 6 * width + 128 + tp_place * grad_bias_inner.shape[0], grad_bias_inner.shape[0], 0
    )
    late = sum_all(
        jnp.concatenate([jnp.sum(d_query, 0), jnp.sum(d_kv[width_local:], 1)]), ("dp", "ctx")
    )
    return (
        result_all[None],
        logits,
        loss_value,
        grad_inputs[None],
        d_scores,
        shard_qkv[:, :width_local],
        shard_qkv[:, width_local : 2 * width_local],
        shard_qkv[:, 2 * width_local :],
        shard_output,
        shard_inner,
        shard_outer,
        late[:width_local],
        late[width_local:],
        sums[0],
        sum_bias_inner,
        sums[1],
        sums[2],
        sums[3],
        sums[4],
        sums[5],
    )


def solution(mesh):
    placed = (
        P("dp", "ctx", None),
        P("dp", "ctx", None),
        P("dp"),
        P("dp", "tp", "ctx", None),
        P("dp", "tp"),
        P("dp", "tp"),
        P("dp", "tp"),
        P("tp", "dp"),
        P("dp", "tp"),
        P("tp", "dp"),
        P("tp"),
        P("tp"),
        P(),
        P("tp"),
        P(),
        P(),
        P(),
        P(),
        P(),
    )
    return jax.shard_map(
        per_device,
        mesh=mesh,
        in_specs=placed,
        out_specs=(
            P("dp", "ctx", None),
            P("dp", "tp", "ctx", None),
            P(),
            P("dp", "ctx", None),
            P("dp", "tp", "ctx", None),
            P("dp", "tp"),
            P("dp", "tp"),
            P("dp", "tp"),
            P("tp", "dp"),
            P("dp", "tp"),
            P("tp", "dp"),
            P("tp"),
            P("tp"),
            P(),
            P("tp"),
            P(),
            P(),
            P(),
            P(),
            P(),
        ),
        check_vma=False,
    )
```

```python
from functools import partial
import math

import jax
import jax.numpy as jnp
from jax import lax
from jax.experimental import pallas as pl
from jax.experimental.pallas import tpu as pltpu
from jax.sharding import PartitionSpec as P

BLK = 256


EPS = 1e-06
MASKED = -1e30


def norm_forward(total, gain_vec, shift_vec):
    center = total - jnp.mean(total, -1, keepdims=True)
    spread = lax.rsqrt(jnp.mean(center * center, -1, keepdims=True) + EPS)
    normed = center * spread
    return (normed, spread, normed * gain_vec + shift_vec)


def norm_backward(gradient, normed, spread, gain_vec):
    scaled = gradient * gain_vec
    inner_term = (
        scaled
        - jnp.mean(scaled, -1, keepdims=True)
        - normed * jnp.mean(scaled * normed, -1, keepdims=True)
    )
    return (inner_term * spread, jnp.sum(gradient * normed, 0), jnp.sum(gradient, 0))


F32, BF16 = jnp.float32, jnp.bfloat16


def dot32(left, right, dims):
    return lax.dot_general(left, right, (dims, ((), ())), preferred_element_type=F32)


def shifted(block, axis, step):
    size = lax.axis_size(axis)
    return lax.ppermute(block, axis, [(i, (i + step) % size) for i in range(size)])


def flipped(block, axis, bit):
    size = lax.axis_size(axis)
    return lax.ppermute(block, axis, [(i, i ^ bit) for i in range(size)])


def tie(*values):
    return lax.optimization_barrier(values)


def own_first(array):
    if lax.axis_size("dp") != 2:
        return array
    half = array.shape[-1] // 2
    turned = jnp.concatenate([array[..., half:], array[..., :half]], -1)
    return jnp.where(lax.axis_index("dp") == 0, array, turned)


def gather_weight(shard, dim):
    if lax.axis_size("dp") != 2:
        return lax.all_gather(shard, "dp", axis=dim, tiled=True)
    return jnp.concatenate([shard, flipped(shard, "dp", 1)], dim)


class WeightSum:
    def __init__(self, gradient, dim):
        self.bits = []
        bit = 1
        while bit < lax.axis_size("ctx"):
            self.bits.append(bit)
            bit *= 2
        if lax.axis_size("dp") == 2:
            kept, given = jnp.split(gradient, 2, dim)
            self.kept, self.moved = kept, flipped(given.astype(BF16), "dp", 1)
        else:
            low = gradient.astype(BF16)
            self.moved = lax.psum_scatter(low, "dp", scatter_dimension=dim, tiled=True)
            self.kept = jnp.zeros(self.moved.shape, F32)

    def step(self):
        low = (self.kept.astype(F32) + self.moved.astype(F32)).astype(BF16)
        self.kept, self.moved = low, flipped(low, "ctx", self.bits.pop(0))

    def total(self):
        while self.bits:
            self.step()
        return self.kept.astype(F32) + self.moved.astype(F32)


class VectorSum:
    def __init__(self, vector, axes):
        self.bits = []
        for axis in axes:
            bit = 1
            while bit < lax.axis_size(axis):
                self.bits.append((axis, bit))
                bit *= 2
        self.kept, self.moved = vector, flipped(vector, *self.bits.pop(0))

    def step(self):
        summed = self.kept + self.moved
        self.kept, self.moved = summed, flipped(summed, *self.bits.pop(0))

    def total(self):
        while self.bits:
            self.step()
        return self.kept + self.moved


def gather_parts(block):
    size = lax.axis_size("ctx")
    held, order, bit = block[None], [0], size // 2
    while bit:
        held = jnp.concatenate([held, flipped(held, "ctx", bit)], 0)
        order = order + [e ^ bit for e in order]
        bit //= 2
    position = jnp.asarray([order.index(e) for e in range(size)], jnp.int32)
    return held, position[lax.axis_index("ctx") ^ jnp.arange(size, dtype=jnp.int32)]


def scatter_parts(blocks):
    size = lax.axis_size("ctx")
    place = lax.axis_index("ctx")
    held = {e: lax.dynamic_index_in_dim(blocks, place ^ e, 0, False).astype(F32) for e in range(size)}
    bit = 1
    while bit < size:
        sent = [e for e in held if e & bit]
        moved = flipped(jnp.stack([held[e].astype(BF16) for e in sent]), "ctx", bit)
        for i, e in enumerate(sent):
            held[e ^ bit] = held[e ^ bit] + moved[i].astype(F32)
            del held[e]
        bit *= 2
    return held[0]


def rows_turn(block):
    size = lax.axis_size("tp")
    place = lax.axis_index("tp")
    blocks = block.reshape((size, block.shape[0] // size) + block.shape[1:])
    return jnp.concatenate(
        [
            lax.dynamic_index_in_dim(blocks, lax.rem(place - e + size, size), 0, False)
            for e in range(size)
        ],
        0,
    )


def rows_sum(total):
    size = lax.axis_size("tp")
    rows = total.shape[0] // size
    low = total.astype(BF16)
    moved = [shifted(low[e * rows : (e + 1) * rows], "tp", size - e) for e in range(1, size)]
    kept = total[:rows]
    for block in moved:
        kept = kept + block.astype(F32)
    return kept


def rows_gather(block):
    size = lax.axis_size("tp")
    return jnp.concatenate([block] + [shifted(block, "tp", e) for e in range(1, size)], 0)


def rows_exchange(blocks):
    size = lax.axis_size("tp")
    return [blocks[0]] + [shifted(blocks[size - j], "tp", j) for j in range(1, size)]


TILE = 128


def attend_kernel(heads, limits, order, query, kv, prior, logits, weights, context, inverse):
    limit = limits[pl.program_id(0)]
    width = query.shape[1]
    size = width // heads
    places, block, unused = kv.shape
    keys = places * block
    column = lax.broadcasted_iota(jnp.int32, (query.shape[0], keys), 1)
    for h in range(heads):
        own = slice(h * size, (h + 1) * size)
        raw = jnp.concatenate(
            [
                lax.dot_general(
                    query[:, own],
                    kv[order[p], :, own],
                    (((1,), (1,)), ((), ())),
                    preferred_element_type=F32,
                )
                for p in range(places)
            ],
            1,
        )
        score = prior[0, h].astype(F32) + raw
        logits[0, h] = score.astype(BF16)
        masked = jnp.where(column < limit, score, MASKED)
        exponent = jnp.exp(masked - jnp.max(masked, -1, keepdims=True))
        scale = 1.0 / jnp.sum(exponent, -1, keepdims=True)
        low = exponent.astype(BF16)
        weights[h] = low
        mixed = sum(
            jnp.dot(
                low[:, p * block : (p + 1) * block],
                kv[order[p], :, width + h * size : width + (h + 1) * size],
                preferred_element_type=F32,
            )
            for p in range(places)
        )
        context[:, own] = (mixed * scale).astype(BF16)
        inverse[:, own] = jnp.broadcast_to(scale, (query.shape[0], size))


def attend(query, kv, order, prior, limits, heads):
    rows, width = query.shape
    keys = kv.shape[0] * kv.shape[1]
    tile = lambda i, *scalars: (i, 0)
    whole = lambda i, *scalars: (0, 0, 0)
    cube = lambda i, *scalars: (0, i, 0)
    quad = lambda i, *scalars: (0, 0, i, 0)
    return pl.pallas_call(
        partial(attend_kernel, heads),
        grid_spec=pltpu.PrefetchScalarGridSpec(
            num_scalar_prefetch=2,
            grid=(rows // TILE,),
            in_specs=[
                pl.BlockSpec((TILE, width), tile),
                pl.BlockSpec(kv.shape, whole),
                pl.BlockSpec((1, heads, TILE, keys), quad),
            ],
            out_specs=[
                pl.BlockSpec((1, heads, TILE, keys), quad),
                pl.BlockSpec((heads, TILE, keys), cube),
                pl.BlockSpec((TILE, width), tile),
                pl.BlockSpec((TILE, width), tile),
            ],
        ),
        out_shape=[
            jax.ShapeDtypeStruct((1, heads, rows, keys), BF16),
            jax.ShapeDtypeStruct((heads, rows, keys), BF16),
            jax.ShapeDtypeStruct((rows, width), BF16),
            jax.ShapeDtypeStruct((rows, width), F32),
        ],
        cost_estimate=pl.CostEstimate(
            flops=4 * heads * rows * keys * width // heads, transcendentals=heads * rows * keys, bytes_accessed=6 * heads * rows * keys
        ),
        name="attend",
    )(limits, order, query, kv, prior)


def attend_back_kernel(
    heads, scale, order, weights, kv, context, d_context, d_context_t, query_t, d_scores, d_query, d_kv, total
):
    width = context.shape[1]
    size = width // heads
    places, block, unused = kv.shape
    step = pl.program_id(0)

    @pl.when(step == 0)
    def _():
        total[...] = jnp.zeros_like(total)

    for h in range(heads):
        own = slice(h * size, (h + 1) * size)
        other = slice(width + h * size, width + (h + 1) * size)
        low = weights[h]
        d_weights = jnp.concatenate(
            [
                lax.dot_general(
                    d_context[:, own],
                    kv[order[p], :, other],
                    (((1,), (1,)), ((), ())),
                    preferred_element_type=F32,
                )
                for p in range(places)
            ],
            1,
        )
        mean = jnp.sum(
            d_context[:, own].astype(F32) * context[:, own].astype(F32), -1, keepdims=True
        )
        change = (low.astype(F32) * (d_weights - mean)).astype(BF16)
        d_scores[0, h] = change
        d_query[:, own] = scale * sum(
            jnp.dot(
                change[:, p * block : (p + 1) * block],
                kv[order[p], :, own],
                preferred_element_type=F32,
            )
            for p in range(places)
        )
        total[own, :] += jnp.dot(query_t[own, :], change, preferred_element_type=F32)
        total[other, :] += jnp.dot(d_context_t[own, :], low, preferred_element_type=F32)

    @pl.when(step == pl.num_programs(0) - 1)
    def _():
        columns = d_kv.shape[2]
        for p in range(d_kv.shape[0]):
            d_kv[p] = total[:, p * columns : (p + 1) * columns].astype(BF16)


def attend_back(weights, kv, order, context, d_context, query, scale):
    heads, rows, keys = weights.shape
    width = context.shape[1]
    places, block, unused = kv.shape
    tile = lambda i, order: (i, 0)
    turned = lambda i, order: (0, i)
    whole = lambda i, order: (0, 0, 0)
    return pl.pallas_call(
        partial(attend_back_kernel, heads, scale),
        grid_spec=pltpu.PrefetchScalarGridSpec(
            num_scalar_prefetch=1,
            grid=(rows // TILE,),
            in_specs=[
                pl.BlockSpec((heads, TILE, keys), lambda i, order: (0, i, 0)),
                pl.BlockSpec(kv.shape, whole),
                pl.BlockSpec((TILE, width), tile),
                pl.BlockSpec((TILE, width), tile),
                pl.BlockSpec((width, TILE), turned),
                pl.BlockSpec((width, TILE), turned),
            ],
            out_specs=[
                pl.BlockSpec((1, heads, TILE, keys), lambda i, order: (0, 0, i, 0)),
                pl.BlockSpec((TILE, width), tile),
                pl.BlockSpec((places, 2 * width, block), whole),
            ],
            scratch_shapes=[pltpu.VMEM((2 * width, keys), F32)],
        ),
        out_shape=[
            jax.ShapeDtypeStruct((1, heads, rows, keys), BF16),
            jax.ShapeDtypeStruct((rows, width), F32),
            jax.ShapeDtypeStruct((places, 2 * width, block), BF16),
        ],
        cost_estimate=pl.CostEstimate(
            flops=10 * heads * rows * keys * width // heads, transcendentals=0, bytes_accessed=6 * heads * rows * keys
        ),
        name="attend_back",
    )(order, weights, kv, context, d_context, d_context.T, query.T)


def per_device(
    inputs,
    teacher_states,
    lengths,
    prev_logits,
    w_query,
    w_key,
    w_value,
    w_output,
    w_inner,
    w_outer,
    bias_query,
    bias_value,
    bias_output,
    bias_inner,
    bias_outer,
    gain_first,
    shift_first,
    gain_second,
    shift_second,
):
    tokens = inputs[0]
    row_count, model_width = tokens.shape
    heads_local = prev_logits.shape[1]
    width_local = w_query.shape[1]
    score_scale = 1.0 / math.sqrt(width_local // heads_local)
    seq_length = lengths[0]
    ctx_place, tp_place = lax.axis_index("ctx"), lax.axis_index("tp")
    tp_size = lax.axis_size("tp")
    part_rows = row_count // tp_size

    qkv_shard = jnp.concatenate([w_query.T, w_key.T, w_value.T], 0)
    full_qkv = gather_weight(qkv_shard, 1)
    row_pos = ctx_place * row_count + jnp.arange(row_count, dtype=jnp.int32)
    limits = jnp.minimum((row_pos[::TILE] // BLK + 1) * BLK, seq_length)

    def own_rows(array):
        return lax.dynamic_slice_in_dim(array, tp_place * part_rows, part_rows, 0)

    tokens_first = own_first(tokens)
    projected = dot32(tokens_first, full_qkv, ((1,), (1,)))
    query_local = (projected[:, :width_local] + bias_query).astype(BF16)
    kv_local = jnp.concatenate(
        [projected[:, width_local : 2 * width_local], projected[:, 2 * width_local :] + bias_value], 1
    ).astype(BF16)
    late_inputs = tie(kv_local, w_output, w_inner, w_outer)
    kv_local, w_output, w_inner, w_outer = late_inputs
    kv_all, order = gather_parts(kv_local)
    full_output = rows_gather(gather_weight(w_output, 1))
    full_inner = gather_weight(w_inner, 0)
    full_outer = gather_weight(w_outer, 1)
    all_count = VectorSum(seq_length.astype(F32), ("dp",)).total()

    query_scaled = (query_local.astype(F32) * score_scale).astype(BF16)
    logits, weights, context, inverse = attend(
        query_scaled, kv_all, order, prev_logits, limits, heads_local
    )
    context_turned = rows_turn(context)
    context_mine = jnp.concatenate(rows_exchange(jnp.split(context_turned, tp_size, 0)), 1)
    attended = own_first(dot32(context_mine, full_output, ((1,), (0,))))
    first_sum = own_rows(tokens).astype(F32) + attended + bias_output
    normed_first, spread_first, hidden = norm_forward(first_sum, gain_first, shift_first)
    hidden_low = rows_gather(own_first(hidden.astype(BF16)))
    pre_act = dot32(hidden_low, full_inner, ((1,), (0,))) + bias_inner
    act_low = jax.nn.gelu(pre_act, approximate=False).astype(BF16)
    fed = own_first(rows_sum(dot32(act_low, full_outer, ((1,), (0,)))))
    second_sum = hidden + fed + bias_outer
    normed_second, spread_second, result = norm_forward(second_sum, gain_second, shift_second)
    valid_rows = (own_rows(row_pos) < seq_length).astype(F32)
    deviation = result - own_rows(teacher_states[0]).astype(F32)
    local_squared = jnp.sum(valid_rows[:, None] * deviation * deviation)
    token_total = row_count * lax.axis_size("ctx") * lax.axis_size("dp")
    d_out = 2.0 * token_total / all_count * valid_rows[:, None] * deviation
    d_second, grad_gain_second, grad_shift_second = norm_backward(
        d_out, normed_second, spread_second, gain_second
    )
    grad_bias_outer = jnp.sum(d_second, 0)
    d_second_low = rows_gather(own_first(d_second.astype(BF16)))
    d_act = dot32(d_second_low, full_outer, ((1,), (1,)))
    gelu_back = jax.vjp(partial(jax.nn.gelu, approximate=False), pre_act)[1]
    d_pre = gelu_back(d_act)[0]
    grad_bias_inner = jnp.sum(d_pre, 0)
    d_pre_low = d_pre.astype(BF16)
    hidden_part = rows_sum(dot32(d_pre_low, full_inner, ((1,), (1,))))
    outer_sum = WeightSum(dot32(act_low, d_second_low, ((0,), (0,))), 1)
    inner_sum = WeightSum(dot32(hidden_low, d_pre_low, ((0,), (0,))), 0)
    d_hidden = d_second + own_first(hidden_part)
    d_first, grad_gain_first, grad_shift_first = norm_backward(
        d_hidden, normed_first, spread_first, gain_first
    )
    grad_bias_output = jnp.sum(d_first, 0)
    d_first, outer_sum.moved = tie(d_first, outer_sum.moved)
    outer_sum.step()
    d_first_low = own_first(d_first.astype(BF16))
    d_context_mine = dot32(d_first_low, full_output, ((1,), (1,))).astype(BF16)
    d_context = jnp.concatenate(rows_exchange(jnp.split(d_context_mine, tp_size, 1)), 0)
    d_context = (rows_turn(d_context).astype(F32) * inverse).astype(BF16)

    places = jnp.arange(tp_size)[:, None] == tp_place
    placed_bias = jnp.where(places, grad_bias_inner[None], 0.0).reshape(-1)
    early_sum = VectorSum(
        jnp.concatenate(
            [
                grad_bias_output,
                grad_bias_outer,
                grad_gain_first,
                grad_shift_first,
                grad_gain_second,
                grad_shift_second,
                jnp.full((128,), local_squared),
                placed_bias,
            ]
        ),
        ("dp", "ctx", "tp"),
    )
    d_context, outer_sum.moved, inner_sum.moved, early_sum.moved = tie(
        d_context, outer_sum.moved, inner_sum.moved, early_sum.moved
    )
    outer_sum.step()
    inner_sum.step()
    early_sum.step()
    result_mine, d_first_low, unused = tie(result.astype(BF16), d_first_low, d_context)
    result_all = rows_turn(rows_gather(result_mine)).astype(F32)
    d_first_all = rows_gather(d_first_low)
    d_scores, d_query, d_kv_parts = attend_back(
        weights, kv_all, order, context, d_context, query_scaled, score_scale
    )
    d_kv_parts, outer_sum.moved, inner_sum.moved, early_sum.moved = tie(
        d_kv_parts, outer_sum.moved, inner_sum.moved, early_sum.moved
    )
    early_sum.step()
    d_kv = scatter_parts(d_kv_parts)
    output_sum = WeightSum(dot32(context_turned, d_first_all, ((0,), (0,))), 1)
    d_query_low = d_query.astype(BF16)
    d_kv_low, inner_sum.moved, early_sum.moved = tie(
        d_kv.astype(BF16), inner_sum.moved, early_sum.moved
    )
    inner_sum.step()
    early_sum.step()
    d_qkv_low = jnp.concatenate([d_query_low, d_kv_low.T], 1)
    tokens_part = rows_sum(dot32(rows_turn(d_qkv_low), full_qkv, ((1,), (0,))))
    qkv_sum = WeightSum(dot32(d_qkv_low, tokens_first, ((0,), (0,))), 1)
    grad_mine = (d_first + own_first(tokens_part)).astype(BF16)
    grad_mine, inner_sum.moved, output_sum.moved, early_sum.moved = tie(
        grad_mine, inner_sum.moved, output_sum.moved, early_sum.moved
    )
    grad_inputs = rows_turn(rows_gather(grad_mine)).astype(F32)
    output_shard = output_sum.total()
    shard_qkv = qkv_sum.total()
    early = early_sum.total()
    width = model_width
    sums = [early[i * width : (i + 1) * width] for i in range(6)]
    loss_value = early[6 * width] / (all_count * width)
    sum_bias_inner = lax.dynamic_slice_in_dim(
        early, 6 * width + 128 + tp_place * grad_bias_inner.shape[0], grad_bias_inner.shape[0], 0
    )
    late = VectorSum(
        jnp.concatenate([jnp.sum(d_query, 0), jnp.sum(d_kv[width_local:], 1)]), ("dp", "ctx")
    ).total()
    return (
        result_all[None],
        logits,
        loss_value,
        grad_inputs[None],
        d_scores,
        shard_qkv[:width_local].T,
        shard_qkv[width_local : 2 * width_local].T,
        shard_qkv[2 * width_local :].T,
        output_shard,
        inner_sum.total(),
        outer_sum.total(),
        late[:width_local],
        late[width_local:],
        sums[0],
        sum_bias_inner,
        sums[1],
        sums[2],
        sums[3],
        sums[4],
        sums[5],
    )


def solution(mesh):
    placed = (
        P("dp", "ctx", None),
        P("dp", "ctx", None),
        P("dp"),
        P("dp", "tp", "ctx", None),
        P("dp", "tp"),
        P("dp", "tp"),
        P("dp", "tp"),
        P("tp", "dp"),
        P("dp", "tp"),
        P("tp", "dp"),
        P("tp"),
        P("tp"),
        P(),
        P("tp"),
        P(),
        P(),
        P(),
        P(),
        P(),
    )
    return jax.shard_map(
        per_device,
        mesh=mesh,
        in_specs=placed,
        out_specs=(
            P("dp", "ctx", None),
            P("dp", "tp", "ctx", None),
            P(),
            P("dp", "ctx", None),
            P("dp", "tp", "ctx", None),
            P("dp", "tp"),
            P("dp", "tp"),
            P("dp", "tp"),
            P("tp", "dp"),
            P("dp", "tp"),
            P("tp", "dp"),
            P("tp"),
            P("tp"),
            P(),
            P("tp"),
            P(),
            P(),
            P(),
            P(),
            P(),
        ),
        check_vma=False,
    )
```

```python
from functools import partial
import math

import jax
import jax.numpy as jnp
from jax import lax
from jax.experimental import pallas as pl
from jax.experimental.pallas import tpu as pltpu
from jax.sharding import PartitionSpec as P

BLK = 256


EPS = 1e-06
MASKED = -1e30


def norm_forward(total, gain_vec, shift_vec):
    center = total - jnp.mean(total, -1, keepdims=True)
    spread = lax.rsqrt(jnp.mean(center * center, -1, keepdims=True) + EPS)
    normed = center * spread
    return (normed, spread, normed * gain_vec + shift_vec)


def norm_backward(gradient, normed, spread, gain_vec):
    scaled = gradient * gain_vec
    inner_term = (
        scaled
        - jnp.mean(scaled, -1, keepdims=True)
        - normed * jnp.mean(scaled * normed, -1, keepdims=True)
    )
    return (inner_term * spread, jnp.sum(gradient * normed, 0), jnp.sum(gradient, 0))


F32, BF16 = jnp.float32, jnp.bfloat16


def dot32(left, right, dims):
    return lax.dot_general(left, right, (dims, ((), ())), preferred_element_type=F32)


def shifted(block, axis, step):
    size = lax.axis_size(axis)
    return lax.ppermute(block, axis, [(i, (i + step) % size) for i in range(size)])


def flipped(block, axis, bit):
    size = lax.axis_size(axis)
    return lax.ppermute(block, axis, [(i, i ^ bit) for i in range(size)])


def tie(*values):
    return lax.optimization_barrier(values)


def own_first(array):
    if lax.axis_size("dp") != 2:
        return array
    half = array.shape[-1] // 2
    turned = jnp.concatenate([array[..., half:], array[..., :half]], -1)
    return jnp.where(lax.axis_index("dp") == 0, array, turned)


def gather_weight(shard, dim):
    if lax.axis_size("dp") != 2:
        return lax.all_gather(shard, "dp", axis=dim, tiled=True)
    return jnp.concatenate([shard, flipped(shard, "dp", 1)], dim)


def gather_late(shard, dim):
    if lax.axis_size("dp") != 2:
        return gather_weight(shard, dim), lambda moved: moved
    moved = flipped(shard, "dp", 1)
    return moved, lambda moved: jnp.concatenate([shard, moved], dim)


class WeightSum:
    def __init__(self, gradient, dim, far_first=False):
        self.bits = []
        bit = 1
        while bit < lax.axis_size("ctx"):
            self.bits.append(bit)
            bit *= 2
        if far_first:
            self.bits.reverse()
        if lax.axis_size("dp") == 2:
            kept, given = jnp.split(gradient, 2, dim)
            self.kept, self.moved = kept, flipped(given.astype(BF16), "dp", 1)
        else:
            low = gradient.astype(BF16)
            self.moved = lax.psum_scatter(low, "dp", scatter_dimension=dim, tiled=True)
            self.kept = jnp.zeros(self.moved.shape, F32)

    def step(self):
        low = (self.kept.astype(F32) + self.moved.astype(F32)).astype(BF16)
        self.kept, self.moved = low, flipped(low, "ctx", self.bits.pop(0))

    def total(self):
        while self.bits:
            self.step()
        return self.kept.astype(F32) + self.moved.astype(F32)


class VectorSum:
    def __init__(self, vector, axes):
        self.bits = []
        for axis in axes:
            bit = 1
            while bit < lax.axis_size(axis):
                self.bits.append((axis, bit))
                bit *= 2
        self.kept, self.moved = vector, flipped(vector, *self.bits.pop(0))

    def step(self):
        summed = self.kept + self.moved
        self.kept, self.moved = summed, flipped(summed, *self.bits.pop(0))

    def total(self):
        while self.bits:
            self.step()
        return self.kept + self.moved


def ctx_order():
    order, bit = [0], lax.axis_size("ctx") // 2
    while bit:
        order = order + [e ^ bit for e in order]
        bit //= 2
    return order


def gather_parts(block):
    held, bit = [block[None]], lax.axis_size("ctx") // 2
    while bit:
        sent = held[0] if len(held) == 1 else jnp.concatenate(held, 0)
        held.append(flipped(sent, "ctx", bit))
        bit //= 2
    return held


def scatter_parts(blocks):
    size, bit = lax.axis_size("ctx"), 1
    while bit < size:
        half = blocks.shape[0] // 2
        moved = flipped(blocks[half:].astype(BF16), "ctx", bit)
        blocks = blocks[:half].astype(F32) + moved.astype(F32)
        bit *= 2
    return blocks[0]


def rows_turn(block):
    size = lax.axis_size("tp")
    place = lax.axis_index("tp")
    blocks = block.reshape((size, block.shape[0] // size) + block.shape[1:])
    return jnp.concatenate(
        [
            lax.dynamic_index_in_dim(blocks, lax.rem(place - e + size, size), 0, False)
            for e in range(size)
        ],
        0,
    )


def rows_sum(total):
    size = lax.axis_size("tp")
    rows = total.shape[0] // size
    low = total.astype(BF16)
    moved = [shifted(low[e * rows : (e + 1) * rows], "tp", size - e) for e in range(1, size)]
    kept = total[:rows]
    for block in moved:
        kept = kept + block.astype(F32)
    return kept


def rows_moved(block):
    moved = []
    for e in range(1, lax.axis_size("tp")):
        moved.append(shifted(block, "tp", e))
    return moved


def rows_gather(block):
    return jnp.concatenate([block] + rows_moved(block), 0)


def rows_exchange(blocks):
    size = lax.axis_size("tp")
    return [blocks[0]] + [shifted(blocks[size - j], "tp", j) for j in range(1, size)]


TILE = 128


def blocks_of(refs):
    return [ref.at[b] for ref in refs for b in range(ref.shape[0])]


def attend_kernel(heads, parts, limits, starts, query, prior, *refs):
    kv, (logits, weights, context, inverse) = blocks_of(refs[:parts]), refs[parts:]
    limit = limits[pl.program_id(0)]
    rows, width = query.shape
    size = width // heads
    block = kv[0].shape[0]
    column = lax.broadcasted_iota(jnp.int32, (rows, block), 1)
    spans = [pl.ds(pl.multiple_of(starts[e], block), block) for e in range(len(kv))]
    for h in range(heads):
        own = slice(h * size, (h + 1) * size)
        masked = []
        for e, span in enumerate(spans):
            raw = lax.dot_general(
                query[:, own], kv[e][:, own], (((1,), (1,)), ((), ())), preferred_element_type=F32
            )
            score = prior[0, h, :, span].astype(F32) + raw
            logits[0, h, :, span] = score.astype(BF16)
            masked.append(jnp.where(column < limit - starts[e], score, MASKED))
        top = jnp.max(masked[0], -1, keepdims=True)
        for part in masked[1:]:
            top = jnp.maximum(top, jnp.max(part, -1, keepdims=True))
        count = jnp.zeros((rows, 1), F32)
        mixed = jnp.zeros((rows, size), F32)
        for e, span in enumerate(spans):
            exponent = jnp.exp(masked[e] - top)
            count = count + jnp.sum(exponent, -1, keepdims=True)
            low = exponent.astype(BF16)
            weights[h, :, span] = low
            mixed = mixed + jnp.dot(
                low, kv[e][:, width + h * size : width + (h + 1) * size], preferred_element_type=F32
            )
        scale = 1.0 / count
        context[:, own] = (mixed * scale).astype(BF16)
        inverse[:, own] = jnp.broadcast_to(scale, (rows, size))


def attend(query, kv, starts, prior, limits, heads):
    rows, width = query.shape
    keys = prior.shape[3]
    tile = lambda i, *scalars: (i, 0)
    whole = lambda i, *scalars: (0, 0, 0)
    cube = lambda i, *scalars: (0, i, 0)
    quad = lambda i, *scalars: (0, 0, i, 0)
    return pl.pallas_call(
        partial(attend_kernel, heads, len(kv)),
        grid_spec=pltpu.PrefetchScalarGridSpec(
            num_scalar_prefetch=2,
            grid=(rows // TILE,),
            in_specs=[pl.BlockSpec((TILE, width), tile), pl.BlockSpec((1, heads, TILE, keys), quad)]
            + [pl.BlockSpec(part.shape, whole) for part in kv],
            out_specs=[
                pl.BlockSpec((1, heads, TILE, keys), quad),
                pl.BlockSpec((heads, TILE, keys), cube),
                pl.BlockSpec((TILE, width), tile),
                pl.BlockSpec((TILE, width), tile),
            ],
        ),
        out_shape=[
            jax.ShapeDtypeStruct((1, heads, rows, keys), BF16),
            jax.ShapeDtypeStruct((heads, rows, keys), BF16),
            jax.ShapeDtypeStruct((rows, width), BF16),
            jax.ShapeDtypeStruct((rows, width), F32),
        ],
        cost_estimate=pl.CostEstimate(
            flops=4 * rows * keys * width, transcendentals=heads * rows * keys, bytes_accessed=6 * heads * rows * keys
        ),
        name="attend",
    )(limits, starts, query, prior, *kv)


def attend_back_kernel(heads, scale, parts, starts, weights, context, d_mixed, inverse, query, *refs):
    kv, (d_scores, d_query, d_kv, total) = blocks_of(refs[:parts]), refs[parts:]
    width = context.shape[1]
    size = width // heads
    block = kv[0].shape[0]
    step = pl.program_id(0)
    spans = [pl.ds(pl.multiple_of(starts[e], block), block) for e in range(len(kv))]

    @pl.when(step == 0)
    def _():
        total[...] = jnp.zeros_like(total)

    scaled = d_mixed[...].astype(F32) * inverse[...]
    product = scaled * context[...].astype(F32)
    d_context = scaled.astype(BF16)
    for h in range(heads):
        own = slice(h * size, (h + 1) * size)
        other = slice(width + h * size, width + (h + 1) * size)
        mean = jnp.sum(product[:, own], -1, keepdims=True)
        d_head = jnp.zeros((context.shape[0], size), F32)
        for e, span in enumerate(spans):
            d_weights = lax.dot_general(
                d_context[:, own], kv[e][:, other], (((1,), (1,)), ((), ())), preferred_element_type=F32
            )
            low = weights[h, :, span]
            change = (low.astype(F32) * (d_weights - mean)).astype(BF16)
            d_scores[0, h, :, span] = change
            d_head = d_head + jnp.dot(change, kv[e][:, own], preferred_element_type=F32)
            total[e, own, :] += lax.dot_general(
                query[:, own], change, (((0,), (0,)), ((), ())), preferred_element_type=F32
            )
            total[e, other, :] += lax.dot_general(
                d_context[:, own], low, (((0,), (0,)), ((), ())), preferred_element_type=F32
            )
        d_query[:, own] = scale * d_head

    @pl.when(step == pl.num_programs(0) - 1)
    def _():
        d_kv[...] = total[...].astype(BF16)


def attend_back(weights, kv, starts, context, d_mixed, inverse, query, scale):
    heads, rows, keys = weights.shape
    width = context.shape[1]
    block = kv[0].shape[1]
    tile = lambda i, *scalars: (i, 0)
    whole = lambda i, *scalars: (0, 0, 0)
    shape = (keys // block, 2 * width, block)
    return pl.pallas_call(
        partial(attend_back_kernel, heads, scale, len(kv)),
        grid_spec=pltpu.PrefetchScalarGridSpec(
            num_scalar_prefetch=1,
            grid=(rows // TILE,),
            in_specs=[pl.BlockSpec((heads, TILE, keys), lambda i, *scalars: (0, i, 0))]
            + [pl.BlockSpec((TILE, width), tile)] * 4
            + [pl.BlockSpec(part.shape, whole) for part in kv],
            out_specs=[
                pl.BlockSpec((1, heads, TILE, keys), lambda i, *scalars: (0, 0, i, 0)),
                pl.BlockSpec((TILE, width), tile),
                pl.BlockSpec(shape, whole),
            ],
            scratch_shapes=[pltpu.VMEM(shape, F32)],
        ),
        out_shape=[
            jax.ShapeDtypeStruct((1, heads, rows, keys), BF16),
            jax.ShapeDtypeStruct((rows, width), F32),
            jax.ShapeDtypeStruct(shape, BF16),
        ],
        cost_estimate=pl.CostEstimate(
            flops=10 * rows * keys * width, transcendentals=0, bytes_accessed=6 * heads * rows * keys
        ),
        name="attend_back",
    )(starts, weights, context, d_mixed, inverse, query, *kv)


def pack_kernel(lead, place, squared, *refs):
    vectors, placed, out = refs[:-2], refs[-2], refs[-1]
    out[...] = jnp.zeros_like(out)
    for i, vector in enumerate(vectors):
        out[i : i + 1, :] = vector[...]
    out[len(vectors) : len(vectors) + 1, :] = jnp.broadcast_to(squared[...], (1, out.shape[1]))
    for p in range((out.shape[0] - lead) // placed.shape[0]):

        @pl.when(place[0] == p)
        def _():
            first = lead + p * placed.shape[0]
            out[first : first + placed.shape[0], :] = placed[...]


def pack(vectors, squared, placed, place, places):
    width = vectors[0].shape[0]
    vmem = pl.BlockSpec(memory_space=pltpu.VMEM)
    rows = placed.reshape(-1, width)
    return pl.pallas_call(
        partial(pack_kernel, 8),
        in_specs=[pl.BlockSpec(memory_space=pltpu.SMEM)] + [vmem] * (len(vectors) + 2),
        out_specs=vmem,
        out_shape=jax.ShapeDtypeStruct((8 + places * rows.shape[0], width), F32),
        name="pack",
    )(place.reshape(1), squared.reshape(1, 1), *[v.reshape(1, width) for v in vectors], rows)


def per_device(
    inputs,
    teacher_states,
    lengths,
    prev_logits,
    w_query,
    w_key,
    w_value,
    w_output,
    w_inner,
    w_outer,
    bias_query,
    bias_value,
    bias_output,
    bias_inner,
    bias_outer,
    gain_first,
    shift_first,
    gain_second,
    shift_second,
):
    tokens = inputs[0]
    row_count, model_width = tokens.shape
    heads_local = prev_logits.shape[1]
    width_local = w_query.shape[1]
    score_scale = 1.0 / math.sqrt(width_local // heads_local)
    seq_length = lengths[0]
    ctx_place, tp_place = lax.axis_index("ctx"), lax.axis_index("tp")
    tp_size = lax.axis_size("tp")
    part_rows = row_count // tp_size

    qkv_shard = jnp.concatenate([w_query.T, w_key.T, w_value.T], 0)
    full_qkv = gather_weight(qkv_shard, 1)
    output_half = jnp.concatenate([w_output] + rows_moved(w_output), 0)
    row_pos = ctx_place * row_count + jnp.arange(row_count, dtype=jnp.int32)
    limits = jnp.minimum((row_pos[::TILE] // BLK + 1) * BLK, seq_length)

    def own_rows(array):
        return lax.dynamic_slice_in_dim(array, tp_place * part_rows, part_rows, 0)

    tokens_first = own_first(tokens)
    projected = dot32(tokens_first, full_qkv, ((1,), (1,)))
    query_local = (projected[:, :width_local] + bias_query).astype(BF16)
    kv_local = jnp.concatenate(
        [projected[:, width_local : 2 * width_local], projected[:, 2 * width_local :] + bias_value], 1
    ).astype(BF16)
    kv_local, output_half = tie(kv_local, output_half)
    output_moved, join_output = gather_late(output_half, 1)
    kv_all = gather_parts(kv_local)
    starts = (ctx_place ^ jnp.asarray(ctx_order(), jnp.int32)) * row_count
    all_count = VectorSum(seq_length.astype(F32), ("dp",)).total()

    query_scaled = (query_local.astype(F32) * score_scale).astype(BF16)
    logits, weights, context, inverse = attend(
        query_scaled, kv_all, starts, prev_logits, limits, heads_local
    )
    context_turned = rows_turn(context)
    context_turned, output_moved, w_inner, w_outer = tie(
        context_turned, output_moved, w_inner, w_outer
    )
    full_output = join_output(output_moved)
    inner_moved, join_inner = gather_late(w_inner, 0)
    outer_moved, join_outer = gather_late(w_outer, 1)
    context_mine = jnp.concatenate(rows_exchange(jnp.split(context_turned, tp_size, 0)), 1)
    attended = own_first(dot32(context_mine, full_output, ((1,), (0,))))
    first_sum = own_rows(tokens).astype(F32) + attended + bias_output
    normed_first, spread_first, hidden = norm_forward(first_sum, gain_first, shift_first)
    hidden_first = own_first(hidden.astype(BF16))
    hidden_moved = rows_moved(hidden_first)
    full_inner, full_outer = join_inner(inner_moved), join_outer(outer_moved)
    hidden_low = jnp.concatenate([hidden_first] + hidden_moved, 0)
    pre_act = dot32(hidden_low, full_inner, ((1,), (0,))) + bias_inner
    act_low = jax.nn.gelu(pre_act, approximate=False).astype(BF16)
    fed = own_first(rows_sum(dot32(act_low, full_outer, ((1,), (0,)))))
    second_sum = hidden + fed + bias_outer
    normed_second, spread_second, result = norm_forward(second_sum, gain_second, shift_second)
    valid_rows = (own_rows(row_pos) < seq_length).astype(F32)
    deviation = result - own_rows(teacher_states[0]).astype(F32)
    local_squared = jnp.sum(valid_rows[:, None] * deviation * deviation)
    token_total = row_count * lax.axis_size("ctx") * lax.axis_size("dp")
    d_out = 2.0 * token_total / all_count * valid_rows[:, None] * deviation
    d_second, grad_gain_second, grad_shift_second = norm_backward(
        d_out, normed_second, spread_second, gain_second
    )
    grad_bias_outer = jnp.sum(d_second, 0)
    d_second_low = rows_gather(own_first(d_second.astype(BF16)))
    d_act = dot32(d_second_low, full_outer, ((1,), (1,)))
    gelu_back = jax.vjp(partial(jax.nn.gelu, approximate=False), pre_act)[1]
    d_pre = gelu_back(d_act)[0]
    grad_bias_inner = jnp.sum(d_pre, 0)
    d_pre_low = d_pre.astype(BF16)
    hidden_part = rows_sum(dot32(d_pre_low, full_inner, ((1,), (1,))))
    outer_sum = WeightSum(dot32(act_low, d_second_low, ((0,), (0,))), 1)
    inner_sum = WeightSum(dot32(hidden_low, d_pre_low, ((0,), (0,))), 0)
    d_hidden = d_second + own_first(hidden_part)
    d_first, grad_gain_first, grad_shift_first = norm_backward(
        d_hidden, normed_first, spread_first, gain_first
    )
    grad_bias_output = jnp.sum(d_first, 0)
    d_first, outer_sum.moved = tie(d_first, outer_sum.moved)
    outer_sum.step()
    d_first_low = own_first(d_first.astype(BF16))
    d_context_mine = dot32(d_first_low, full_output, ((1,), (1,))).astype(BF16)
    d_context = jnp.concatenate(rows_exchange(jnp.split(d_context_mine, tp_size, 1)), 0)
    d_context = rows_turn(d_context)

    early_sum = VectorSum(
        pack(
            [
                grad_bias_output,
                grad_bias_outer,
                grad_gain_first,
                grad_shift_first,
                grad_gain_second,
                grad_shift_second,
            ],
            local_squared,
            grad_bias_inner,
            tp_place,
            tp_size,
        ),
        ("dp", "ctx", "tp"),
    )
    d_context, outer_sum.moved, inner_sum.moved, early_sum.moved = tie(
        d_context, outer_sum.moved, inner_sum.moved, early_sum.moved
    )
    outer_sum.step()
    inner_sum.step()
    early_sum.step()
    result_mine, d_first_low, _ = tie(result.astype(BF16), d_first_low, d_context)
    d_first_moved = rows_moved(d_first_low)
    result_moved = rows_moved(result_mine)
    d_scores, d_query, d_kv_parts = attend_back(
        weights, kv_all, starts, context, d_context, inverse, query_scaled, score_scale
    )
    d_kv_parts, outer_sum.moved, inner_sum.moved, early_sum.moved = tie(
        d_kv_parts, outer_sum.moved, inner_sum.moved, early_sum.moved
    )
    early_sum.step()
    d_kv = scatter_parts(d_kv_parts)
    d_query_low = d_query.astype(BF16)
    d_kv_low, inner_sum.moved, early_sum.moved = tie(
        d_kv.astype(BF16), inner_sum.moved, early_sum.moved
    )
    inner_sum.step()
    early_sum.step()
    d_kv_low, *d_first_moved = tie(d_kv_low, *d_first_moved)
    d_first_all = jnp.concatenate([d_first_low] + d_first_moved, 0)
    output_sum = WeightSum(dot32(context_turned, d_first_all, ((0,), (0,))), 1, True)
    d_qkv_low = jnp.concatenate([d_query_low, d_kv_low.T], 1)
    tokens_part = rows_sum(dot32(rows_turn(d_qkv_low), full_qkv, ((1,), (0,))))
    qkv_sum = WeightSum(dot32(d_qkv_low, tokens_first, ((0,), (0,))), 1, True)
    late_sum = VectorSum(
        jnp.concatenate([jnp.sum(d_query, 0), jnp.sum(d_kv[width_local:], 1)]), ("dp", "ctx")
    )
    grad_mine = (d_first + own_first(tokens_part)).astype(BF16)
    sums = (inner_sum, output_sum, early_sum, qkv_sum, late_sum)
    grad_mine, *moved = tie(grad_mine, *[one.moved for one in sums])
    for one, value in zip(sums, moved):
        one.moved = value
    for one in (output_sum, early_sum, qkv_sum, late_sum):
        one.step()
    grad_mine, *result_moved = tie(grad_mine, *result_moved)
    result_all = rows_turn(jnp.concatenate([result_mine] + result_moved, 0)).astype(F32)
    grad_inputs = rows_turn(rows_gather(grad_mine)).astype(F32)
    output_shard = output_sum.total()
    shard_qkv = qkv_sum.total()
    early = early_sum.total()
    loss_value = early[6, 0] / (all_count * model_width)
    inner_rows = grad_bias_inner.shape[0] // model_width
    sum_bias_inner = lax.dynamic_slice_in_dim(early, 8 + tp_place * inner_rows, inner_rows, 0).reshape(-1)
    late = late_sum.total()
    return (
        result_all[None],
        logits,
        loss_value,
        grad_inputs[None],
        d_scores,
        shard_qkv[:width_local].T,
        shard_qkv[width_local : 2 * width_local].T,
        shard_qkv[2 * width_local :].T,
        output_shard,
        inner_sum.total(),
        outer_sum.total(),
        late[:width_local],
        late[width_local:],
        early[0],
        sum_bias_inner,
        early[1],
        early[2],
        early[3],
        early[4],
        early[5],
    )


def solution(mesh):
    placed = (
        P("dp", "ctx", None),
        P("dp", "ctx", None),
        P("dp"),
        P("dp", "tp", "ctx", None),
        P("dp", "tp"),
        P("dp", "tp"),
        P("dp", "tp"),
        P("tp", "dp"),
        P("dp", "tp"),
        P("tp", "dp"),
        P("tp"),
        P("tp"),
        P(),
        P("tp"),
        P(),
        P(),
        P(),
        P(),
        P(),
    )
    return jax.shard_map(
        per_device,
        mesh=mesh,
        in_specs=placed,
        out_specs=(
            P("dp", "ctx", None),
            P("dp", "tp", "ctx", None),
            P(),
            P("dp", "ctx", None),
            P("dp", "tp", "ctx", None),
            P("dp", "tp"),
            P("dp", "tp"),
            P("dp", "tp"),
            P("tp", "dp"),
            P("dp", "tp"),
            P("tp", "dp"),
            P("tp"),
            P("tp"),
            P(),
            P("tp"),
            P(),
            P(),
            P(),
            P(),
            P(),
        ),
        check_vma=False,
    )
```

```python
from functools import partial
import math

import jax
import jax.numpy as jnp
from jax import lax
from jax.experimental import pallas as pl
from jax.experimental.pallas import tpu as pltpu
from jax.sharding import PartitionSpec as P

BLK = 256


EPS = 1e-06
MASKED = -1e30


def norm_forward(total, gain_vec, shift_vec):
    center = total - jnp.mean(total, -1, keepdims=True)
    spread = lax.rsqrt(jnp.mean(center * center, -1, keepdims=True) + EPS)
    normed = center * spread
    return (normed, spread, normed * gain_vec + shift_vec)


def norm_backward(gradient, normed, spread, gain_vec):
    scaled = gradient * gain_vec
    inner_term = (
        scaled
        - jnp.mean(scaled, -1, keepdims=True)
        - normed * jnp.mean(scaled * normed, -1, keepdims=True)
    )
    return (inner_term * spread, jnp.sum(gradient * normed, 0), jnp.sum(gradient, 0))


F32, BF16 = jnp.float32, jnp.bfloat16


def dot32(left, right, dims):
    return lax.dot_general(left, right, (dims, ((), ())), preferred_element_type=F32)


def shifted(block, axis, step):
    size = lax.axis_size(axis)
    return lax.ppermute(block, axis, [(i, (i + step) % size) for i in range(size)])


def flipped(block, axis, bit):
    size = lax.axis_size(axis)
    return lax.ppermute(block, axis, [(i, i ^ bit) for i in range(size)])


def tie(*values):
    return lax.optimization_barrier(values)


def own_first(array):
    if lax.axis_size("dp") != 2:
        return array
    half = array.shape[-1] // 2
    turned = jnp.concatenate([array[..., half:], array[..., :half]], -1)
    return jnp.where(lax.axis_index("dp") == 0, array, turned)


def gather_weight(shard, dim):
    if lax.axis_size("dp") != 2:
        return lax.all_gather(shard, "dp", axis=dim, tiled=True)
    return jnp.concatenate([shard, flipped(shard, "dp", 1)], dim)


def gather_late(shard, dim):
    if lax.axis_size("dp") != 2:
        return gather_weight(shard, dim), lambda moved: moved
    moved = flipped(shard, "dp", 1)
    return moved, lambda moved: jnp.concatenate([shard, moved], dim)


class WeightSum:
    def __init__(self, gradient, dim, far_first=False):
        self.bits = []
        bit = 1
        while bit < lax.axis_size("ctx"):
            self.bits.append(bit)
            bit *= 2
        if far_first:
            self.bits.reverse()
        if lax.axis_size("dp") == 2:
            kept, given = jnp.split(gradient, 2, dim)
            self.kept, self.moved = kept, flipped(given.astype(BF16), "dp", 1)
        else:
            low = gradient.astype(BF16)
            self.moved = lax.psum_scatter(low, "dp", scatter_dimension=dim, tiled=True)
            self.kept = jnp.zeros(self.moved.shape, F32)

    def step(self):
        low = (self.kept.astype(F32) + self.moved.astype(F32)).astype(BF16)
        self.kept, self.moved = low, flipped(low, "ctx", self.bits.pop(0))

    def total(self):
        while self.bits:
            self.step()
        return self.kept.astype(F32) + self.moved.astype(F32)


class VectorSum:
    def __init__(self, vector, axes):
        self.bits = []
        for axis in axes:
            bit = 1
            while bit < lax.axis_size(axis):
                self.bits.append((axis, bit))
                bit *= 2
        self.kept, self.moved = vector, flipped(vector, *self.bits.pop(0))

    def step(self):
        summed = self.kept + self.moved
        self.kept, self.moved = summed, flipped(summed, *self.bits.pop(0))

    def total(self):
        while self.bits:
            self.step()
        return self.kept + self.moved


def ctx_order():
    order, bit = [0], lax.axis_size("ctx") // 2
    while bit:
        order = order + [e ^ bit for e in order]
        bit //= 2
    return order


def gather_parts(block):
    held, bit = [block[None]], lax.axis_size("ctx") // 2
    while bit:
        sent = held[0] if len(held) == 1 else jnp.concatenate(held, 0)
        held.append(flipped(sent, "ctx", bit))
        bit //= 2
    return held


def scatter_parts(blocks):
    size, bit = lax.axis_size("ctx"), 1
    while bit < size:
        half = blocks.shape[0] // 2
        moved = flipped(blocks[half:].astype(BF16), "ctx", bit)
        blocks = blocks[:half].astype(F32) + moved.astype(F32)
        bit *= 2
    return blocks[0]


def rows_turn(block):
    size = lax.axis_size("tp")
    place = lax.axis_index("tp")
    blocks = block.reshape((size, block.shape[0] // size) + block.shape[1:])
    return jnp.concatenate(
        [
            lax.dynamic_index_in_dim(blocks, lax.rem(place - e + size, size), 0, False)
            for e in range(size)
        ],
        0,
    )


def rows_sum(total):
    size = lax.axis_size("tp")
    rows = total.shape[0] // size
    low = total.astype(BF16)
    moved = [shifted(low[e * rows : (e + 1) * rows], "tp", size - e) for e in range(1, size)]
    kept = total[:rows]
    for block in moved:
        kept = kept + block.astype(F32)
    return kept


def rows_moved(block):
    moved = []
    for e in range(1, lax.axis_size("tp")):
        moved.append(shifted(block, "tp", e))
    return moved


def rows_gather(block):
    return jnp.concatenate([block] + rows_moved(block), 0)


def rows_exchange(blocks):
    size = lax.axis_size("tp")
    return [blocks[0]] + [shifted(blocks[size - j], "tp", j) for j in range(1, size)]


TILE = 128


def blocks_of(refs):
    return [ref.at[b] for ref in refs for b in range(ref.shape[0])]


def attend_kernel(heads, parts, limits, starts, query, prior, *refs):
    kv, (logits, weights, context, inverse) = blocks_of(refs[:parts]), refs[parts:]
    limit = limits[pl.program_id(0)]
    rows, width = query.shape
    size = width // heads
    block = kv[0].shape[0]
    column = lax.broadcasted_iota(jnp.int32, (rows, block), 1)
    spans = [pl.ds(pl.multiple_of(starts[e], block), block) for e in range(len(kv))]
    for h in range(heads):
        own = slice(h * size, (h + 1) * size)
        masked = []
        for e, span in enumerate(spans):
            raw = lax.dot_general(
                query[:, own], kv[e][:, own], (((1,), (1,)), ((), ())), preferred_element_type=F32
            )
            score = prior[0, h, :, span].astype(F32) + raw
            logits[0, h, :, span] = score.astype(BF16)
            masked.append(jnp.where(column < limit - starts[e], score, MASKED))
        top = jnp.max(masked[0], -1, keepdims=True)
        for part in masked[1:]:
            top = jnp.maximum(top, jnp.max(part, -1, keepdims=True))
        count = jnp.zeros((rows, 1), F32)
        mixed = jnp.zeros((rows, size), F32)
        for e, span in enumerate(spans):
            exponent = jnp.exp(masked[e] - top)
            count = count + jnp.sum(exponent, -1, keepdims=True)
            low = exponent.astype(BF16)
            weights[h, :, span] = low
            mixed = mixed + jnp.dot(
                low, kv[e][:, width + h * size : width + (h + 1) * size], preferred_element_type=F32
            )
        scale = 1.0 / count
        context[:, own] = (mixed * scale).astype(BF16)
        inverse[:, own] = jnp.broadcast_to(scale, (rows, size))


def attend(query, kv, starts, prior, limits, heads):
    rows, width = query.shape
    keys = prior.shape[3]
    tile = lambda i, *scalars: (i, 0)
    whole = lambda i, *scalars: (0, 0, 0)
    cube = lambda i, *scalars: (0, i, 0)
    quad = lambda i, *scalars: (0, 0, i, 0)
    return pl.pallas_call(
        partial(attend_kernel, heads, len(kv)),
        grid_spec=pltpu.PrefetchScalarGridSpec(
            num_scalar_prefetch=2,
            grid=(rows // TILE,),
            in_specs=[pl.BlockSpec((TILE, width), tile), pl.BlockSpec((1, heads, TILE, keys), quad)]
            + [pl.BlockSpec(part.shape, whole) for part in kv],
            out_specs=[
                pl.BlockSpec((1, heads, TILE, keys), quad),
                pl.BlockSpec((heads, TILE, keys), cube),
                pl.BlockSpec((TILE, width), tile),
                pl.BlockSpec((TILE, width), tile),
            ],
        ),
        out_shape=[
            jax.ShapeDtypeStruct((1, heads, rows, keys), BF16),
            jax.ShapeDtypeStruct((heads, rows, keys), BF16),
            jax.ShapeDtypeStruct((rows, width), BF16),
            jax.ShapeDtypeStruct((rows, width), F32),
        ],
        cost_estimate=pl.CostEstimate(
            flops=4 * rows * keys * width, transcendentals=heads * rows * keys, bytes_accessed=6 * heads * rows * keys
        ),
        name="attend",
    )(limits, starts, query, prior, *kv)


def attend_back_kernel(heads, scale, parts, starts, weights, context, d_mixed, inverse, query, *refs):
    kv, (d_scores, d_query, d_kv, total) = blocks_of(refs[:parts]), refs[parts:]
    width = context.shape[1]
    size = width // heads
    block = kv[0].shape[0]
    step = pl.program_id(0)
    spans = [pl.ds(pl.multiple_of(starts[e], block), block) for e in range(len(kv))]

    @pl.when(step == 0)
    def _():
        total[...] = jnp.zeros_like(total)

    scaled = d_mixed[...].astype(F32) * inverse[...]
    product = scaled * context[...].astype(F32)
    d_context = scaled.astype(BF16)
    d_context_t = scaled.T.astype(BF16)
    query_t = query[...].astype(F32).T.astype(BF16)
    for h in range(heads):
        own = slice(h * size, (h + 1) * size)
        other = slice(width + h * size, width + (h + 1) * size)
        mean = jnp.sum(product[:, own], -1, keepdims=True)
        d_head = jnp.zeros((context.shape[0], size), F32)
        for e, span in enumerate(spans):
            d_weights = lax.dot_general(
                d_context[:, own], kv[e][:, other], (((1,), (1,)), ((), ())), preferred_element_type=F32
            )
            low = weights[h, :, span]
            change = (low.astype(F32) * (d_weights - mean)).astype(BF16)
            d_scores[0, h, :, span] = change
            d_head = d_head + jnp.dot(change, kv[e][:, own], preferred_element_type=F32)
            total[e, own, :] += jnp.dot(query_t[own, :], change, preferred_element_type=F32)
            total[e, other, :] += jnp.dot(d_context_t[own, :], low, preferred_element_type=F32)
        d_query[:, own] = scale * d_head

    @pl.when(step == pl.num_programs(0) - 1)
    def _():
        d_kv[...] = total[...].astype(BF16)


def attend_back(weights, kv, starts, context, d_mixed, inverse, query, scale):
    heads, rows, keys = weights.shape
    width = context.shape[1]
    block = kv[0].shape[1]
    tile = lambda i, *scalars: (i, 0)
    whole = lambda i, *scalars: (0, 0, 0)
    shape = (keys // block, 2 * width, block)
    return pl.pallas_call(
        partial(attend_back_kernel, heads, scale, len(kv)),
        grid_spec=pltpu.PrefetchScalarGridSpec(
            num_scalar_prefetch=1,
            grid=(rows // TILE,),
            in_specs=[pl.BlockSpec((heads, TILE, keys), lambda i, *scalars: (0, i, 0))]
            + [pl.BlockSpec((TILE, width), tile)] * 4
            + [pl.BlockSpec(part.shape, whole) for part in kv],
            out_specs=[
                pl.BlockSpec((1, heads, TILE, keys), lambda i, *scalars: (0, 0, i, 0)),
                pl.BlockSpec((TILE, width), tile),
                pl.BlockSpec(shape, whole),
            ],
            scratch_shapes=[pltpu.VMEM(shape, F32)],
        ),
        out_shape=[
            jax.ShapeDtypeStruct((1, heads, rows, keys), BF16),
            jax.ShapeDtypeStruct((rows, width), F32),
            jax.ShapeDtypeStruct(shape, BF16),
        ],
        cost_estimate=pl.CostEstimate(
            flops=10 * rows * keys * width, transcendentals=0, bytes_accessed=6 * heads * rows * keys
        ),
        name="attend_back",
    )(starts, weights, context, d_mixed, inverse, query, *kv)


def pack_kernel(lead, place, squared, *refs):
    vectors, placed, out = refs[:-2], refs[-2], refs[-1]
    out[...] = jnp.zeros_like(out)
    for i, vector in enumerate(vectors):
        out[i : i + 1, :] = vector[...]
    out[len(vectors) : len(vectors) + 1, :] = jnp.broadcast_to(squared[...], (1, out.shape[1]))
    for p in range((out.shape[0] - lead) // placed.shape[0]):

        @pl.when(place[0] == p)
        def _():
            first = lead + p * placed.shape[0]
            out[first : first + placed.shape[0], :] = placed[...]


def pack(vectors, squared, placed, place, places):
    width = vectors[0].shape[0]
    vmem = pl.BlockSpec(memory_space=pltpu.VMEM)
    rows = placed.reshape(-1, width)
    return pl.pallas_call(
        partial(pack_kernel, 8),
        in_specs=[pl.BlockSpec(memory_space=pltpu.SMEM)] + [vmem] * (len(vectors) + 2),
        out_specs=vmem,
        out_shape=jax.ShapeDtypeStruct((8 + places * rows.shape[0], width), F32),
        name="pack",
    )(place.reshape(1), squared.reshape(1, 1), *[v.reshape(1, width) for v in vectors], rows)


def per_device(
    inputs,
    teacher_states,
    lengths,
    prev_logits,
    w_query,
    w_key,
    w_value,
    w_output,
    w_inner,
    w_outer,
    bias_query,
    bias_value,
    bias_output,
    bias_inner,
    bias_outer,
    gain_first,
    shift_first,
    gain_second,
    shift_second,
):
    tokens = inputs[0]
    row_count, model_width = tokens.shape
    heads_local = prev_logits.shape[1]
    width_local = w_query.shape[1]
    score_scale = 1.0 / math.sqrt(width_local // heads_local)
    seq_length = lengths[0]
    ctx_place, tp_place = lax.axis_index("ctx"), lax.axis_index("tp")
    tp_size = lax.axis_size("tp")
    part_rows = row_count // tp_size

    qkv_shard = jnp.concatenate([w_query.T, w_key.T, w_value.T], 0)
    full_qkv = gather_weight(qkv_shard, 1)
    output_half = jnp.concatenate([w_output] + rows_moved(w_output), 0)
    row_pos = ctx_place * row_count + jnp.arange(row_count, dtype=jnp.int32)
    limits = jnp.minimum((row_pos[::TILE] // BLK + 1) * BLK, seq_length)

    def own_rows(array):
        return lax.dynamic_slice_in_dim(array, tp_place * part_rows, part_rows, 0)

    tokens_first = own_first(tokens)
    query_scaled = dot32(tokens_first, full_qkv[:width_local], ((1,), (1,))) + bias_query
    query_scaled = (query_scaled.astype(BF16).astype(F32) * score_scale).astype(BF16)
    bias_kv = jnp.concatenate([jnp.zeros_like(bias_value), bias_value])
    kv_local = (dot32(tokens_first, full_qkv[width_local:], ((1,), (1,))) + bias_kv).astype(BF16)
    kv_all = gather_parts(kv_local)
    kv_all[-1], output_half = tie(kv_all[-1], output_half)
    output_moved, join_output = gather_late(output_half, 1)
    starts = (ctx_place ^ jnp.asarray(ctx_order(), jnp.int32)) * row_count
    all_count = VectorSum(seq_length.astype(F32), ("dp",)).total()

    logits, weights, context, inverse = attend(
        query_scaled, kv_all, starts, prev_logits, limits, heads_local
    )
    context_turned = rows_turn(context)
    context_turned, output_moved, w_inner, w_outer = tie(
        context_turned, output_moved, w_inner, w_outer
    )
    full_output = join_output(output_moved)
    inner_moved, join_inner = gather_late(w_inner, 0)
    outer_moved, join_outer = gather_late(w_outer, 1)
    context_mine = jnp.concatenate(rows_exchange(jnp.split(context_turned, tp_size, 0)), 1)
    attended = own_first(dot32(context_mine, full_output, ((1,), (0,))))
    first_sum = own_rows(tokens).astype(F32) + attended + bias_output
    normed_first, spread_first, hidden = norm_forward(first_sum, gain_first, shift_first)
    hidden_first = own_first(hidden.astype(BF16))
    hidden_moved = rows_moved(hidden_first)
    full_inner, full_outer = join_inner(inner_moved), join_outer(outer_moved)
    hidden_low = jnp.concatenate([hidden_first] + hidden_moved, 0)
    pre_act = dot32(hidden_low, full_inner, ((1,), (0,))) + bias_inner
    act_low = jax.nn.gelu(pre_act, approximate=False).astype(BF16)
    fed = own_first(rows_sum(dot32(act_low, full_outer, ((1,), (0,)))))
    second_sum = hidden + fed + bias_outer
    normed_second, spread_second, result = norm_forward(second_sum, gain_second, shift_second)
    valid_rows = (own_rows(row_pos) < seq_length).astype(F32)
    deviation = result - own_rows(teacher_states[0]).astype(F32)
    local_squared = jnp.sum(valid_rows[:, None] * deviation * deviation)
    token_total = row_count * lax.axis_size("ctx") * lax.axis_size("dp")
    d_out = 2.0 * token_total / all_count * valid_rows[:, None] * deviation
    d_second, grad_gain_second, grad_shift_second = norm_backward(
        d_out, normed_second, spread_second, gain_second
    )
    grad_bias_outer = jnp.sum(d_second, 0)
    d_second_low = rows_gather(own_first(d_second.astype(BF16)))
    d_act = dot32(d_second_low, full_outer, ((1,), (1,)))
    gelu_back = jax.vjp(partial(jax.nn.gelu, approximate=False), pre_act)[1]
    d_pre = gelu_back(d_act)[0]
    grad_bias_inner = jnp.sum(d_pre, 0)
    d_pre_low = d_pre.astype(BF16)
    hidden_part = rows_sum(dot32(d_pre_low, full_inner, ((1,), (1,))))
    outer_sum = WeightSum(dot32(act_low, d_second_low, ((0,), (0,))), 1)
    inner_sum = WeightSum(dot32(hidden_low, d_pre_low, ((0,), (0,))), 0)
    d_hidden = d_second + own_first(hidden_part)
    d_first, grad_gain_first, grad_shift_first = norm_backward(
        d_hidden, normed_first, spread_first, gain_first
    )
    grad_bias_output = jnp.sum(d_first, 0)
    d_first_low = own_first(d_first.astype(BF16))
    d_context_mine = dot32(d_first_low, full_output, ((1,), (1,))).astype(BF16)
    d_context = jnp.concatenate(rows_exchange(jnp.split(d_context_mine, tp_size, 1)), 0)
    d_context = rows_turn(d_context)

    packed = (
        pack(
            [
                grad_bias_output,
                grad_bias_outer,
                grad_gain_first,
                grad_shift_first,
                grad_gain_second,
                grad_shift_second,
            ],
            local_squared,
            grad_bias_inner,
            tp_place,
            tp_size,
        )
    )
    early_sum = VectorSum(packed, ("dp", "ctx", "tp"))
    d_context, outer_sum.moved, inner_sum.moved = tie(
        d_context, outer_sum.moved, inner_sum.moved
    )
    outer_sum.step()
    inner_sum.step()
    both_mine = jnp.concatenate([d_first_low, result.astype(BF16)], 1)
    both_mine, _ = tie(both_mine, d_context)
    both_moved = rows_moved(both_mine)
    d_scores, d_query, d_kv_parts = attend_back(
        weights, kv_all, starts, context, d_context, inverse, query_scaled, score_scale
    )
    d_kv_parts, early_sum.moved = tie(d_kv_parts, early_sum.moved)
    early_sum.step()
    d_kv = scatter_parts(d_kv_parts)
    d_query_low = d_query.astype(BF16)
    d_kv_low, inner_sum.moved, outer_sum.moved, early_sum.moved, *both_moved = tie(
        d_kv.astype(BF16), inner_sum.moved, outer_sum.moved, early_sum.moved, *both_moved
    )
    inner_sum.step()
    outer_sum.step()
    early_sum.step()
    both = jnp.concatenate([both_mine] + both_moved, 0)
    d_first_all = both[:, :model_width]
    output_sum = WeightSum(dot32(context_turned, d_first_all, ((0,), (0,))), 1, True)
    d_qkv_low = jnp.concatenate([d_query_low, d_kv_low.T], 1)
    tokens_part = rows_sum(dot32(rows_turn(d_qkv_low), full_qkv, ((1,), (0,))))
    qkv_sum = WeightSum(dot32(d_qkv_low, tokens_first, ((0,), (0,))), 1, True)
    late_sum = VectorSum(
        jnp.concatenate([jnp.sum(d_query, 0), jnp.sum(d_kv[width_local:], 1)]), ("dp", "ctx")
    )
    grad_mine = (d_first + own_first(tokens_part)).astype(BF16)
    sums = (output_sum, early_sum, qkv_sum, late_sum)
    grad_mine, *moved = tie(grad_mine, *[one.moved for one in sums])
    for one, value in zip(sums, moved):
        one.moved = value
    for one in sums:
        one.step()
    result_all = rows_turn(both[:, model_width:]).astype(F32)
    grad_inputs = rows_turn(rows_gather(grad_mine)).astype(F32)
    output_shard = output_sum.total()
    shard_qkv = qkv_sum.total()
    early = early_sum.total()
    loss_value = early[6, 0] / (all_count * model_width)
    inner_rows = grad_bias_inner.shape[0] // model_width
    sum_bias_inner = lax.dynamic_slice_in_dim(early, 8 + tp_place * inner_rows, inner_rows, 0).reshape(-1)
    late = late_sum.total()
    return (
        result_all[None],
        logits,
        loss_value,
        grad_inputs[None],
        d_scores,
        shard_qkv[:width_local].T,
        shard_qkv[width_local : 2 * width_local].T,
        shard_qkv[2 * width_local :].T,
        output_shard,
        inner_sum.total(),
        outer_sum.total(),
        late[:width_local],
        late[width_local:],
        early[0],
        sum_bias_inner,
        early[1],
        early[2],
        early[3],
        early[4],
        early[5],
    )


def solution(mesh):
    placed = (
        P("dp", "ctx", None),
        P("dp", "ctx", None),
        P("dp"),
        P("dp", "tp", "ctx", None),
        P("dp", "tp"),
        P("dp", "tp"),
        P("dp", "tp"),
        P("tp", "dp"),
        P("dp", "tp"),
        P("tp", "dp"),
        P("tp"),
        P("tp"),
        P(),
        P("tp"),
        P(),
        P(),
        P(),
        P(),
        P(),
    )
    return jax.shard_map(
        per_device,
        mesh=mesh,
        in_specs=placed,
        out_specs=(
            P("dp", "ctx", None),
            P("dp", "tp", "ctx", None),
            P(),
            P("dp", "ctx", None),
            P("dp", "tp", "ctx", None),
            P("dp", "tp"),
            P("dp", "tp"),
            P("dp", "tp"),
            P("tp", "dp"),
            P("dp", "tp"),
            P("tp", "dp"),
            P("tp"),
            P("tp"),
            P(),
            P("tp"),
            P(),
            P(),
            P(),
            P(),
            P(),
        ),
        check_vma=False,
    )
```

```python
from functools import partial
import math

import jax
import jax.numpy as jnp
from jax import lax
from jax.experimental import pallas as pl
from jax.experimental.pallas import tpu as pltpu
from jax.sharding import PartitionSpec as P

BLK = 256


EPS = 1e-06
MASKED = -1e30


def norm_forward(total, gain_vec, shift_vec):
    center = total - jnp.mean(total, -1, keepdims=True)
    spread = lax.rsqrt(jnp.mean(center * center, -1, keepdims=True) + EPS)
    normed = center * spread
    return (normed, spread, normed * gain_vec + shift_vec)


def norm_backward(gradient, normed, spread, gain_vec):
    scaled = gradient * gain_vec
    inner_term = (
        scaled
        - jnp.mean(scaled, -1, keepdims=True)
        - normed * jnp.mean(scaled * normed, -1, keepdims=True)
    )
    return (inner_term * spread, jnp.sum(gradient * normed, 0), jnp.sum(gradient, 0))


F32, BF16 = jnp.float32, jnp.bfloat16


def dot32(left, right, dims):
    return lax.dot_general(left, right, (dims, ((), ())), preferred_element_type=F32)


def shifted(block, axis, step):
    size = lax.axis_size(axis)
    return lax.ppermute(block, axis, [(i, (i + step) % size) for i in range(size)])


def flipped(block, axis, bit):
    size = lax.axis_size(axis)
    return lax.ppermute(block, axis, [(i, i ^ bit) for i in range(size)])


def tie(*values):
    return lax.optimization_barrier(values)


def own_first(array):
    if lax.axis_size("dp") != 2:
        return array
    half = array.shape[-1] // 2
    turned = jnp.concatenate([array[..., half:], array[..., :half]], -1)
    return jnp.where(lax.axis_index("dp") == 0, array, turned)


def gather_weight(shard, dim):
    if lax.axis_size("dp") != 2:
        return lax.all_gather(shard, "dp", axis=dim, tiled=True)
    return jnp.concatenate([shard, flipped(shard, "dp", 1)], dim)


def gather_late(shard, dim):
    if lax.axis_size("dp") != 2:
        return gather_weight(shard, dim), lambda moved: moved
    moved = flipped(shard, "dp", 1)
    return moved, lambda moved: jnp.concatenate([shard, moved], dim)


class WeightSum:
    def __init__(self, gradient, dim, far_first=False):
        self.bits = []
        bit = 1
        while bit < lax.axis_size("ctx"):
            self.bits.append(bit)
            bit *= 2
        if far_first:
            self.bits.reverse()
        if lax.axis_size("dp") == 2:
            kept, given = jnp.split(gradient, 2, dim)
            self.kept, self.moved = kept, flipped(given.astype(BF16), "dp", 1)
        else:
            low = gradient.astype(BF16)
            self.moved = lax.psum_scatter(low, "dp", scatter_dimension=dim, tiled=True)
            self.kept = jnp.zeros(self.moved.shape, F32)

    def step(self):
        low = (self.kept.astype(F32) + self.moved.astype(F32)).astype(BF16)
        self.kept, self.moved = low, flipped(low, "ctx", self.bits.pop(0))

    def total(self):
        while self.bits:
            self.step()
        return self.kept.astype(F32) + self.moved.astype(F32)


class VectorSum:
    def __init__(self, vector, axes):
        self.bits = []
        for axis in axes:
            bit = 1
            while bit < lax.axis_size(axis):
                self.bits.append((axis, bit))
                bit *= 2
        self.kept, self.moved = vector, flipped(vector, *self.bits.pop(0))

    def step(self):
        summed = self.kept + self.moved
        self.kept, self.moved = summed, flipped(summed, *self.bits.pop(0))

    def total(self):
        while self.bits:
            self.step()
        return self.kept + self.moved


def ctx_order():
    order, bit = [0], lax.axis_size("ctx") // 2
    while bit:
        order = order + [e ^ bit for e in order]
        bit //= 2
    return order


def gather_parts(block, beside):
    held, bit = [block[None]], lax.axis_size("ctx") // 2
    while bit:
        sent = held[0] if len(held) == 1 else jnp.concatenate(held, 0)
        held.append(flipped(sent, "ctx", bit))
        if bit == lax.axis_size("ctx") // 2:
            held[-1], beside = tie(held[-1], beside)
        bit //= 2
    return held, beside


def scatter_parts(blocks):
    size, bit = lax.axis_size("ctx"), 1
    while bit < size:
        half = blocks.shape[0] // 2
        moved = flipped(blocks[half:].astype(BF16), "ctx", bit)
        blocks = blocks[:half].astype(F32) + moved.astype(F32)
        bit *= 2
    return blocks[0]


def rows_turn(block):
    size = lax.axis_size("tp")
    place = lax.axis_index("tp")
    blocks = block.reshape((size, block.shape[0] // size) + block.shape[1:])
    return jnp.concatenate(
        [
            lax.dynamic_index_in_dim(blocks, lax.rem(place - e + size, size), 0, False)
            for e in range(size)
        ],
        0,
    )


def rows_sum(total):
    size = lax.axis_size("tp")
    rows = total.shape[0] // size
    low = total.astype(BF16)
    moved = []
    for e in range(1, size):
        moved.append(shifted(low[e * rows : (e + 1) * rows], "tp", size - e))
    kept = total[:rows]
    for block in moved:
        kept = kept + block.astype(F32)
    return kept


def rows_moved(block):
    moved = []
    for e in range(1, lax.axis_size("tp")):
        moved.append(shifted(block, "tp", e))
    return moved


def rows_gather(block):
    return jnp.concatenate([block] + rows_moved(block), 0)


def rows_exchange(blocks):
    size = lax.axis_size("tp")
    return [blocks[0]] + [shifted(blocks[size - j], "tp", j) for j in range(1, size)]


TILE = 256


def blocks_of(refs):
    return [ref.at[b] for ref in refs for b in range(ref.shape[0])]


def attend_kernel(heads, parts, limits, starts, query, prior, *refs):
    kv, (logits, weights, context, inverse) = blocks_of(refs[:parts]), refs[parts:]
    limit = limits[pl.program_id(0)]
    rows, width = query.shape
    size = width // heads
    block = kv[0].shape[0]
    column = lax.broadcasted_iota(jnp.int32, (rows, block), 1)
    spans = [pl.ds(pl.multiple_of(starts[e], block), block) for e in range(len(kv))]
    for h in range(heads):
        own = slice(h * size, (h + 1) * size)
        masked = []
        for e, span in enumerate(spans):
            raw = lax.dot_general(
                query[:, own], kv[e][:, own], (((1,), (1,)), ((), ())), preferred_element_type=F32
            )
            score = prior[0, h, :, span].astype(F32) + raw
            logits[0, h, :, span] = score.astype(BF16)
            masked.append(jnp.where(column < limit - starts[e], score, MASKED))
        top = jnp.max(masked[0], -1, keepdims=True)
        for part in masked[1:]:
            top = jnp.maximum(top, jnp.max(part, -1, keepdims=True))
        count = jnp.zeros((rows, 1), F32)
        mixed = jnp.zeros((rows, size), F32)
        for e, span in enumerate(spans):
            exponent = jnp.exp(masked[e] - top)
            count = count + jnp.sum(exponent, -1, keepdims=True)
            low = exponent.astype(BF16)
            weights[h, :, span] = low
            mixed = mixed + jnp.dot(
                low, kv[e][:, width + h * size : width + (h + 1) * size], preferred_element_type=F32
            )
        scale = 1.0 / count
        context[:, own] = (mixed * scale).astype(BF16)
        inverse[:, own] = jnp.broadcast_to(scale, (rows, size))


def attend(query, kv, starts, prior, limits, heads):
    rows, width = query.shape
    keys = prior.shape[3]
    tile = lambda i, *scalars: (i, 0)
    whole = lambda i, *scalars: (0, 0, 0)
    cube = lambda i, *scalars: (0, i, 0)
    quad = lambda i, *scalars: (0, 0, i, 0)
    return pl.pallas_call(
        partial(attend_kernel, heads, len(kv)),
        grid_spec=pltpu.PrefetchScalarGridSpec(
            num_scalar_prefetch=2,
            grid=(rows // TILE,),
            in_specs=[pl.BlockSpec((TILE, width), tile), pl.BlockSpec((1, heads, TILE, keys), quad)]
            + [pl.BlockSpec(part.shape, whole) for part in kv],
            out_specs=[
                pl.BlockSpec((1, heads, TILE, keys), quad),
                pl.BlockSpec((heads, TILE, keys), cube),
                pl.BlockSpec((TILE, width), tile),
                pl.BlockSpec((TILE, width), tile),
            ],
        ),
        out_shape=[
            jax.ShapeDtypeStruct((1, heads, rows, keys), BF16),
            jax.ShapeDtypeStruct((heads, rows, keys), BF16),
            jax.ShapeDtypeStruct((rows, width), BF16),
            jax.ShapeDtypeStruct((rows, width), F32),
        ],
        cost_estimate=pl.CostEstimate(
            flops=4 * rows * keys * width, transcendentals=heads * rows * keys, bytes_accessed=6 * heads * rows * keys
        ),
        name="attend",
    )(limits, starts, query, prior, *kv)


def attend_back_kernel(heads, scale, parts, starts, weights, context, d_mixed, inverse, query, *refs):
    kv, (d_scores, d_query, d_kv, total) = blocks_of(refs[:parts]), refs[parts:]
    width = context.shape[1]
    size = width // heads
    block = kv[0].shape[0]
    step = pl.program_id(0)
    spans = [pl.ds(pl.multiple_of(starts[e], block), block) for e in range(len(kv))]

    @pl.when(step == 0)
    def _():
        total[...] = jnp.zeros_like(total)

    scaled = d_mixed[...].astype(F32) * inverse[...]
    product = scaled * context[...].astype(F32)
    d_context = scaled.astype(BF16)
    d_context_t = scaled.T.astype(BF16)
    query_t = query[...].astype(F32).T.astype(BF16)
    for h in range(heads):
        own = slice(h * size, (h + 1) * size)
        other = slice(width + h * size, width + (h + 1) * size)
        mean = jnp.sum(product[:, own], -1, keepdims=True)
        changes, lows = [], []
        d_head = jnp.zeros((context.shape[0], size), F32)
        for e, span in enumerate(spans):
            d_weights = lax.dot_general(
                d_context[:, own], kv[e][:, other], (((1,), (1,)), ((), ())), preferred_element_type=F32
            )
            low = weights[h, :, span]
            change = (low.astype(F32) * (d_weights - mean)).astype(BF16)
            d_scores[0, h, :, span] = change
            d_head = d_head + jnp.dot(change, kv[e][:, own], preferred_element_type=F32)
            changes.append(change)
            lows.append(low)
        total[own, :] += jnp.dot(
            query_t[own, :], jnp.concatenate(changes, 1), preferred_element_type=F32
        )
        total[other, :] += jnp.dot(
            d_context_t[own, :], jnp.concatenate(lows, 1), preferred_element_type=F32
        )
        d_query[:, own] = scale * d_head

    @pl.when(step == pl.num_programs(0) - 1)
    def _():
        for e in range(len(kv)):
            d_kv[e] = total[:, e * block : (e + 1) * block].astype(BF16)


def attend_back(weights, kv, starts, context, d_mixed, inverse, query, scale):
    heads, rows, keys = weights.shape
    width = context.shape[1]
    block = kv[0].shape[1]
    tile = lambda i, *scalars: (i, 0)
    whole = lambda i, *scalars: (0, 0, 0)
    shape = (keys // block, 2 * width, block)
    return pl.pallas_call(
        partial(attend_back_kernel, heads, scale, len(kv)),
        grid_spec=pltpu.PrefetchScalarGridSpec(
            num_scalar_prefetch=1,
            grid=(rows // TILE,),
            in_specs=[pl.BlockSpec((heads, TILE, keys), lambda i, *scalars: (0, i, 0))]
            + [pl.BlockSpec((TILE, width), tile)] * 4
            + [pl.BlockSpec(part.shape, whole) for part in kv],
            out_specs=[
                pl.BlockSpec((1, heads, TILE, keys), lambda i, *scalars: (0, 0, i, 0)),
                pl.BlockSpec((TILE, width), tile),
                pl.BlockSpec(shape, whole),
            ],
            scratch_shapes=[pltpu.VMEM((2 * width, keys), F32)],
        ),
        out_shape=[
            jax.ShapeDtypeStruct((1, heads, rows, keys), BF16),
            jax.ShapeDtypeStruct((rows, width), F32),
            jax.ShapeDtypeStruct(shape, BF16),
        ],
        cost_estimate=pl.CostEstimate(
            flops=10 * rows * keys * width, transcendentals=0, bytes_accessed=6 * heads * rows * keys
        ),
        name="attend_back",
    )(starts, weights, context, d_mixed, inverse, query, *kv)


def pack_kernel(lead, place, squared, *refs):
    vectors, placed, out = refs[:-2], refs[-2], refs[-1]
    out[...] = jnp.zeros_like(out)
    for i, vector in enumerate(vectors):
        out[i : i + 1, :] = vector[...]
    out[len(vectors) : len(vectors) + 1, :] = jnp.broadcast_to(squared[...], (1, out.shape[1]))
    for p in range((out.shape[0] - lead) // placed.shape[0]):

        @pl.when(place[0] == p)
        def _():
            first = lead + p * placed.shape[0]
            out[first : first + placed.shape[0], :] = placed[...]


def pack(vectors, squared, placed, place, places):
    width = vectors[0].shape[0]
    vmem = pl.BlockSpec(memory_space=pltpu.VMEM)
    rows = placed.reshape(-1, width)
    return pl.pallas_call(
        partial(pack_kernel, 8),
        in_specs=[pl.BlockSpec(memory_space=pltpu.SMEM)] + [vmem] * (len(vectors) + 2),
        out_specs=vmem,
        out_shape=jax.ShapeDtypeStruct((8 + places * rows.shape[0], width), F32),
        name="pack",
    )(place.reshape(1), squared.reshape(1, 1), *[v.reshape(1, width) for v in vectors], rows)


def per_device(
    inputs,
    teacher_states,
    lengths,
    prev_logits,
    w_query,
    w_key,
    w_value,
    w_output,
    w_inner,
    w_outer,
    bias_query,
    bias_value,
    bias_output,
    bias_inner,
    bias_outer,
    gain_first,
    shift_first,
    gain_second,
    shift_second,
):
    tokens = inputs[0]
    row_count, model_width = tokens.shape
    heads_local = prev_logits.shape[1]
    width_local = w_query.shape[1]
    score_scale = 1.0 / math.sqrt(width_local // heads_local)
    seq_length = lengths[0]
    ctx_place, tp_place = lax.axis_index("ctx"), lax.axis_index("tp")
    tp_size = lax.axis_size("tp")
    part_rows = row_count // tp_size

    qkv_shard = jnp.concatenate([w_query.T, w_key.T, w_value.T], 0)
    full_qkv = gather_weight(qkv_shard, 1)
    output_half = jnp.concatenate([w_output] + rows_moved(w_output), 0)
    row_pos = ctx_place * row_count + jnp.arange(row_count, dtype=jnp.int32)
    limits = jnp.minimum((row_pos[::TILE] // BLK + 1) * BLK, seq_length)

    def own_rows(array):
        return lax.dynamic_slice_in_dim(array, tp_place * part_rows, part_rows, 0)

    tokens_first = own_first(tokens)
    query_scaled = dot32(tokens_first, full_qkv[:width_local], ((1,), (1,))) + bias_query
    query_scaled = (query_scaled.astype(BF16).astype(F32) * score_scale).astype(BF16)
    bias_kv = jnp.concatenate([jnp.zeros_like(bias_value), bias_value])
    kv_local = (dot32(tokens_first, full_qkv[width_local:], ((1,), (1,))) + bias_kv).astype(BF16)
    kv_local, output_half = tie(kv_local, output_half)
    kv_all, query_scaled = gather_parts(kv_local, query_scaled)
    output_moved, join_output = gather_late(output_half, 1)
    starts = (ctx_place ^ jnp.asarray(ctx_order(), jnp.int32)) * row_count
    all_count = VectorSum(seq_length.astype(F32), ("dp",)).total()

    logits, weights, context, inverse = attend(
        query_scaled, kv_all, starts, prev_logits, limits, heads_local
    )
    context_turned = rows_turn(context)
    context_turned, output_moved, w_inner, w_outer = tie(
        context_turned, output_moved, w_inner, w_outer
    )
    full_output = join_output(output_moved)
    inner_moved, join_inner = gather_late(w_inner, 0)
    outer_moved, join_outer = gather_late(w_outer, 1)
    context_mine = jnp.concatenate(rows_exchange(jnp.split(context_turned, tp_size, 0)), 1)
    attended = own_first(dot32(context_mine, full_output, ((1,), (0,))))
    first_sum = own_rows(tokens).astype(F32) + attended + bias_output
    normed_first, spread_first, hidden = norm_forward(first_sum, gain_first, shift_first)
    hidden_first = own_first(hidden.astype(BF16))
    hidden_moved = rows_moved(hidden_first)
    full_inner, full_outer = join_inner(inner_moved), join_outer(outer_moved)
    hidden_low = jnp.concatenate([hidden_first] + hidden_moved, 0)
    pre_act = dot32(hidden_low, full_inner, ((1,), (0,))) + bias_inner
    act_low = jax.nn.gelu(pre_act, approximate=False).astype(BF16)
    fed = own_first(rows_sum(dot32(act_low, full_outer, ((1,), (0,)))))
    second_sum = hidden + fed + bias_outer
    normed_second, spread_second, result = norm_forward(second_sum, gain_second, shift_second)
    valid_rows = (own_rows(row_pos) < seq_length).astype(F32)
    deviation = result - own_rows(teacher_states[0]).astype(F32)
    local_squared = jnp.sum(valid_rows[:, None] * deviation * deviation)
    token_total = row_count * lax.axis_size("ctx") * lax.axis_size("dp")
    d_out = 2.0 * token_total / all_count * valid_rows[:, None] * deviation
    d_second, grad_gain_second, grad_shift_second = norm_backward(
        d_out, normed_second, spread_second, gain_second
    )
    grad_bias_outer = jnp.sum(d_second, 0)
    d_second_low = rows_gather(own_first(d_second.astype(BF16)))
    d_act = dot32(d_second_low, full_outer, ((1,), (1,)))
    gelu_back = jax.vjp(partial(jax.nn.gelu, approximate=False), pre_act)[1]
    d_pre = gelu_back(d_act)[0]
    grad_bias_inner = jnp.sum(d_pre, 0)
    d_pre_low = d_pre.astype(BF16)
    hidden_part = rows_sum(dot32(d_pre_low, full_inner, ((1,), (1,))))
    outer_sum = WeightSum(dot32(act_low, d_second_low, ((0,), (0,))), 1, True)
    inner_sum = WeightSum(dot32(hidden_low, d_pre_low, ((0,), (0,))), 0)
    d_hidden = d_second + own_first(hidden_part)
    d_first, grad_gain_first, grad_shift_first = norm_backward(
        d_hidden, normed_first, spread_first, gain_first
    )
    grad_bias_output = jnp.sum(d_first, 0)
    d_first_low = own_first(d_first.astype(BF16))
    d_context_mine = dot32(d_first_low, full_output, ((1,), (1,))).astype(BF16)
    d_context = jnp.concatenate(rows_exchange(jnp.split(d_context_mine, tp_size, 1)), 0)
    d_context = rows_turn(d_context)

    packed = (
        pack(
            [
                grad_bias_output,
                grad_bias_outer,
                grad_gain_first,
                grad_shift_first,
                grad_gain_second,
                grad_shift_second,
            ],
            local_squared,
            grad_bias_inner,
            tp_place,
            tp_size,
        )
    )
    early_sum = VectorSum(packed, ("dp", "ctx", "tp"))
    d_context, outer_sum.moved, inner_sum.moved = tie(
        d_context, outer_sum.moved, inner_sum.moved
    )
    outer_sum.step()
    inner_sum.step()
    both_mine = jnp.concatenate([d_first_low, result.astype(BF16)], 1)
    both_mine, _ = tie(both_mine, d_context)
    both_moved = rows_moved(both_mine)
    d_scores, d_query, d_kv_parts = attend_back(
        weights, kv_all, starts, context, d_context, inverse, query_scaled, score_scale
    )
    d_kv_parts, early_sum.moved = tie(d_kv_parts, early_sum.moved)
    early_sum.step()
    d_kv = scatter_parts(d_kv_parts)
    d_query_low = d_query.astype(BF16)
    d_kv_low, inner_sum.moved, outer_sum.moved, early_sum.moved, *both_moved = tie(
        d_kv.astype(BF16), inner_sum.moved, outer_sum.moved, early_sum.moved, *both_moved
    )
    inner_sum.step()
    outer_sum.step()
    early_sum.step()
    both = jnp.concatenate([both_mine] + both_moved, 0)
    d_first_all = both[:, :model_width]
    output_gradient = dot32(context_turned, d_first_all, ((0,), (0,)))
    output_sum = WeightSum(output_gradient, 1, True)
    d_qkv_low = jnp.concatenate([d_query_low, d_kv_low.T], 1)
    tokens_part = rows_sum(dot32(rows_turn(d_qkv_low), full_qkv, ((1,), (0,))))
    qkv_gradient = dot32(d_qkv_low, tokens_first, ((0,), (0,)))
    qkv_sum = WeightSum(qkv_gradient, 1, True)
    late_vector = jnp.concatenate([jnp.sum(d_query, 0), jnp.sum(d_kv[width_local:], 1)])
    late_sum = VectorSum(late_vector, ("dp", "ctx"))
    grad_mine = (d_first + own_first(tokens_part)).astype(BF16)
    sums = (output_sum, early_sum, qkv_sum, late_sum)
    grad_mine, *moved = tie(grad_mine, *[one.moved for one in sums])
    for one, value in zip(sums, moved):
        one.moved = value
    for one in sums:
        one.step()
    grad_moved = rows_moved(grad_mine)
    inner_shard, outer_shard = inner_sum.total(), outer_sum.total()
    result_all = rows_turn(both[:, model_width:]).astype(F32)
    grad_moved[-1], inner_shard, outer_shard, result_all = tie(
        grad_moved[-1], inner_shard, outer_shard, result_all
    )
    grad_inputs = rows_turn(jnp.concatenate([grad_mine] + grad_moved, 0)).astype(F32)
    output_shard = output_sum.total()
    shard_qkv = qkv_sum.total()
    early = early_sum.total()
    loss_value = early[6, 0] / (all_count * model_width)
    inner_rows = grad_bias_inner.shape[0] // model_width
    sum_bias_inner = lax.dynamic_slice_in_dim(early, 8 + tp_place * inner_rows, inner_rows, 0).reshape(-1)
    late = late_sum.total()
    return (
        result_all[None],
        logits,
        loss_value,
        grad_inputs[None],
        d_scores,
        shard_qkv[:width_local].T,
        shard_qkv[width_local : 2 * width_local].T,
        shard_qkv[2 * width_local :].T,
        output_shard,
        inner_shard,
        outer_shard,
        late[:width_local],
        late[width_local:],
        early[0],
        sum_bias_inner,
        early[1],
        early[2],
        early[3],
        early[4],
        early[5],
    )


def solution(mesh):
    placed = (
        P("dp", "ctx", None),
        P("dp", "ctx", None),
        P("dp"),
        P("dp", "tp", "ctx", None),
        P("dp", "tp"),
        P("dp", "tp"),
        P("dp", "tp"),
        P("tp", "dp"),
        P("dp", "tp"),
        P("tp", "dp"),
        P("tp"),
        P("tp"),
        P(),
        P("tp"),
        P(),
        P(),
        P(),
        P(),
        P(),
    )
    return jax.shard_map(
        per_device,
        mesh=mesh,
        in_specs=placed,
        out_specs=(
            P("dp", "ctx", None),
            P("dp", "tp", "ctx", None),
            P(),
            P("dp", "ctx", None),
            P("dp", "tp", "ctx", None),
            P("dp", "tp"),
            P("dp", "tp"),
            P("dp", "tp"),
            P("tp", "dp"),
            P("dp", "tp"),
            P("tp", "dp"),
            P("tp"),
            P("tp"),
            P(),
            P("tp"),
            P(),
            P(),
            P(),
            P(),
            P(),
        ),
        check_vma=False,
    )
```

```python
from functools import partial
import math

import jax
import jax.numpy as jnp
from jax import lax
from jax.experimental import pallas as pl
from jax.experimental.pallas import tpu as pltpu
from jax.sharding import PartitionSpec as P

BLK = 256


EPS = 1e-06
MASKED = -1e30


def norm_forward(total, gain_vec, shift_vec):
    center = total - jnp.mean(total, -1, keepdims=True)
    spread = lax.rsqrt(jnp.mean(center * center, -1, keepdims=True) + EPS)
    normed = center * spread
    return (normed, spread, normed * gain_vec + shift_vec)


def norm_backward(gradient, normed, spread, gain_vec):
    scaled = gradient * gain_vec
    inner_term = (
        scaled
        - jnp.mean(scaled, -1, keepdims=True)
        - normed * jnp.mean(scaled * normed, -1, keepdims=True)
    )
    return (inner_term * spread, jnp.sum(gradient * normed, 0), jnp.sum(gradient, 0))


F32, BF16 = jnp.float32, jnp.bfloat16


def dot32(left, right, dims):
    return lax.dot_general(left, right, (dims, ((), ())), preferred_element_type=F32)


def shifted(block, axis, step):
    size = lax.axis_size(axis)
    return lax.ppermute(block, axis, [(i, (i + step) % size) for i in range(size)])


def flipped(block, axis, bit):
    size = lax.axis_size(axis)
    return lax.ppermute(block, axis, [(i, i ^ bit) for i in range(size)])


def tie(*values):
    return lax.optimization_barrier(values)


def own_first(array):
    if lax.axis_size("dp") != 2:
        return array
    half = array.shape[-1] // 2
    turned = jnp.concatenate([array[..., half:], array[..., :half]], -1)
    return jnp.where(lax.axis_index("dp") == 0, array, turned)


def gather_weight(shard, dim):
    if lax.axis_size("dp") != 2:
        return lax.all_gather(shard, "dp", axis=dim, tiled=True)
    return jnp.concatenate([shard, flipped(shard, "dp", 1)], dim)


def gather_late(shard, dim):
    if lax.axis_size("dp") != 2:
        return gather_weight(shard, dim), lambda moved: moved
    moved = flipped(shard, "dp", 1)
    return moved, lambda moved: jnp.concatenate([shard, moved], dim)


class WeightSum:
    def __init__(self, gradient, dim, far_first=False):
        self.bits = []
        bit = 1
        while bit < lax.axis_size("ctx"):
            self.bits.append(bit)
            bit *= 2
        if far_first:
            self.bits.reverse()
        if lax.axis_size("dp") == 2:
            kept, given = jnp.split(gradient, 2, dim)
            self.kept, self.moved = kept, flipped(given.astype(BF16), "dp", 1)
        else:
            low = gradient.astype(BF16)
            self.moved = lax.psum_scatter(low, "dp", scatter_dimension=dim, tiled=True)
            self.kept = jnp.zeros(self.moved.shape, F32)

    def step(self):
        low = (self.kept.astype(F32) + self.moved.astype(F32)).astype(BF16)
        self.kept, self.moved = low, flipped(low, "ctx", self.bits.pop(0))

    def total(self):
        while self.bits:
            self.step()
        return self.kept.astype(F32) + self.moved.astype(F32)


class VectorSum:
    def __init__(self, vector, axes, far_first=False):
        self.bits = []
        for axis in axes:
            bit = 1
            while bit < lax.axis_size(axis):
                self.bits.append((axis, bit))
                bit *= 2
        if far_first:
            self.bits.reverse()
        self.kept, self.moved = vector, flipped(vector, *self.bits.pop(0))

    def step(self):
        summed = self.kept + self.moved
        self.kept, self.moved = summed, flipped(summed, *self.bits.pop(0))

    def total(self):
        while self.bits:
            self.step()
        return self.kept + self.moved


def ctx_order():
    order, bit = [0], lax.axis_size("ctx") // 2
    while bit:
        order = order + [e ^ bit for e in order]
        bit //= 2
    return order


def gather_parts(block, beside):
    held, bit = [block[None]], lax.axis_size("ctx") // 2
    while bit:
        sent = held[0] if len(held) == 1 else jnp.concatenate(held, 0)
        held.append(flipped(sent, "ctx", bit))
        if bit == lax.axis_size("ctx") // 2:
            held[-1], beside = tie(held[-1], beside)
        bit //= 2
    return held, beside


def scatter_parts(blocks, sent):
    size, bit = lax.axis_size("ctx"), 1
    while bit < size:
        blocks = blocks.astype(F32) + flipped(sent.astype(BF16), "ctx", bit).astype(F32)
        half = blocks.shape[0] // 2
        if half:
            blocks, sent = blocks[:half], blocks[half:]
        bit *= 2
    return blocks[0]


def rows_turn(block):
    size = lax.axis_size("tp")
    place = lax.axis_index("tp")
    blocks = block.reshape((size, block.shape[0] // size) + block.shape[1:])
    return jnp.concatenate(
        [
            lax.dynamic_index_in_dim(blocks, lax.rem(place - e + size, size), 0, False)
            for e in range(size)
        ],
        0,
    )


def rows_place(blocks):
    size = lax.axis_size("tp")
    place = lax.axis_index("tp")
    return jnp.concatenate(
        [lax.select_n(lax.rem(place - p + size, size), *blocks) for p in range(size)], 0
    )


def columns_turn(block):
    size = lax.axis_size("tp")
    place = lax.axis_index("tp")
    blocks = jnp.split(block, size, 1)
    return jnp.concatenate(
        [lax.select_n(lax.rem(place - e + size, size), *blocks) for e in range(size)], 1
    )


def rows_sum(total):
    size = lax.axis_size("tp")
    rows = total.shape[0] // size
    low = total.astype(BF16)
    moved = []
    for e in range(1, size):
        moved.append(shifted(low[e * rows : (e + 1) * rows], "tp", size - e))
    kept = total[:rows]
    for block in moved:
        kept = kept + block.astype(F32)
    return kept


def rows_moved(block):
    moved = []
    for e in range(1, lax.axis_size("tp")):
        moved.append(shifted(block, "tp", e))
    return moved


def rows_gather(block):
    return jnp.concatenate([block] + rows_moved(block), 0)


def rows_exchange(blocks):
    size = lax.axis_size("tp")
    return [blocks[0]] + [shifted(blocks[size - j], "tp", j) for j in range(1, size)]


TILE = 256


def blocks_of(refs):
    return [ref.at[b] for ref in refs for b in range(ref.shape[0])]


def attend_kernel(heads, parts, limits, starts, query, prior, *refs):
    kv, (logits, weights, context, inverse) = blocks_of(refs[:parts]), refs[parts:]
    limit = limits[pl.program_id(0)]
    rows, width = query.shape
    size = width // heads
    block = kv[0].shape[0]
    column = lax.broadcasted_iota(jnp.int32, (rows, block), 1)
    spans = [pl.ds(pl.multiple_of(starts[e], block), block) for e in range(len(kv))]
    for h in range(heads):
        own = slice(h * size, (h + 1) * size)
        masked = []
        for e, span in enumerate(spans):
            raw = lax.dot_general(
                query[:, own], kv[e][:, own], (((1,), (1,)), ((), ())), preferred_element_type=F32
            )
            score = prior[0, h, :, span].astype(F32) + raw
            logits[0, h, :, span] = score.astype(BF16)
            masked.append(jnp.where(column < limit - starts[e], score, MASKED))
        top = jnp.max(masked[0], -1, keepdims=True)
        for part in masked[1:]:
            top = jnp.maximum(top, jnp.max(part, -1, keepdims=True))
        count = jnp.zeros((rows, 1), F32)
        mixed = jnp.zeros((rows, size), F32)
        for e, span in enumerate(spans):
            exponent = jnp.exp(masked[e] - top)
            count = count + jnp.sum(exponent, -1, keepdims=True)
            low = exponent.astype(BF16)
            weights[h, :, span] = low
            mixed = mixed + jnp.dot(
                low, kv[e][:, width + h * size : width + (h + 1) * size], preferred_element_type=F32
            )
        scale = 1.0 / count
        context[:, own] = (mixed * scale).astype(BF16)
        inverse[:, own] = jnp.broadcast_to(scale, (rows, size))


def attend(query, kv, starts, prior, limits, heads):
    rows, width = query.shape
    keys = prior.shape[3]
    tile = lambda i, *scalars: (i, 0)
    whole = lambda i, *scalars: (0, 0, 0)
    cube = lambda i, *scalars: (0, i, 0)
    quad = lambda i, *scalars: (0, 0, i, 0)
    return pl.pallas_call(
        partial(attend_kernel, heads, len(kv)),
        grid_spec=pltpu.PrefetchScalarGridSpec(
            num_scalar_prefetch=2,
            grid=(rows // TILE,),
            in_specs=[pl.BlockSpec((TILE, width), tile), pl.BlockSpec((1, heads, TILE, keys), quad)]
            + [pl.BlockSpec(part.shape, whole) for part in kv],
            out_specs=[
                pl.BlockSpec((1, heads, TILE, keys), quad),
                pl.BlockSpec((heads, TILE, keys), cube),
                pl.BlockSpec((TILE, width), tile),
                pl.BlockSpec((TILE, width), tile),
            ],
        ),
        out_shape=[
            jax.ShapeDtypeStruct((1, heads, rows, keys), BF16),
            jax.ShapeDtypeStruct((heads, rows, keys), BF16),
            jax.ShapeDtypeStruct((rows, width), BF16),
            jax.ShapeDtypeStruct((rows, width), F32),
        ],
        cost_estimate=pl.CostEstimate(
            flops=4 * rows * keys * width, transcendentals=heads * rows * keys, bytes_accessed=6 * heads * rows * keys
        ),
        name="attend",
    )(limits, starts, query, prior, *kv)


def attend_back_kernel(heads, scale, parts, starts, weights, context, d_mixed, inverse, query, *refs):
    kv, (d_scores, d_query, d_kept, d_sent, total) = blocks_of(refs[:parts]), refs[parts:]
    width = context.shape[1]
    size = width // heads
    block = kv[0].shape[0]
    step = pl.program_id(0)
    spans = [pl.ds(pl.multiple_of(starts[e], block), block) for e in range(len(kv))]

    @pl.when(step == 0)
    def _():
        total[...] = jnp.zeros_like(total)

    scaled = d_mixed[...].astype(F32) * inverse[...]
    product = scaled * context[...].astype(F32)
    d_context = scaled.astype(BF16)
    d_context_t = scaled.T.astype(BF16)
    query_t = query[...].astype(F32).T.astype(BF16)
    for h in range(heads):
        own = slice(h * size, (h + 1) * size)
        other = slice(width + h * size, width + (h + 1) * size)
        mean = jnp.sum(product[:, own], -1, keepdims=True)
        changes, lows = [], []
        d_head = jnp.zeros((context.shape[0], size), F32)
        for e, span in enumerate(spans):
            d_weights = lax.dot_general(
                d_context[:, own], kv[e][:, other], (((1,), (1,)), ((), ())), preferred_element_type=F32
            )
            low = weights[h, :, span]
            change = (low.astype(F32) * (d_weights - mean)).astype(BF16)
            d_scores[0, h, :, span] = change
            d_head = d_head + jnp.dot(change, kv[e][:, own], preferred_element_type=F32)
            changes.append(change)
            lows.append(low)
        total[own, :] += jnp.dot(
            query_t[own, :], jnp.concatenate(changes, 1), preferred_element_type=F32
        )
        total[other, :] += jnp.dot(
            d_context_t[own, :], jnp.concatenate(lows, 1), preferred_element_type=F32
        )
        d_query[:, own] = scale * d_head

    @pl.when(step == pl.num_programs(0) - 1)
    def _():
        for e in range(len(kv)):
            half = d_kept.shape[0]
            target, index = (d_kept, e) if e < half else (d_sent, e - half)
            target[index] = total[:, e * block : (e + 1) * block].astype(BF16)


def attend_back(weights, kv, starts, context, d_mixed, inverse, query, scale):
    heads, rows, keys = weights.shape
    width = context.shape[1]
    block = kv[0].shape[1]
    tile = lambda i, *scalars: (i, 0)
    whole = lambda i, *scalars: (0, 0, 0)
    shape = (keys // block // 2, 2 * width, block)
    return pl.pallas_call(
        partial(attend_back_kernel, heads, scale, len(kv)),
        grid_spec=pltpu.PrefetchScalarGridSpec(
            num_scalar_prefetch=1,
            grid=(rows // TILE,),
            in_specs=[pl.BlockSpec((heads, TILE, keys), lambda i, *scalars: (0, i, 0))]
            + [pl.BlockSpec((TILE, width), tile)] * 4
            + [pl.BlockSpec(part.shape, whole) for part in kv],
            out_specs=[
                pl.BlockSpec((1, heads, TILE, keys), lambda i, *scalars: (0, 0, i, 0)),
                pl.BlockSpec((TILE, width), tile),
                pl.BlockSpec(shape, whole),
                pl.BlockSpec(shape, whole),
            ],
            scratch_shapes=[pltpu.VMEM((2 * width, keys), F32)],
        ),
        out_shape=[
            jax.ShapeDtypeStruct((1, heads, rows, keys), BF16),
            jax.ShapeDtypeStruct((rows, width), F32),
            jax.ShapeDtypeStruct(shape, BF16),
            jax.ShapeDtypeStruct(shape, BF16),
        ],
        cost_estimate=pl.CostEstimate(
            flops=10 * rows * keys * width, transcendentals=0, bytes_accessed=6 * heads * rows * keys
        ),
        name="attend_back",
    )(starts, weights, context, d_mixed, inverse, query, *kv)


def pack_kernel(lead, place, squared, *refs):
    vectors, placed, out = refs[:-2], refs[-2], refs[-1]
    out[...] = jnp.zeros_like(out)
    for i, vector in enumerate(vectors):
        out[i : i + 1, :] = vector[...]
    out[len(vectors) : len(vectors) + 1, :] = jnp.broadcast_to(squared[...], (1, out.shape[1]))
    for p in range((out.shape[0] - lead) // placed.shape[0]):

        @pl.when(place[0] == p)
        def _():
            first = lead + p * placed.shape[0]
            out[first : first + placed.shape[0], :] = placed[...]


def pack(vectors, squared, placed, place, places):
    width = vectors[0].shape[0]
    vmem = pl.BlockSpec(memory_space=pltpu.VMEM)
    rows = placed.reshape(-1, width)
    return pl.pallas_call(
        partial(pack_kernel, 8),
        in_specs=[pl.BlockSpec(memory_space=pltpu.SMEM)] + [vmem] * (len(vectors) + 2),
        out_specs=vmem,
        out_shape=jax.ShapeDtypeStruct((8 + places * rows.shape[0], width), F32),
        name="pack",
    )(place.reshape(1), squared.reshape(1, 1), *[v.reshape(1, width) for v in vectors], rows)


def per_device(
    inputs,
    teacher_states,
    lengths,
    prev_logits,
    w_query,
    w_key,
    w_value,
    w_output,
    w_inner,
    w_outer,
    bias_query,
    bias_value,
    bias_output,
    bias_inner,
    bias_outer,
    gain_first,
    shift_first,
    gain_second,
    shift_second,
):
    tokens = inputs[0]
    row_count, model_width = tokens.shape
    heads_local = prev_logits.shape[1]
    width_local = w_query.shape[1]
    score_scale = 1.0 / math.sqrt(width_local // heads_local)
    seq_length = lengths[0]
    ctx_place, tp_place = lax.axis_index("ctx"), lax.axis_index("tp")
    tp_size = lax.axis_size("tp")
    part_rows = row_count // tp_size

    qkv_shard = jnp.concatenate([w_query.T, w_key.T, w_value.T], 0)
    full_qkv = gather_weight(qkv_shard, 1)
    output_half = jnp.concatenate([w_output] + rows_moved(w_output), 0)
    row_pos = ctx_place * row_count + jnp.arange(row_count, dtype=jnp.int32)
    limits = jnp.minimum((row_pos[::TILE] // BLK + 1) * BLK, seq_length)

    def own_rows(array):
        return lax.dynamic_slice_in_dim(array, tp_place * part_rows, part_rows, 0)

    tokens_first = own_first(tokens)
    query_scaled = dot32(tokens_first, full_qkv[:width_local], ((1,), (1,))) + bias_query
    query_scaled = (query_scaled.astype(BF16).astype(F32) * score_scale).astype(BF16)
    bias_kv = jnp.concatenate([jnp.zeros_like(bias_value), bias_value])
    kv_local = (dot32(tokens_first, full_qkv[width_local:], ((1,), (1,))) + bias_kv).astype(BF16)
    kv_local, output_half = tie(kv_local, output_half)
    kv_all, query_scaled = gather_parts(kv_local, query_scaled)
    output_moved, join_output = gather_late(output_half, 1)
    starts = (ctx_place ^ jnp.asarray(ctx_order(), jnp.int32)) * row_count
    all_count = VectorSum(seq_length.astype(F32), ("dp",)).total()

    logits, weights, context, inverse = attend(
        query_scaled, kv_all, starts, prev_logits, limits, heads_local
    )
    context_turned = rows_turn(context)
    context_turned, output_moved, w_inner, w_outer = tie(
        context_turned, output_moved, w_inner, w_outer
    )
    full_output = join_output(output_moved)
    inner_moved, join_inner = gather_late(w_inner, 0)
    outer_moved, join_outer = gather_late(w_outer, 1)
    context_mine = jnp.concatenate(rows_exchange(jnp.split(context_turned, tp_size, 0)), 1)
    attended = own_first(dot32(context_mine, full_output, ((1,), (0,))))
    first_sum = own_rows(tokens).astype(F32) + attended + bias_output
    normed_first, spread_first, hidden = norm_forward(first_sum, gain_first, shift_first)
    hidden_first = own_first(hidden.astype(BF16))
    hidden_moved = rows_moved(hidden_first)
    full_inner, full_outer = join_inner(inner_moved), join_outer(outer_moved)
    hidden_low = jnp.concatenate([hidden_first] + hidden_moved, 0)
    pre_act = dot32(hidden_low, full_inner, ((1,), (0,))) + bias_inner
    act_low = jax.nn.gelu(pre_act, approximate=False).astype(BF16)
    fed = own_first(rows_sum(dot32(act_low, full_outer, ((1,), (0,)))))
    second_sum = hidden + fed + bias_outer
    normed_second, spread_second, result = norm_forward(second_sum, gain_second, shift_second)
    valid_rows = (own_rows(row_pos) < seq_length).astype(F32)
    deviation = result - own_rows(teacher_states[0]).astype(F32)
    local_squared = jnp.sum(valid_rows[:, None] * deviation * deviation)
    token_total = row_count * lax.axis_size("ctx") * lax.axis_size("dp")
    d_out = 2.0 * token_total / all_count * valid_rows[:, None] * deviation
    d_second, grad_gain_second, grad_shift_second = norm_backward(
        d_out, normed_second, spread_second, gain_second
    )
    grad_bias_outer = jnp.sum(d_second, 0)
    d_second_low = rows_gather(own_first(d_second.astype(BF16)))
    d_act = dot32(d_second_low, full_outer, ((1,), (1,)))
    gelu_back = jax.vjp(partial(jax.nn.gelu, approximate=False), pre_act)[1]
    d_pre = gelu_back(d_act)[0]
    grad_bias_inner = jnp.sum(d_pre, 0)
    d_pre_low = d_pre.astype(BF16)
    hidden_part = rows_sum(dot32(d_pre_low, full_inner, ((1,), (1,))))
    outer_sum = WeightSum(dot32(act_low, d_second_low, ((0,), (0,))), 1, True)
    inner_sum = WeightSum(dot32(hidden_low, d_pre_low, ((0,), (0,))), 0)
    d_hidden = d_second + own_first(hidden_part)
    d_first, grad_gain_first, grad_shift_first = norm_backward(
        d_hidden, normed_first, spread_first, gain_first
    )
    grad_bias_output = jnp.sum(d_first, 0)
    d_first_low = own_first(d_first.astype(BF16))
    d_context_mine = dot32(d_first_low, full_output, ((1,), (1,))).astype(BF16)
    d_context = rows_place(rows_exchange(jnp.split(d_context_mine, tp_size, 1)))

    packed = (
        pack(
            [
                grad_bias_output,
                grad_bias_outer,
                grad_gain_first,
                grad_shift_first,
                grad_gain_second,
                grad_shift_second,
            ],
            local_squared,
            grad_bias_inner,
            tp_place,
            tp_size,
        )
    )
    early_sum = VectorSum(packed, ("dp", "ctx"))
    d_context, outer_sum.moved, inner_sum.moved = tie(
        d_context, outer_sum.moved, inner_sum.moved
    )
    outer_sum.step()
    inner_sum.step()
    both_mine = jnp.concatenate([d_first_low, result.astype(BF16)], 1)
    both_mine, _ = tie(both_mine, d_context)
    both_moved = rows_moved(both_mine)
    d_scores, d_query, d_kept, d_sent = attend_back(
        weights, kv_all, starts, context, d_context, inverse, query_scaled, score_scale
    )
    d_sent, early_sum.moved = tie(d_sent, early_sum.moved)
    early_sum.step()
    d_kv = scatter_parts(d_kept, d_sent)
    d_query_low = d_query.astype(BF16)
    d_kv_low, inner_sum.moved, outer_sum.moved, early_sum.moved = tie(
        d_kv.astype(BF16), inner_sum.moved, outer_sum.moved, early_sum.moved
    )
    tokens_part = rows_sum(
        dot32(rows_turn(d_query_low), full_qkv[:width_local], ((1,), (0,)))
        + dot32(columns_turn(d_kv_low), full_qkv[width_local:], ((0,), (0,))),
    )
    inner_sum.step()
    outer_sum.step()
    early_sum.step()
    query_gradient = dot32(d_query_low, tokens_first, ((0,), (0,)))
    kv_gradient = dot32(d_kv_low, tokens_first, ((1,), (0,)))
    qkv_gradient = jnp.concatenate([query_gradient, kv_gradient], 0)
    qkv_sum = WeightSum(qkv_gradient, 1, True)
    both = [both_mine] + both_moved
    output_gradient = sum(
        dot32(rows, moved[:, :model_width], ((0,), (0,)))
        for rows, moved in zip(jnp.split(context_turned, tp_size, 0), both)
    )
    output_sum = WeightSum(output_gradient, 1, True)
    late_vector = jnp.concatenate([jnp.sum(d_query, 0), jnp.sum(d_kv[width_local:], 1)])
    late_sum = VectorSum(late_vector, ("dp", "ctx"), True)
    grad_mine = (d_first + own_first(tokens_part)).astype(BF16)
    sums = (output_sum, early_sum, qkv_sum, late_sum)
    grad_mine, *moved = tie(grad_mine, *[one.moved for one in sums])
    for one, value in zip(sums, moved):
        one.moved = value
    early = early_sum.total()
    moved = []
    for e in range(1, tp_size):
        moved.append(flipped(early, "tp", e))
    early = [early] + moved
    while len(early) > 1:
        early = [left + right for left, right in zip(early[::2], early[1::2])]
    early = early[0]
    for one in (output_sum, qkv_sum, late_sum):
        one.step()
    grad_moved = rows_moved(grad_mine)
    inner_shard, outer_shard = inner_sum.total(), outer_sum.total()
    result_all = rows_place([block[:, model_width:] for block in both]).astype(F32)
    grad_moved[-1], inner_shard, outer_shard, result_all = tie(
        grad_moved[-1], inner_shard, outer_shard, result_all
    )
    grad_inputs = rows_place([grad_mine] + grad_moved).astype(F32)
    output_shard = output_sum.total()
    shard_qkv = qkv_sum.total()
    loss_value = early[6, 0] / (all_count * model_width)
    inner_rows = grad_bias_inner.shape[0] // model_width
    sum_bias_inner = lax.dynamic_slice_in_dim(early, 8 + tp_place * inner_rows, inner_rows, 0).reshape(-1)
    late = late_sum.total()
    return (
        result_all[None],
        logits,
        loss_value,
        grad_inputs[None],
        d_scores,
        shard_qkv[:width_local].T,
        shard_qkv[width_local : 2 * width_local].T,
        shard_qkv[2 * width_local :].T,
        output_shard,
        inner_shard,
        outer_shard,
        late[:width_local],
        late[width_local:],
        early[0],
        sum_bias_inner,
        early[1],
        early[2],
        early[3],
        early[4],
        early[5],
    )


def solution(mesh):
    placed = (
        P("dp", "ctx", None),
        P("dp", "ctx", None),
        P("dp"),
        P("dp", "tp", "ctx", None),
        P("dp", "tp"),
        P("dp", "tp"),
        P("dp", "tp"),
        P("tp", "dp"),
        P("dp", "tp"),
        P("tp", "dp"),
        P("tp"),
        P("tp"),
        P(),
        P("tp"),
        P(),
        P(),
        P(),
        P(),
        P(),
    )
    return jax.shard_map(
        per_device,
        mesh=mesh,
        in_specs=placed,
        out_specs=(
            P("dp", "ctx", None),
            P("dp", "tp", "ctx", None),
            P(),
            P("dp", "ctx", None),
            P("dp", "tp", "ctx", None),
            P("dp", "tp"),
            P("dp", "tp"),
            P("dp", "tp"),
            P("tp", "dp"),
            P("dp", "tp"),
            P("tp", "dp"),
            P("tp"),
            P("tp"),
            P(),
            P("tp"),
            P(),
            P(),
            P(),
            P(),
            P(),
        ),
        check_vma=False,
    )
```

```python
from functools import partial
import math

import jax
import jax.numpy as jnp
from jax import lax
from jax.experimental import pallas as pl
from jax.experimental.pallas import tpu as pltpu
from jax.sharding import PartitionSpec as P

BLK = 256


EPS = 1e-06
MASKED = -1e30


def norm_forward(total, gain_vec, shift_vec):
    center = total - jnp.mean(total, -1, keepdims=True)
    spread = lax.rsqrt(jnp.mean(center * center, -1, keepdims=True) + EPS)
    normed = center * spread
    return (normed, spread, normed * gain_vec + shift_vec)


def norm_backward(gradient, normed, spread, gain_vec):
    scaled = gradient * gain_vec
    inner_term = (
        scaled
        - jnp.mean(scaled, -1, keepdims=True)
        - normed * jnp.mean(scaled * normed, -1, keepdims=True)
    )
    return (inner_term * spread, jnp.sum(gradient * normed, 0), jnp.sum(gradient, 0))


F32, BF16 = jnp.float32, jnp.bfloat16


def dot32(left, right, dims):
    return lax.dot_general(left, right, (dims, ((), ())), preferred_element_type=F32)


def shifted(block, axis, step):
    size = lax.axis_size(axis)
    return lax.ppermute(block, axis, [(i, (i + step) % size) for i in range(size)])


def flipped(block, axis, bit):
    size = lax.axis_size(axis)
    return lax.ppermute(block, axis, [(i, i ^ bit) for i in range(size)])


def tie(*values):
    return lax.optimization_barrier(values)


def own_first(array):
    if lax.axis_size("dp") != 2:
        return array
    half = array.shape[-1] // 2
    turned = jnp.concatenate([array[..., half:], array[..., :half]], -1)
    return jnp.where(lax.axis_index("dp") == 0, array, turned)


def gather_weight(shard, dim):
    if lax.axis_size("dp") != 2:
        return lax.all_gather(shard, "dp", axis=dim, tiled=True)
    return jnp.concatenate([shard, flipped(shard, "dp", 1)], dim)


def gather_late(shard, dim):
    if lax.axis_size("dp") != 2:
        return gather_weight(shard, dim), lambda moved: moved
    moved = flipped(shard, "dp", 1)
    return moved, lambda moved: jnp.concatenate([shard, moved], dim)


class WeightSum:
    def __init__(self, gradient, dim, far_first=False):
        self.bits = []
        bit = 1
        while bit < lax.axis_size("ctx"):
            self.bits.append(bit)
            bit *= 2
        if far_first:
            self.bits.reverse()
        if lax.axis_size("dp") == 2:
            kept, given = jnp.split(gradient, 2, dim)
            self.kept, self.moved = kept, flipped(given.astype(BF16), "dp", 1)
        else:
            low = gradient.astype(BF16)
            self.moved = lax.psum_scatter(low, "dp", scatter_dimension=dim, tiled=True)
            self.kept = jnp.zeros(self.moved.shape, F32)

    def step(self):
        low = (self.kept.astype(F32) + self.moved.astype(F32)).astype(BF16)
        self.kept, self.moved = low, flipped(low, "ctx", self.bits.pop(0))

    def total(self):
        while self.bits:
            self.step()
        return self.kept.astype(F32) + self.moved.astype(F32)


class VectorSum:
    def __init__(self, vector, axes, far_first=False):
        self.bits = []
        for axis in axes:
            bit = 1
            while bit < lax.axis_size(axis):
                self.bits.append((axis, bit))
                bit *= 2
        if far_first:
            self.bits.reverse()
        self.kept, self.moved = vector, flipped(vector, *self.bits.pop(0))

    def step(self):
        summed = self.kept + self.moved
        self.kept, self.moved = summed, flipped(summed, *self.bits.pop(0))

    def total(self):
        while self.bits:
            self.step()
        return self.kept + self.moved


def ctx_order():
    order, bit = [0], lax.axis_size("ctx") // 2
    while bit:
        order = order + [e ^ bit for e in order]
        bit //= 2
    return order


def gather_parts(block, beside):
    held, bit = [block[None]], lax.axis_size("ctx") // 2
    while bit:
        sent = held[0] if len(held) == 1 else jnp.concatenate(held, 0)
        held.append(flipped(sent, "ctx", bit))
        if bit == lax.axis_size("ctx") // 2:
            held[-1], beside = tie(held[-1], beside)
        bit //= 2
    return held, beside


def scatter_parts(blocks, sent):
    size, bit = lax.axis_size("ctx"), 1
    while bit < size:
        blocks = blocks.astype(F32) + flipped(sent.astype(BF16), "ctx", bit).astype(F32)
        half = blocks.shape[0] // 2
        if half:
            blocks, sent = blocks[:half], blocks[half:]
        bit *= 2
    return blocks[0]


def rows_turn(block):
    size = lax.axis_size("tp")
    place = lax.axis_index("tp")
    blocks = block.reshape((size, block.shape[0] // size) + block.shape[1:])
    return jnp.concatenate(
        [
            lax.dynamic_index_in_dim(blocks, lax.rem(place - e + size, size), 0, False)
            for e in range(size)
        ],
        0,
    )


def rows_place(blocks):
    size = lax.axis_size("tp")
    place = lax.axis_index("tp")
    return jnp.concatenate(
        [lax.select_n(lax.rem(place - p + size, size), *blocks) for p in range(size)], 0
    )


def columns_turn(block):
    size = lax.axis_size("tp")
    place = lax.axis_index("tp")
    blocks = jnp.split(block, size, 1)
    return jnp.concatenate(
        [lax.select_n(lax.rem(place - e + size, size), *blocks) for e in range(size)], 1
    )


def rows_sum(total):
    size = lax.axis_size("tp")
    rows = total.shape[0] // size
    low = total.astype(BF16)
    moved = []
    for e in range(1, size):
        moved.append(shifted(low[e * rows : (e + 1) * rows], "tp", size - e))
    kept = total[:rows]
    for block in moved:
        kept = kept + block.astype(F32)
    return kept


def rows_moved(block):
    moved = []
    for e in range(1, lax.axis_size("tp")):
        moved.append(shifted(block, "tp", e))
    return moved


def rows_gather(block):
    return jnp.concatenate([block] + rows_moved(block), 0)


def rows_exchange(blocks):
    size = lax.axis_size("tp")
    return [blocks[0]] + [shifted(blocks[size - j], "tp", j) for j in range(1, size)]


TILE = 256


def blocks_of(refs):
    return [ref.at[b] for ref in refs for b in range(ref.shape[0])]


def attend_kernel(heads, parts, limits, starts, query, prior, *refs):
    kv, (logits, weights, context, inverse) = blocks_of(refs[:parts]), refs[parts:]
    limit = limits[pl.program_id(0)]
    rows, width = query.shape
    size = width // heads
    block = kv[0].shape[0]
    column = lax.broadcasted_iota(jnp.int32, (rows, block), 1)
    spans = [pl.ds(pl.multiple_of(starts[e], block), block) for e in range(len(kv))]
    for h in range(heads):
        own = slice(h * size, (h + 1) * size)
        masked = []
        for e, span in enumerate(spans):
            raw = lax.dot_general(
                query[:, own], kv[e][:, own], (((1,), (1,)), ((), ())), preferred_element_type=F32
            )
            score = prior[0, h, :, span].astype(F32) + raw
            logits[0, h, :, span] = score.astype(BF16)
            masked.append(jnp.where(column < limit - starts[e], score, MASKED))
        top = jnp.max(masked[0], -1, keepdims=True)
        for part in masked[1:]:
            top = jnp.maximum(top, jnp.max(part, -1, keepdims=True))
        count = jnp.zeros((rows, 1), F32)
        mixed = jnp.zeros((rows, size), F32)
        for e, span in enumerate(spans):
            exponent = jnp.exp(masked[e] - top)
            count = count + jnp.sum(exponent, -1, keepdims=True)
            low = exponent.astype(BF16)
            weights[h, :, span] = low
            mixed = mixed + jnp.dot(
                low, kv[e][:, width + h * size : width + (h + 1) * size], preferred_element_type=F32
            )
        scale = 1.0 / count
        context[:, own] = (mixed * scale).astype(BF16)
        inverse[:, own] = jnp.broadcast_to(scale, (rows, size))


def attend(query, kv, starts, prior, limits, heads):
    rows, width = query.shape
    keys = prior.shape[3]
    tile = lambda i, *scalars: (i, 0)
    whole = lambda i, *scalars: (0, 0, 0)
    cube = lambda i, *scalars: (0, i, 0)
    quad = lambda i, *scalars: (0, 0, i, 0)
    return pl.pallas_call(
        partial(attend_kernel, heads, len(kv)),
        grid_spec=pltpu.PrefetchScalarGridSpec(
            num_scalar_prefetch=2,
            grid=(rows // TILE,),
            in_specs=[pl.BlockSpec((TILE, width), tile), pl.BlockSpec((1, heads, TILE, keys), quad)]
            + [pl.BlockSpec(part.shape, whole) for part in kv],
            out_specs=[
                pl.BlockSpec((1, heads, TILE, keys), quad),
                pl.BlockSpec((heads, TILE, keys), cube),
                pl.BlockSpec((TILE, width), tile),
                pl.BlockSpec((TILE, width), tile),
            ],
        ),
        out_shape=[
            jax.ShapeDtypeStruct((1, heads, rows, keys), BF16),
            jax.ShapeDtypeStruct((heads, rows, keys), BF16),
            jax.ShapeDtypeStruct((rows, width), BF16),
            jax.ShapeDtypeStruct((rows, width), F32),
        ],
        cost_estimate=pl.CostEstimate(
            flops=4 * rows * keys * width, transcendentals=heads * rows * keys, bytes_accessed=6 * heads * rows * keys
        ),
        name="attend",
    )(limits, starts, query, prior, *kv)


def attend_back_kernel(heads, scale, parts, starts, weights, context, d_mixed, inverse, query, *refs):
    kv, (d_scores, d_query, d_kept, d_sent, total) = blocks_of(refs[:parts]), refs[parts:]
    width = context.shape[1]
    size = width // heads
    block = kv[0].shape[0]
    step = pl.program_id(0)
    spans = [pl.ds(pl.multiple_of(starts[e], block), block) for e in range(len(kv))]

    @pl.when(step == 0)
    def _():
        total[...] = jnp.zeros_like(total)

    scaled = d_mixed[...].astype(F32) * inverse[...]
    product = scaled * context[...].astype(F32)
    d_context = scaled.astype(BF16)
    d_context_t = scaled.T.astype(BF16)
    query_t = query[...].astype(F32).T.astype(BF16)
    for h in range(heads):
        own = slice(h * size, (h + 1) * size)
        other = slice(width + h * size, width + (h + 1) * size)
        mean = jnp.sum(product[:, own], -1, keepdims=True)
        changes, lows = [], []
        d_head = jnp.zeros((context.shape[0], size), F32)
        for e, span in enumerate(spans):
            d_weights = lax.dot_general(
                d_context[:, own], kv[e][:, other], (((1,), (1,)), ((), ())), preferred_element_type=F32
            )
            low = weights[h, :, span]
            change = (low.astype(F32) * (d_weights - mean)).astype(BF16)
            d_scores[0, h, :, span] = change
            d_head = d_head + jnp.dot(change, kv[e][:, own], preferred_element_type=F32)
            changes.append(change)
            lows.append(low)
        total[own, :] += jnp.dot(
            query_t[own, :], jnp.concatenate(changes, 1), preferred_element_type=F32
        )
        total[other, :] += jnp.dot(
            d_context_t[own, :], jnp.concatenate(lows, 1), preferred_element_type=F32
        )
        d_query[:, own] = scale * d_head

    @pl.when(step == pl.num_programs(0) - 1)
    def _():
        for e in range(len(kv)):
            half = d_kept.shape[0]
            target, index = (d_kept, e) if e < half else (d_sent, e - half)
            target[index] = total[:, e * block : (e + 1) * block].astype(BF16)


def attend_back(weights, kv, starts, context, d_mixed, inverse, query, scale):
    heads, rows, keys = weights.shape
    width = context.shape[1]
    block = kv[0].shape[1]
    tile = lambda i, *scalars: (i, 0)
    whole = lambda i, *scalars: (0, 0, 0)
    shape = (keys // block // 2, 2 * width, block)
    return pl.pallas_call(
        partial(attend_back_kernel, heads, scale, len(kv)),
        grid_spec=pltpu.PrefetchScalarGridSpec(
            num_scalar_prefetch=1,
            grid=(rows // TILE,),
            in_specs=[pl.BlockSpec((heads, TILE, keys), lambda i, *scalars: (0, i, 0))]
            + [pl.BlockSpec((TILE, width), tile)] * 4
            + [pl.BlockSpec(part.shape, whole) for part in kv],
            out_specs=[
                pl.BlockSpec((1, heads, TILE, keys), lambda i, *scalars: (0, 0, i, 0)),
                pl.BlockSpec((TILE, width), tile),
                pl.BlockSpec(shape, whole),
                pl.BlockSpec(shape, whole),
            ],
            scratch_shapes=[pltpu.VMEM((2 * width, keys), F32)],
        ),
        out_shape=[
            jax.ShapeDtypeStruct((1, heads, rows, keys), BF16),
            jax.ShapeDtypeStruct((rows, width), F32),
            jax.ShapeDtypeStruct(shape, BF16),
            jax.ShapeDtypeStruct(shape, BF16),
        ],
        cost_estimate=pl.CostEstimate(
            flops=10 * rows * keys * width, transcendentals=0, bytes_accessed=6 * heads * rows * keys
        ),
        name="attend_back",
    )(starts, weights, context, d_mixed, inverse, query, *kv)


def pack_kernel(lead, place, squared, *refs):
    vectors, placed, out = refs[:-2], refs[-2], refs[-1]
    out[...] = jnp.zeros_like(out)
    for i, vector in enumerate(vectors):
        out[i : i + 1, :] = vector[...]
    out[len(vectors) : len(vectors) + 1, :] = jnp.broadcast_to(squared[...], (1, out.shape[1]))
    for p in range((out.shape[0] - lead) // placed.shape[0]):

        @pl.when(place[0] == p)
        def _():
            first = lead + p * placed.shape[0]
            out[first : first + placed.shape[0], :] = placed[...]


def pack(vectors, squared, placed, place, places):
    width = vectors[0].shape[0]
    vmem = pl.BlockSpec(memory_space=pltpu.VMEM)
    rows = placed.reshape(-1, width)
    return pl.pallas_call(
        partial(pack_kernel, 8),
        in_specs=[pl.BlockSpec(memory_space=pltpu.SMEM)] + [vmem] * (len(vectors) + 2),
        out_specs=vmem,
        out_shape=jax.ShapeDtypeStruct((8 + places * rows.shape[0], width), F32),
        name="pack",
    )(place.reshape(1), squared.reshape(1, 1), *[v.reshape(1, width) for v in vectors], rows)


def per_device(
    inputs,
    teacher_states,
    lengths,
    prev_logits,
    w_query,
    w_key,
    w_value,
    w_output,
    w_inner,
    w_outer,
    bias_query,
    bias_value,
    bias_output,
    bias_inner,
    bias_outer,
    gain_first,
    shift_first,
    gain_second,
    shift_second,
):
    tokens = inputs[0]
    row_count, model_width = tokens.shape
    heads_local = prev_logits.shape[1]
    width_local = w_query.shape[1]
    score_scale = 1.0 / math.sqrt(width_local // heads_local)
    seq_length = lengths[0]
    ctx_place, tp_place = lax.axis_index("ctx"), lax.axis_index("tp")
    tp_size = lax.axis_size("tp")
    part_rows = row_count // tp_size

    qkv_shard = jnp.concatenate([w_query.T, w_key.T, w_value.T], 0)
    full_qkv = gather_weight(qkv_shard, 1)
    output_half = jnp.concatenate([w_output] + rows_moved(w_output), 0)
    row_pos = ctx_place * row_count + jnp.arange(row_count, dtype=jnp.int32)
    limits = jnp.minimum((row_pos[::TILE] // BLK + 1) * BLK, seq_length)

    def own_rows(array):
        return lax.dynamic_slice_in_dim(array, tp_place * part_rows, part_rows, 0)

    tokens_first = own_first(tokens)
    query_scaled = dot32(tokens_first, full_qkv[:width_local], ((1,), (1,))) + bias_query
    query_scaled = (query_scaled.astype(BF16).astype(F32) * score_scale).astype(BF16)
    bias_kv = jnp.concatenate([jnp.zeros_like(bias_value), bias_value])
    kv_local = (dot32(tokens_first, full_qkv[width_local:], ((1,), (1,))) + bias_kv).astype(BF16)
    kv_local, output_half = tie(kv_local, output_half)
    kv_all, query_scaled = gather_parts(kv_local, query_scaled)
    output_moved, join_output = gather_late(output_half, 1)
    starts = (ctx_place ^ jnp.asarray(ctx_order(), jnp.int32)) * row_count
    all_count = VectorSum(seq_length.astype(F32), ("dp",)).total()

    logits, weights, context, inverse = attend(
        query_scaled, kv_all, starts, prev_logits, limits, heads_local
    )
    context_turned = rows_turn(context)
    context_turned, output_moved, w_inner, w_outer = tie(
        context_turned, output_moved, w_inner, w_outer
    )
    full_output = join_output(output_moved)
    inner_moved, join_inner = gather_late(w_inner, 0)
    outer_moved, join_outer = gather_late(w_outer, 1)
    context_mine = jnp.concatenate(rows_exchange(jnp.split(context_turned, tp_size, 0)), 1)
    attended = own_first(dot32(context_mine, full_output, ((1,), (0,))))
    first_sum = own_rows(tokens).astype(F32) + attended + bias_output
    normed_first, spread_first, hidden = norm_forward(first_sum, gain_first, shift_first)
    hidden_first = own_first(hidden.astype(BF16))
    hidden_moved = rows_moved(hidden_first)
    full_inner, full_outer = join_inner(inner_moved), join_outer(outer_moved)
    hidden_low = jnp.concatenate([hidden_first] + hidden_moved, 0)
    pre_act = dot32(hidden_low, full_inner, ((1,), (0,))) + bias_inner
    act_low = jax.nn.gelu(pre_act, approximate=False).astype(BF16)
    fed = own_first(rows_sum(dot32(act_low, full_outer, ((1,), (0,)))))
    second_sum = hidden + fed + bias_outer
    normed_second, spread_second, result = norm_forward(second_sum, gain_second, shift_second)
    valid_rows = (own_rows(row_pos) < seq_length).astype(F32)
    deviation = result - own_rows(teacher_states[0]).astype(F32)
    local_squared = jnp.sum(valid_rows[:, None] * deviation * deviation)
    token_total = row_count * lax.axis_size("ctx") * lax.axis_size("dp")
    d_out = 2.0 * token_total / all_count * valid_rows[:, None] * deviation
    d_second, grad_gain_second, grad_shift_second = norm_backward(
        d_out, normed_second, spread_second, gain_second
    )
    grad_bias_outer = jnp.sum(d_second, 0)
    d_second_low = rows_gather(own_first(d_second.astype(BF16)))
    d_act = dot32(d_second_low, full_outer, ((1,), (1,)))
    gelu_back = jax.vjp(partial(jax.nn.gelu, approximate=False), pre_act)[1]
    d_pre = gelu_back(d_act)[0]
    grad_bias_inner = jnp.sum(d_pre, 0)
    d_pre_low = d_pre.astype(BF16)
    hidden_part = rows_sum(dot32(d_pre_low, full_inner, ((1,), (1,))))
    outer_sum = WeightSum(dot32(act_low, d_second_low, ((0,), (0,))), 1, True)
    inner_sum = WeightSum(dot32(hidden_low, d_pre_low, ((0,), (0,))), 0)
    d_hidden = d_second + own_first(hidden_part)
    d_first, grad_gain_first, grad_shift_first = norm_backward(
        d_hidden, normed_first, spread_first, gain_first
    )
    grad_bias_output = jnp.sum(d_first, 0)
    d_first_low = own_first(d_first.astype(BF16))
    d_context_mine = dot32(d_first_low, full_output, ((1,), (1,))).astype(BF16)
    d_context = rows_place(rows_exchange(jnp.split(d_context_mine, tp_size, 1)))

    packed = (
        pack(
            [
                grad_bias_output,
                grad_bias_outer,
                grad_gain_first,
                grad_shift_first,
                grad_gain_second,
                grad_shift_second,
            ],
            local_squared,
            grad_bias_inner,
            tp_place,
            tp_size,
        )
    )
    early_sum = VectorSum(packed, ("dp", "ctx"))
    d_context, outer_sum.moved, inner_sum.moved = tie(
        d_context, outer_sum.moved, inner_sum.moved
    )
    outer_sum.step()
    inner_sum.step()
    both_mine = jnp.concatenate([d_first_low, result.astype(BF16)], 1)
    both_mine, _ = tie(both_mine, d_context)
    both_moved = rows_moved(both_mine)
    d_scores, d_query, d_kept, d_sent = attend_back(
        weights, kv_all, starts, context, d_context, inverse, query_scaled, score_scale
    )
    d_sent, early_sum.moved = tie(d_sent, early_sum.moved)
    early_sum.step()
    d_kv = scatter_parts(d_kept, d_sent)
    d_query_low = d_query.astype(BF16)
    d_kv_low, inner_sum.moved, outer_sum.moved, early_sum.moved, *both_moved = tie(
        d_kv.astype(BF16), inner_sum.moved, outer_sum.moved, early_sum.moved, *both_moved
    )
    tokens_part = rows_sum(
        dot32(rows_turn(d_query_low), full_qkv[:width_local], ((1,), (0,)))
        + dot32(columns_turn(d_kv_low), full_qkv[width_local:], ((0,), (0,))),
    )
    inner_sum.step()
    outer_sum.step()
    early_sum.step()
    query_gradient = dot32(d_query_low, tokens_first, ((0,), (0,)))
    kv_gradient = dot32(d_kv_low, tokens_first, ((1,), (0,)))
    qkv_gradient = jnp.concatenate([query_gradient, kv_gradient], 0)
    qkv_sum = WeightSum(qkv_gradient, 1, True)
    both = [both_mine] + both_moved
    output_gradient = sum(
        dot32(rows, moved[:, :model_width], ((0,), (0,)))
        for rows, moved in zip(jnp.split(context_turned, tp_size, 0), both)
    )
    output_sum = WeightSum(output_gradient, 1, True)
    late_vector = jnp.concatenate([jnp.sum(d_query, 0), jnp.sum(d_kv[width_local:], 1)])
    late_sum = VectorSum(late_vector, ("dp", "ctx"), True)
    grad_mine = (d_first + own_first(tokens_part)).astype(BF16)
    sums = (early_sum, late_sum)
    grad_mine, *moved = tie(grad_mine, *[one.moved for one in sums])
    for one, value in zip(sums, moved):
        one.moved = value
    early = early_sum.total()
    moved = []
    for e in range(1, tp_size):
        moved.append(flipped(early, "tp", e))
    early = [early] + moved
    while len(early) > 1:
        early = [left + right for left, right in zip(early[::2], early[1::2])]
    early = early[0]
    qkv_sum.step()
    output_sum.step()
    late_sum.step()
    grad_moved = rows_moved(grad_mine)
    inner_shard, outer_shard = inner_sum.total(), outer_sum.total()
    result_all = rows_place([block[:, model_width:] for block in both]).astype(F32)
    grad_moved[-1], inner_shard, outer_shard, result_all = tie(
        grad_moved[-1], inner_shard, outer_shard, result_all
    )
    grad_inputs = rows_place([grad_mine] + grad_moved).astype(F32)
    output_shard = output_sum.total()
    shard_qkv = qkv_sum.total()
    loss_value = early[6, 0] / (all_count * model_width)
    inner_rows = grad_bias_inner.shape[0] // model_width
    sum_bias_inner = lax.dynamic_slice_in_dim(early, 8 + tp_place * inner_rows, inner_rows, 0).reshape(-1)
    late = late_sum.total()
    return (
        result_all[None],
        logits,
        loss_value,
        grad_inputs[None],
        d_scores,
        shard_qkv[:width_local].T,
        shard_qkv[width_local : 2 * width_local].T,
        shard_qkv[2 * width_local :].T,
        output_shard,
        inner_shard,
        outer_shard,
        late[:width_local],
        late[width_local:],
        early[0],
        sum_bias_inner,
        early[1],
        early[2],
        early[3],
        early[4],
        early[5],
    )


def solution(mesh):
    placed = (
        P("dp", "ctx", None),
        P("dp", "ctx", None),
        P("dp"),
        P("dp", "tp", "ctx", None),
        P("dp", "tp"),
        P("dp", "tp"),
        P("dp", "tp"),
        P("tp", "dp"),
        P("dp", "tp"),
        P("tp", "dp"),
        P("tp"),
        P("tp"),
        P(),
        P("tp"),
        P(),
        P(),
        P(),
        P(),
        P(),
    )
    return jax.shard_map(
        per_device,
        mesh=mesh,
        in_specs=placed,
        out_specs=(
            P("dp", "ctx", None),
            P("dp", "tp", "ctx", None),
            P(),
            P("dp", "ctx", None),
            P("dp", "tp", "ctx", None),
            P("dp", "tp"),
            P("dp", "tp"),
            P("dp", "tp"),
            P("tp", "dp"),
            P("dp", "tp"),
            P("tp", "dp"),
            P("tp"),
            P("tp"),
            P(),
            P("tp"),
            P(),
            P(),
            P(),
            P(),
            P(),
        ),
        check_vma=False,
    )
```

```python
from functools import partial
import math

import jax
import jax.numpy as jnp
from jax import lax
from jax.experimental import pallas as pl
from jax.experimental.pallas import tpu as pltpu
from jax.sharding import PartitionSpec as P

BLK = 256


EPS = 1e-06
MASKED = -1e30


def norm_forward(total, gain_vec, shift_vec):
    center = total - jnp.mean(total, -1, keepdims=True)
    spread = lax.rsqrt(jnp.mean(center * center, -1, keepdims=True) + EPS)
    normed = center * spread
    return (normed, spread, normed * gain_vec + shift_vec)


def norm_backward(gradient, normed, spread, gain_vec):
    scaled = gradient * gain_vec
    inner_term = (
        scaled
        - jnp.mean(scaled, -1, keepdims=True)
        - normed * jnp.mean(scaled * normed, -1, keepdims=True)
    )
    return (inner_term * spread, jnp.sum(gradient * normed, 0), jnp.sum(gradient, 0))


F32, BF16 = jnp.float32, jnp.bfloat16


def dot32(left, right, dims):
    return lax.dot_general(left, right, (dims, ((), ())), preferred_element_type=F32)


def shifted(block, axis, step):
    size = lax.axis_size(axis)
    return lax.ppermute(block, axis, [(i, (i + step) % size) for i in range(size)])


def flipped(block, axis, bit):
    size = lax.axis_size(axis)
    return lax.ppermute(block, axis, [(i, i ^ bit) for i in range(size)])


def tie(*values):
    return lax.optimization_barrier(values)


def own_first(array):
    if lax.axis_size("dp") != 2:
        return array
    half = array.shape[-1] // 2
    turned = jnp.concatenate([array[..., half:], array[..., :half]], -1)
    return jnp.where(lax.axis_index("dp") == 0, array, turned)


def gather_weight(shard, dim):
    if lax.axis_size("dp") != 2:
        return lax.all_gather(shard, "dp", axis=dim, tiled=True)
    return jnp.concatenate([shard, flipped(shard, "dp", 1)], dim)


def gather_late(shard, dim):
    if lax.axis_size("dp") != 2:
        return gather_weight(shard, dim), lambda moved: moved
    moved = flipped(shard, "dp", 1)
    return moved, lambda moved: jnp.concatenate([shard, moved], dim)


class WeightSum:
    def __init__(self, gradient, dim, far_first=False):
        self.bits = []
        bit = 1
        while bit < lax.axis_size("ctx"):
            self.bits.append(bit)
            bit *= 2
        if far_first:
            self.bits.reverse()
        if lax.axis_size("dp") == 2:
            kept, given = jnp.split(gradient, 2, dim)
            self.kept, self.moved = kept, flipped(given.astype(BF16), "dp", 1)
        else:
            low = gradient.astype(BF16)
            self.moved = lax.psum_scatter(low, "dp", scatter_dimension=dim, tiled=True)
            self.kept = jnp.zeros(self.moved.shape, F32)

    def step(self):
        low = (self.kept.astype(F32) + self.moved.astype(F32)).astype(BF16)
        self.kept, self.moved = low, flipped(low, "ctx", self.bits.pop(0))

    def total(self):
        while self.bits:
            self.step()
        return self.kept.astype(F32) + self.moved.astype(F32)


class VectorSum:
    def __init__(self, vector, axes, far_first=False):
        self.bits = []
        for axis in axes:
            bit = 1
            while bit < lax.axis_size(axis):
                self.bits.append((axis, bit))
                bit *= 2
        if far_first:
            self.bits.reverse()
        self.kept, self.moved = vector, flipped(vector, *self.bits.pop(0))

    def step(self):
        summed = self.kept + self.moved
        self.kept, self.moved = summed, flipped(summed, *self.bits.pop(0))

    def total(self):
        while self.bits:
            self.step()
        return self.kept + self.moved


def ctx_order():
    order, bit = [0], lax.axis_size("ctx") // 2
    while bit:
        order = order + [e ^ bit for e in order]
        bit //= 2
    return order


def gather_parts(block, beside):
    held, bit = [block[None]], lax.axis_size("ctx") // 2
    while bit:
        sent = held[0] if len(held) == 1 else jnp.concatenate(held, 0)
        held.append(flipped(sent, "ctx", bit))
        if bit == lax.axis_size("ctx") // 2:
            held[-1], beside = tie(held[-1], beside)
        bit //= 2
    return held, beside


def scatter_parts(blocks, sent):
    size, bit = lax.axis_size("ctx"), 1
    while bit < size:
        blocks = blocks.astype(F32) + flipped(sent.astype(BF16), "ctx", bit).astype(F32)
        half = blocks.shape[0] // 2
        if half:
            blocks, sent = blocks[:half], blocks[half:]
        bit *= 2
    return blocks[0]


def rows_turn(block):
    size = lax.axis_size("tp")
    place = lax.axis_index("tp")
    blocks = block.reshape((size, block.shape[0] // size) + block.shape[1:])
    return jnp.concatenate(
        [
            lax.dynamic_index_in_dim(blocks, lax.rem(place - e + size, size), 0, False)
            for e in range(size)
        ],
        0,
    )


def rows_place(blocks):
    size = lax.axis_size("tp")
    place = lax.axis_index("tp")
    return jnp.concatenate(
        [lax.select_n(lax.rem(place - p + size, size), *blocks) for p in range(size)], 0
    )


def rows_sum(total):
    size = lax.axis_size("tp")
    rows = total.shape[0] // size
    low = total.astype(BF16)
    moved = []
    for e in range(1, size):
        moved.append(shifted(low[e * rows : (e + 1) * rows], "tp", size - e))
    kept = total[:rows]
    for block in moved:
        kept = kept + block.astype(F32)
    return kept


def rows_moved(block):
    moved = []
    for e in range(1, lax.axis_size("tp")):
        moved.append(shifted(block, "tp", e))
    return moved


def rows_gather(block):
    return jnp.concatenate([block] + rows_moved(block), 0)


def rows_exchange(blocks):
    size = lax.axis_size("tp")
    return [blocks[0]] + [shifted(blocks[size - j], "tp", j) for j in range(1, size)]


TILE = 256


def blocks_of(refs):
    return [ref.at[b] for ref in refs for b in range(ref.shape[0])]


def attend_kernel(heads, parts, limits, starts, query, prior, *refs):
    kv, (logits, weights, context, inverse) = blocks_of(refs[:parts]), refs[parts:]
    limit = limits[pl.program_id(0)]
    rows, width = query.shape
    size = width // heads
    block = kv[0].shape[0]
    column = lax.broadcasted_iota(jnp.int32, (rows, block), 1)
    spans = [pl.ds(pl.multiple_of(starts[e], block), block) for e in range(len(kv))]
    for h in range(heads):
        own = slice(h * size, (h + 1) * size)
        masked = []
        for e, span in enumerate(spans):
            raw = lax.dot_general(
                query[:, own], kv[e][:, own], (((1,), (1,)), ((), ())), preferred_element_type=F32
            )
            score = prior[0, h, :, span].astype(F32) + raw
            logits[0, h, :, span] = score.astype(BF16)
            masked.append(jnp.where(column < limit - starts[e], score, MASKED))
        top = jnp.max(masked[0], -1, keepdims=True)
        for part in masked[1:]:
            top = jnp.maximum(top, jnp.max(part, -1, keepdims=True))
        count = jnp.zeros((rows, 1), F32)
        mixed = jnp.zeros((rows, size), F32)
        for e, span in enumerate(spans):
            exponent = jnp.exp(masked[e] - top)
            count = count + jnp.sum(exponent, -1, keepdims=True)
            low = exponent.astype(BF16)
            weights[h, :, span] = low
            mixed = mixed + jnp.dot(
                low, kv[e][:, width + h * size : width + (h + 1) * size], preferred_element_type=F32
            )
        scale = 1.0 / count
        context[:, own] = (mixed * scale).astype(BF16)
        inverse[:, own] = jnp.broadcast_to(scale, (rows, size))


def attend(query, kv, starts, prior, limits, heads):
    rows, width = query.shape
    keys = prior.shape[3]
    tile = lambda i, *scalars: (i, 0)
    whole = lambda i, *scalars: (0, 0, 0)
    cube = lambda i, *scalars: (0, i, 0)
    quad = lambda i, *scalars: (0, 0, i, 0)
    return pl.pallas_call(
        partial(attend_kernel, heads, len(kv)),
        grid_spec=pltpu.PrefetchScalarGridSpec(
            num_scalar_prefetch=2,
            grid=(rows // TILE,),
            in_specs=[pl.BlockSpec((TILE, width), tile), pl.BlockSpec((1, heads, TILE, keys), quad)]
            + [pl.BlockSpec(part.shape, whole) for part in kv],
            out_specs=[
                pl.BlockSpec((1, heads, TILE, keys), quad),
                pl.BlockSpec((heads, TILE, keys), cube),
                pl.BlockSpec((TILE, width), tile),
                pl.BlockSpec((TILE, width), tile),
            ],
        ),
        out_shape=[
            jax.ShapeDtypeStruct((1, heads, rows, keys), BF16),
            jax.ShapeDtypeStruct((heads, rows, keys), BF16),
            jax.ShapeDtypeStruct((rows, width), BF16),
            jax.ShapeDtypeStruct((rows, width), F32),
        ],
        cost_estimate=pl.CostEstimate(
            flops=4 * rows * keys * width, transcendentals=heads * rows * keys, bytes_accessed=6 * heads * rows * keys
        ),
        name="attend",
    )(limits, starts, query, prior, *kv)


def attend_back_kernel(heads, scale, parts, starts, weights, context, d_mixed, inverse, query, *refs):
    kv, (d_scores, d_query, d_kept, d_sent, total) = blocks_of(refs[:parts]), refs[parts:]
    width = context.shape[1]
    size = width // heads
    block = kv[0].shape[0]
    step = pl.program_id(0)
    spans = [pl.ds(pl.multiple_of(starts[e], block), block) for e in range(len(kv))]

    @pl.when(step == 0)
    def _():
        total[...] = jnp.zeros_like(total)

    scaled = d_mixed[...].astype(F32) * inverse[...]
    product = scaled * context[...].astype(F32)
    d_context = scaled.astype(BF16)
    d_context_t = scaled.T.astype(BF16)
    query_t = query[...].astype(F32).T.astype(BF16)
    for h in range(heads):
        own = slice(h * size, (h + 1) * size)
        other = slice(width + h * size, width + (h + 1) * size)
        mean = jnp.sum(product[:, own], -1, keepdims=True)
        changes, lows = [], []
        d_head = jnp.zeros((context.shape[0], size), F32)
        for e, span in enumerate(spans):
            d_weights = lax.dot_general(
                d_context[:, own], kv[e][:, other], (((1,), (1,)), ((), ())), preferred_element_type=F32
            )
            low = weights[h, :, span]
            change = (low.astype(F32) * (d_weights - mean)).astype(BF16)
            d_scores[0, h, :, span] = change
            d_head = d_head + jnp.dot(change, kv[e][:, own], preferred_element_type=F32)
            changes.append(change)
            lows.append(low)
        total[own, :] += jnp.dot(
            query_t[own, :], jnp.concatenate(changes, 1), preferred_element_type=F32
        )
        total[other, :] += jnp.dot(
            d_context_t[own, :], jnp.concatenate(lows, 1), preferred_element_type=F32
        )
        d_query[:, own] = scale * d_head

    @pl.when(step == pl.num_programs(0) - 1)
    def _():
        for e in range(len(kv)):
            half = d_kept.shape[0]
            target, index = (d_kept, e) if e < half else (d_sent, e - half)
            target[index] = total[:, e * block : (e + 1) * block].astype(BF16)


def attend_back(weights, kv, starts, context, d_mixed, inverse, query, scale):
    heads, rows, keys = weights.shape
    width = context.shape[1]
    block = kv[0].shape[1]
    tile = lambda i, *scalars: (i, 0)
    whole = lambda i, *scalars: (0, 0, 0)
    shape = (keys // block // 2, 2 * width, block)
    return pl.pallas_call(
        partial(attend_back_kernel, heads, scale, len(kv)),
        grid_spec=pltpu.PrefetchScalarGridSpec(
            num_scalar_prefetch=1,
            grid=(rows // TILE,),
            in_specs=[pl.BlockSpec((heads, TILE, keys), lambda i, *scalars: (0, i, 0))]
            + [pl.BlockSpec((TILE, width), tile)] * 4
            + [pl.BlockSpec(part.shape, whole) for part in kv],
            out_specs=[
                pl.BlockSpec((1, heads, TILE, keys), lambda i, *scalars: (0, 0, i, 0)),
                pl.BlockSpec((TILE, width), tile),
                pl.BlockSpec(shape, whole),
                pl.BlockSpec(shape, whole),
            ],
            scratch_shapes=[pltpu.VMEM((2 * width, keys), F32)],
        ),
        out_shape=[
            jax.ShapeDtypeStruct((1, heads, rows, keys), BF16),
            jax.ShapeDtypeStruct((rows, width), F32),
            jax.ShapeDtypeStruct(shape, BF16),
            jax.ShapeDtypeStruct(shape, BF16),
        ],
        cost_estimate=pl.CostEstimate(
            flops=10 * rows * keys * width, transcendentals=0, bytes_accessed=6 * heads * rows * keys
        ),
        name="attend_back",
    )(starts, weights, context, d_mixed, inverse, query, *kv)


def pack_kernel(lead, place, squared, *refs):
    vectors, placed, out = refs[:-2], refs[-2], refs[-1]
    out[...] = jnp.zeros_like(out)
    for i, vector in enumerate(vectors):
        out[i : i + 1, :] = vector[...]
    out[len(vectors) : len(vectors) + 1, :] = jnp.broadcast_to(squared[...], (1, out.shape[1]))
    for p in range((out.shape[0] - lead) // placed.shape[0]):

        @pl.when(place[0] == p)
        def _():
            first = lead + p * placed.shape[0]
            out[first : first + placed.shape[0], :] = placed[...]


def pack(vectors, squared, placed, place, places):
    width = vectors[0].shape[0]
    vmem = pl.BlockSpec(memory_space=pltpu.VMEM)
    rows = placed.reshape(-1, width)
    return pl.pallas_call(
        partial(pack_kernel, 8),
        in_specs=[pl.BlockSpec(memory_space=pltpu.SMEM)] + [vmem] * (len(vectors) + 2),
        out_specs=vmem,
        out_shape=jax.ShapeDtypeStruct((8 + places * rows.shape[0], width), F32),
        name="pack",
    )(place.reshape(1), squared.reshape(1, 1), *[v.reshape(1, width) for v in vectors], rows)


def per_device(
    inputs,
    teacher_states,
    lengths,
    prev_logits,
    w_query,
    w_key,
    w_value,
    w_output,
    w_inner,
    w_outer,
    bias_query,
    bias_value,
    bias_output,
    bias_inner,
    bias_outer,
    gain_first,
    shift_first,
    gain_second,
    shift_second,
):
    tokens = inputs[0]
    row_count, model_width = tokens.shape
    heads_local = prev_logits.shape[1]
    width_local = w_query.shape[1]
    score_scale = 1.0 / math.sqrt(width_local // heads_local)
    seq_length = lengths[0]
    ctx_place, tp_place = lax.axis_index("ctx"), lax.axis_index("tp")
    tp_size = lax.axis_size("tp")
    part_rows = row_count // tp_size

    qkv_shard = jnp.concatenate([w_query.T, w_key.T, w_value.T], 0)
    full_qkv = gather_weight(qkv_shard, 1)
    output_half = jnp.concatenate([w_output] + rows_moved(w_output), 0)
    row_pos = ctx_place * row_count + jnp.arange(row_count, dtype=jnp.int32)
    limits = jnp.minimum((row_pos[::TILE] // BLK + 1) * BLK, seq_length)

    def own_rows(array):
        return lax.dynamic_slice_in_dim(array, tp_place * part_rows, part_rows, 0)

    tokens_first = own_first(tokens)
    query_scaled = dot32(tokens_first, full_qkv[:width_local], ((1,), (1,))) + bias_query
    query_scaled = (query_scaled.astype(BF16).astype(F32) * score_scale).astype(BF16)
    bias_kv = jnp.concatenate([jnp.zeros_like(bias_value), bias_value])
    kv_local = (dot32(tokens_first, full_qkv[width_local:], ((1,), (1,))) + bias_kv).astype(BF16)
    kv_local, output_half = tie(kv_local, output_half)
    kv_all, query_scaled = gather_parts(kv_local, query_scaled)
    output_moved, join_output = gather_late(output_half, 1)
    starts = (ctx_place ^ jnp.asarray(ctx_order(), jnp.int32)) * row_count
    all_count = VectorSum(seq_length.astype(F32), ("dp",)).total()

    logits, weights, context, inverse = attend(
        query_scaled, kv_all, starts, prev_logits, limits, heads_local
    )
    context_turned = rows_turn(context)
    context_turned, output_moved, w_inner, w_outer = tie(
        context_turned, output_moved, w_inner, w_outer
    )
    full_output = join_output(output_moved)
    inner_moved, join_inner = gather_late(w_inner, 0)
    outer_moved, join_outer = gather_late(w_outer, 1)
    context_mine = jnp.concatenate(rows_exchange(jnp.split(context_turned, tp_size, 0)), 1)
    attended = own_first(dot32(context_mine, full_output, ((1,), (0,))))
    first_sum = own_rows(tokens).astype(F32) + attended + bias_output
    normed_first, spread_first, hidden = norm_forward(first_sum, gain_first, shift_first)
    hidden_first = own_first(hidden.astype(BF16))
    hidden_moved = rows_moved(hidden_first)
    full_inner, full_outer = join_inner(inner_moved), join_outer(outer_moved)
    hidden_low = jnp.concatenate([hidden_first] + hidden_moved, 0)
    pre_act = dot32(hidden_low, full_inner, ((1,), (0,))) + bias_inner
    act_low = jax.nn.gelu(pre_act, approximate=False).astype(BF16)
    fed = own_first(rows_sum(dot32(act_low, full_outer, ((1,), (0,)))))
    second_sum = hidden + fed + bias_outer
    normed_second, spread_second, result = norm_forward(second_sum, gain_second, shift_second)
    valid_rows = (own_rows(row_pos) < seq_length).astype(F32)
    deviation = result - own_rows(teacher_states[0]).astype(F32)
    local_squared = jnp.sum(valid_rows[:, None] * deviation * deviation)
    token_total = row_count * lax.axis_size("ctx") * lax.axis_size("dp")
    d_out = 2.0 * token_total / all_count * valid_rows[:, None] * deviation
    d_second, grad_gain_second, grad_shift_second = norm_backward(
        d_out, normed_second, spread_second, gain_second
    )
    grad_bias_outer = jnp.sum(d_second, 0)
    d_second_low = rows_gather(own_first(d_second.astype(BF16)))
    d_act = dot32(d_second_low, full_outer, ((1,), (1,)))
    gelu_back = jax.vjp(partial(jax.nn.gelu, approximate=False), pre_act)[1]
    d_pre = gelu_back(d_act)[0]
    grad_bias_inner = jnp.sum(d_pre, 0)
    d_pre_low = d_pre.astype(BF16)
    hidden_part = rows_sum(dot32(d_pre_low, full_inner, ((1,), (1,))))
    outer_sum = WeightSum(dot32(act_low, d_second_low, ((0,), (0,))), 1, True)
    inner_sum = WeightSum(dot32(hidden_low, d_pre_low, ((0,), (0,))), 0)
    d_hidden = d_second + own_first(hidden_part)
    d_first, grad_gain_first, grad_shift_first = norm_backward(
        d_hidden, normed_first, spread_first, gain_first
    )
    grad_bias_output = jnp.sum(d_first, 0)
    d_first_low = own_first(d_first.astype(BF16))
    d_context_mine = dot32(d_first_low, full_output, ((1,), (1,))).astype(BF16)
    d_context = jnp.concatenate(rows_exchange(jnp.split(d_context_mine, tp_size, 1)), 0)
    d_context = rows_turn(d_context)

    packed = (
        pack(
            [
                grad_bias_output,
                grad_bias_outer,
                grad_gain_first,
                grad_shift_first,
                grad_gain_second,
                grad_shift_second,
            ],
            local_squared,
            grad_bias_inner,
            tp_place,
            tp_size,
        )
    )
    early_sum = VectorSum(packed, ("dp", "ctx"))
    d_context, outer_sum.moved, inner_sum.moved = tie(
        d_context, outer_sum.moved, inner_sum.moved
    )
    outer_sum.step()
    inner_sum.step()
    both_mine = jnp.concatenate([d_first_low, result.astype(BF16)], 1)
    both_mine, _ = tie(both_mine, d_context)
    both_moved = rows_moved(both_mine)
    d_scores, d_query, d_kept, d_sent = attend_back(
        weights, kv_all, starts, context, d_context, inverse, query_scaled, score_scale
    )
    d_sent, early_sum.moved = tie(d_sent, early_sum.moved)
    early_sum.step()
    d_kv = scatter_parts(d_kept, d_sent)
    d_query_low = d_query.astype(BF16)
    d_kv_low, inner_sum.moved, outer_sum.moved, early_sum.moved, *both_moved = tie(
        d_kv.astype(BF16), inner_sum.moved, outer_sum.moved, early_sum.moved, *both_moved
    )
    d_qkv_low = jnp.concatenate([d_query_low, d_kv_low.T], 1)
    tokens_part = rows_sum(dot32(rows_turn(d_qkv_low), full_qkv, ((1,), (0,))))
    inner_sum.step()
    outer_sum.step()
    early_sum.step()
    qkv_gradient = dot32(d_qkv_low, tokens_first, ((0,), (0,)))
    qkv_sum = WeightSum(qkv_gradient, 1, True)
    both = [both_mine] + both_moved
    d_first_all = jnp.concatenate([block[:, :model_width] for block in both], 0)
    output_gradient = dot32(context_turned, d_first_all, ((0,), (0,)))
    output_sum = WeightSum(output_gradient, 1, True)
    late_vector = jnp.concatenate([jnp.sum(d_query, 0), jnp.sum(d_kv[width_local:], 1)])
    late_sum = VectorSum(late_vector, ("dp", "ctx"), True)
    grad_mine = (d_first + own_first(tokens_part)).astype(BF16)
    sums = (early_sum,)
    grad_mine, *moved = tie(grad_mine, *[one.moved for one in sums])
    for one, value in zip(sums, moved):
        one.moved = value
    early = early_sum.total()
    moved = []
    for e in range(1, tp_size):
        moved.append(flipped(early, "tp", e))
    early = [early] + moved
    while len(early) > 1:
        early = [left + right for left, right in zip(early[::2], early[1::2])]
    early = early[0]
    qkv_sum.step()
    output_sum.step()
    late_sum.step()
    output_sum.step()
    qkv_sum.step()
    grad_moved = rows_moved(grad_mine)
    inner_shard, outer_shard = inner_sum.total(), outer_sum.total()
    result_all = rows_place([block[:, model_width:] for block in both]).astype(F32)
    grad_moved[-1], inner_shard, outer_shard, result_all = tie(
        grad_moved[-1], inner_shard, outer_shard, result_all
    )
    grad_inputs = rows_place([grad_mine] + grad_moved).astype(F32)
    output_shard = output_sum.total()
    shard_qkv = qkv_sum.total()
    loss_value = early[6, 0] / (all_count * model_width)
    inner_rows = grad_bias_inner.shape[0] // model_width
    sum_bias_inner = lax.dynamic_slice_in_dim(early, 8 + tp_place * inner_rows, inner_rows, 0).reshape(-1)
    late = late_sum.total()
    return (
        result_all[None],
        logits,
        loss_value,
        grad_inputs[None],
        d_scores,
        shard_qkv[:width_local].T,
        shard_qkv[width_local : 2 * width_local].T,
        shard_qkv[2 * width_local :].T,
        output_shard,
        inner_shard,
        outer_shard,
        late[:width_local],
        late[width_local:],
        early[0],
        sum_bias_inner,
        early[1],
        early[2],
        early[3],
        early[4],
        early[5],
    )


def solution(mesh):
    placed = (
        P("dp", "ctx", None),
        P("dp", "ctx", None),
        P("dp"),
        P("dp", "tp", "ctx", None),
        P("dp", "tp"),
        P("dp", "tp"),
        P("dp", "tp"),
        P("tp", "dp"),
        P("dp", "tp"),
        P("tp", "dp"),
        P("tp"),
        P("tp"),
        P(),
        P("tp"),
        P(),
        P(),
        P(),
        P(),
        P(),
    )
    return jax.shard_map(
        per_device,
        mesh=mesh,
        in_specs=placed,
        out_specs=(
            P("dp", "ctx", None),
            P("dp", "tp", "ctx", None),
            P(),
            P("dp", "ctx", None),
            P("dp", "tp", "ctx", None),
            P("dp", "tp"),
            P("dp", "tp"),
            P("dp", "tp"),
            P("tp", "dp"),
            P("dp", "tp"),
            P("tp", "dp"),
            P("tp"),
            P("tp"),
            P(),
            P("tp"),
            P(),
            P(),
            P(),
            P(),
            P(),
        ),
        check_vma=False,
    )
```

```python
from functools import partial
import math

import jax
import jax.numpy as jnp
from jax import lax
from jax.experimental import pallas as pl
from jax.experimental.pallas import tpu as pltpu
from jax.sharding import PartitionSpec as P

BLK = 256


EPS = 1e-06
MASKED = -1e30


def norm_forward(total, gain_vec, shift_vec):
    center = total - jnp.mean(total, -1, keepdims=True)
    spread = lax.rsqrt(jnp.mean(center * center, -1, keepdims=True) + EPS)
    normed = center * spread
    return (normed, spread, normed * gain_vec + shift_vec)


def norm_backward(gradient, normed, spread, gain_vec):
    scaled = gradient * gain_vec
    inner_term = (
        scaled
        - jnp.mean(scaled, -1, keepdims=True)
        - normed * jnp.mean(scaled * normed, -1, keepdims=True)
    )
    return (inner_term * spread, jnp.sum(gradient * normed, 0), jnp.sum(gradient, 0))


F32, BF16 = jnp.float32, jnp.bfloat16
DP_, CTX_, TP_ = "dp", "ctx", "tp"


def dot32(left, right, dims):
    return lax.dot_general(left, right, (dims, ((), ())), preferred_element_type=F32)


def shifted(block, axis, step):
    size = lax.axis_size(axis)
    return lax.ppermute(block, axis, [(i, (i + step) % size) for i in range(size)])


def flipped(block, axis, bit):
    size = lax.axis_size(axis)
    return lax.ppermute(block, axis, [(i, i ^ bit) for i in range(size)])


def tie(*values):
    return lax.optimization_barrier(values)


def own_first(array):
    if lax.axis_size(DP_) != 2:
        return array
    half = array.shape[-1] // 2
    turned = jnp.concatenate([array[..., half:], array[..., :half]], -1)
    return jnp.where(lax.axis_index(DP_) == 0, array, turned)


def gather_weight(shard, dim):
    if lax.axis_size(DP_) != 2:
        return lax.all_gather(shard, DP_, axis=dim, tiled=True)
    return jnp.concatenate([shard, flipped(shard, DP_, 1)], dim)


def gather_late(shard, dim):
    if lax.axis_size(DP_) != 2:
        return gather_weight(shard, dim), lambda moved: moved
    moved = flipped(shard, DP_, 1)
    return moved, lambda moved: jnp.concatenate([shard, moved], dim)


class WeightSum:
    def __init__(self, gradient, dim, far_first=False):
        self.bits = []
        bit = 1
        while bit < lax.axis_size(CTX_):
            self.bits.append(bit)
            bit *= 2
        if far_first:
            self.bits.reverse()
        if lax.axis_size(DP_) == 2:
            kept, given = jnp.split(gradient, 2, dim)
            self.kept, self.moved = kept, flipped(given.astype(BF16), DP_, 1)
        else:
            low = gradient.astype(BF16)
            self.moved = lax.psum_scatter(low, DP_, scatter_dimension=dim, tiled=True)
            self.kept = jnp.zeros(self.moved.shape, F32)

    def step(self):
        low = (self.kept.astype(F32) + self.moved.astype(F32)).astype(BF16)
        self.kept, self.moved = low, flipped(low, CTX_, self.bits.pop(0))

    def total(self):
        while self.bits:
            self.step()
        return self.kept.astype(F32) + self.moved.astype(F32)


class VectorSum:
    def __init__(self, vector, axes, far_first=False):
        self.bits = []
        for axis in axes:
            bit = 1
            while bit < lax.axis_size(axis):
                self.bits.append((axis, bit))
                bit *= 2
        if far_first:
            self.bits.reverse()
        self.kept, self.moved = vector, flipped(vector, *self.bits.pop(0))

    def step(self):
        summed = self.kept + self.moved
        self.kept, self.moved = summed, flipped(summed, *self.bits.pop(0))

    def total(self):
        while self.bits:
            self.step()
        return self.kept + self.moved


def ctx_order():
    order, bit = [0], lax.axis_size(CTX_) // 2
    while bit:
        order = order + [e ^ bit for e in order]
        bit //= 2
    return order


def gather_parts(block, beside):
    held, bit = [block[None]], lax.axis_size(CTX_) // 2
    while bit:
        sent = held[0] if len(held) == 1 else jnp.concatenate(held, 0)
        held.append(flipped(sent, CTX_, bit))
        if bit == lax.axis_size(CTX_) // 2:
            held[-1], beside = tie(held[-1], beside)
        bit //= 2
    return held, beside


def scatter_parts(blocks, sent):
    size, bit = lax.axis_size(CTX_), 1
    while bit < size:
        blocks = blocks.astype(F32) + flipped(sent.astype(BF16), CTX_, bit).astype(F32)
        half = blocks.shape[0] // 2
        if half:
            blocks, sent = blocks[:half], blocks[half:]
        bit *= 2
    return blocks[0]


def rows_turn(block):
    size = lax.axis_size(TP_)
    place = lax.axis_index(TP_)
    blocks = block.reshape((size, block.shape[0] // size) + block.shape[1:])
    return jnp.concatenate(
        [
            lax.dynamic_index_in_dim(blocks, lax.rem(place - e + size, size), 0, False)
            for e in range(size)
        ],
        0,
    )


def rows_place(blocks):
    size = lax.axis_size(TP_)
    place = lax.axis_index(TP_)
    return jnp.concatenate(
        [lax.select_n(lax.rem(place - p + size, size), *blocks) for p in range(size)], 0
    )


def rows_sum(total):
    size = lax.axis_size(TP_)
    rows = total.shape[0] // size
    low = total.astype(BF16)
    moved = []
    for e in range(1, size):
        moved.append(shifted(low[e * rows : (e + 1) * rows], TP_, size - e))
    kept = total[:rows]
    for block in moved:
        kept = kept + block.astype(F32)
    return kept


def rows_moved(block):
    moved = []
    for e in range(1, lax.axis_size(TP_)):
        moved.append(shifted(block, TP_, e))
    return moved


def rows_gather(block):
    return jnp.concatenate([block] + rows_moved(block), 0)


def rows_exchange(blocks):
    size = lax.axis_size(TP_)
    return [blocks[0]] + [shifted(blocks[size - j], TP_, j) for j in range(1, size)]


TILE = 256


def blocks_of(refs):
    return [ref.at[b] for ref in refs for b in range(ref.shape[0])]


def attend_kernel(heads, parts, limits, starts, query, prior, *refs):
    kv, (logits, weights, context, inverse) = blocks_of(refs[:parts]), refs[parts:]
    limit = limits[pl.program_id(0)]
    rows, width = query.shape
    size = width // heads
    block = kv[0].shape[0]
    column = lax.broadcasted_iota(jnp.int32, (rows, block), 1)
    spans = [pl.ds(pl.multiple_of(starts[e], block), block) for e in range(len(kv))]
    for h in range(heads):
        own = slice(h * size, (h + 1) * size)
        masked = []
        for e, span in enumerate(spans):
            raw = lax.dot_general(
                query[:, own], kv[e][:, own], (((1,), (1,)), ((), ())), preferred_element_type=F32
            )
            score = prior[0, h, :, span].astype(F32) + raw
            logits[0, h, :, span] = score.astype(BF16)
            masked.append(jnp.where(column < limit - starts[e], score, MASKED))
        top = jnp.max(masked[0], -1, keepdims=True)
        for part in masked[1:]:
            top = jnp.maximum(top, jnp.max(part, -1, keepdims=True))
        count = jnp.zeros((rows, 1), F32)
        mixed = jnp.zeros((rows, size), F32)
        for e, span in enumerate(spans):
            exponent = jnp.exp(masked[e] - top)
            count = count + jnp.sum(exponent, -1, keepdims=True)
            low = exponent.astype(BF16)
            weights[h, :, span] = low
            mixed = mixed + jnp.dot(
                low, kv[e][:, width + h * size : width + (h + 1) * size], preferred_element_type=F32
            )
        scale = 1.0 / count
        context[:, own] = (mixed * scale).astype(BF16)
        inverse[:, own] = jnp.broadcast_to(scale, (rows, size))


def attend(query, kv, starts, prior, limits, heads):
    rows, width = query.shape
    keys = prior.shape[3]
    tile = lambda i, *scalars: (i, 0)
    whole = lambda i, *scalars: (0, 0, 0)
    cube = lambda i, *scalars: (0, i, 0)
    quad = lambda i, *scalars: (0, 0, i, 0)
    return pl.pallas_call(
        partial(attend_kernel, heads, len(kv)),
        grid_spec=pltpu.PrefetchScalarGridSpec(
            num_scalar_prefetch=2,
            grid=(rows // TILE,),
            in_specs=[pl.BlockSpec((TILE, width), tile), pl.BlockSpec((1, heads, TILE, keys), quad)]
            + [pl.BlockSpec(part.shape, whole) for part in kv],
            out_specs=[
                pl.BlockSpec((1, heads, TILE, keys), quad),
                pl.BlockSpec((heads, TILE, keys), cube),
                pl.BlockSpec((TILE, width), tile),
                pl.BlockSpec((TILE, width), tile),
            ],
        ),
        out_shape=[
            jax.ShapeDtypeStruct((1, heads, rows, keys), BF16),
            jax.ShapeDtypeStruct((heads, rows, keys), BF16),
            jax.ShapeDtypeStruct((rows, width), BF16),
            jax.ShapeDtypeStruct((rows, width), F32),
        ],
        cost_estimate=pl.CostEstimate(
            flops=4 * rows * keys * width, transcendentals=heads * rows * keys, bytes_accessed=6 * heads * rows * keys
        ),
        name="attend",
    )(limits, starts, query, prior, *kv)


def attend_back_kernel(heads, scale, parts, starts, weights, context, d_mixed, inverse, query, *refs):
    kv, (d_scores, d_query, d_kept, d_sent, total) = blocks_of(refs[:parts]), refs[parts:]
    width = context.shape[1]
    size = width // heads
    block = kv[0].shape[0]
    step = pl.program_id(0)
    spans = [pl.ds(pl.multiple_of(starts[e], block), block) for e in range(len(kv))]

    @pl.when(step == 0)
    def _():
        total[...] = jnp.zeros_like(total)

    scaled = d_mixed[...].astype(F32) * inverse[...]
    product = scaled * context[...].astype(F32)
    d_context = scaled.astype(BF16)
    d_context_t = scaled.T.astype(BF16)
    query_t = query[...].astype(F32).T.astype(BF16)
    for h in range(heads):
        own = slice(h * size, (h + 1) * size)
        other = slice(width + h * size, width + (h + 1) * size)
        mean = jnp.sum(product[:, own], -1, keepdims=True)
        changes, lows = [], []
        d_head = jnp.zeros((context.shape[0], size), F32)
        for e, span in enumerate(spans):
            d_weights = lax.dot_general(
                d_context[:, own], kv[e][:, other], (((1,), (1,)), ((), ())), preferred_element_type=F32
            )
            low = weights[h, :, span]
            change = (low.astype(F32) * (d_weights - mean)).astype(BF16)
            d_scores[0, h, :, span] = change
            d_head = d_head + jnp.dot(change, kv[e][:, own], preferred_element_type=F32)
            changes.append(change)
            lows.append(low)
        total[own, :] += jnp.dot(
            query_t[own, :], jnp.concatenate(changes, 1), preferred_element_type=F32
        )
        total[other, :] += jnp.dot(
            d_context_t[own, :], jnp.concatenate(lows, 1), preferred_element_type=F32
        )
        d_query[:, own] = scale * d_head

    @pl.when(step == pl.num_programs(0) - 1)
    def _():
        for e in range(len(kv)):
            half = d_kept.shape[0]
            target, index = (d_kept, e) if e < half else (d_sent, e - half)
            target[index] = total[:, e * block : (e + 1) * block].astype(BF16)


def attend_back(weights, kv, starts, context, d_mixed, inverse, query, scale):
    heads, rows, keys = weights.shape
    width = context.shape[1]
    block = kv[0].shape[1]
    tile = lambda i, *scalars: (i, 0)
    whole = lambda i, *scalars: (0, 0, 0)
    shape = (keys // block // 2, 2 * width, block)
    return pl.pallas_call(
        partial(attend_back_kernel, heads, scale, len(kv)),
        grid_spec=pltpu.PrefetchScalarGridSpec(
            num_scalar_prefetch=1,
            grid=(rows // TILE,),
            in_specs=[pl.BlockSpec((heads, TILE, keys), lambda i, *scalars: (0, i, 0))]
            + [pl.BlockSpec((TILE, width), tile)] * 4
            + [pl.BlockSpec(part.shape, whole) for part in kv],
            out_specs=[
                pl.BlockSpec((1, heads, TILE, keys), lambda i, *scalars: (0, 0, i, 0)),
                pl.BlockSpec((TILE, width), tile),
                pl.BlockSpec(shape, whole),
                pl.BlockSpec(shape, whole),
            ],
            scratch_shapes=[pltpu.VMEM((2 * width, keys), F32)],
        ),
        out_shape=[
            jax.ShapeDtypeStruct((1, heads, rows, keys), BF16),
            jax.ShapeDtypeStruct((rows, width), F32),
            jax.ShapeDtypeStruct(shape, BF16),
            jax.ShapeDtypeStruct(shape, BF16),
        ],
        cost_estimate=pl.CostEstimate(
            flops=10 * rows * keys * width, transcendentals=0, bytes_accessed=6 * heads * rows * keys
        ),
        name="attend_back",
    )(starts, weights, context, d_mixed, inverse, query, *kv)


def pack_kernel(lead, place, squared, *refs):
    vectors, placed, out = refs[:-2], refs[-2], refs[-1]
    out[...] = jnp.zeros_like(out)
    for i, vector in enumerate(vectors):
        out[i : i + 1, :] = vector[...]
    out[len(vectors) : len(vectors) + 1, :] = jnp.broadcast_to(squared[...], (1, out.shape[1]))
    for p in range((out.shape[0] - lead) // placed.shape[0]):

        @pl.when(place[0] == p)
        def _():
            first = lead + p * placed.shape[0]
            out[first : first + placed.shape[0], :] = placed[...]


def pack(vectors, squared, placed, place, places):
    width = vectors[0].shape[0]
    vmem = pl.BlockSpec(memory_space=pltpu.VMEM)
    rows = placed.reshape(-1, width)
    return pl.pallas_call(
        partial(pack_kernel, 8),
        in_specs=[pl.BlockSpec(memory_space=pltpu.SMEM)] + [vmem] * (len(vectors) + 2),
        out_specs=vmem,
        out_shape=jax.ShapeDtypeStruct((8 + places * rows.shape[0], width), F32),
        name="pack",
    )(place.reshape(1), squared.reshape(1, 1), *[v.reshape(1, width) for v in vectors], rows)


def per_device(
    inputs,
    teacher_states,
    lengths,
    prev_logits,
    w_query,
    w_key,
    w_value,
    w_output,
    w_inner,
    w_outer,
    bias_query,
    bias_value,
    bias_output,
    bias_inner,
    bias_outer,
    gain_first,
    shift_first,
    gain_second,
    shift_second,
):
    tokens = inputs[0]
    row_count, model_width = tokens.shape
    heads_local = prev_logits.shape[1]
    width_local = w_query.shape[1]
    score_scale = 1.0 / math.sqrt(width_local // heads_local)
    seq_length = lengths[0]
    ctx_place, tp_place = lax.axis_index(CTX_), lax.axis_index(TP_)
    tp_size = lax.axis_size(TP_)
    part_rows = row_count // tp_size

    qkv_shard = jnp.concatenate([w_query.T, w_key.T, w_value.T], 0)
    full_qkv = gather_weight(qkv_shard, 1)
    output_half = jnp.concatenate([w_output] + rows_moved(w_output), 0)
    row_pos = ctx_place * row_count + jnp.arange(row_count, dtype=jnp.int32)
    limits = jnp.minimum((row_pos[::TILE] // BLK + 1) * BLK, seq_length)

    def own_rows(array):
        return lax.dynamic_slice_in_dim(array, tp_place * part_rows, part_rows, 0)

    tokens_first = own_first(tokens)
    query_scaled = dot32(tokens_first, full_qkv[:width_local], ((1,), (1,))) + bias_query
    query_scaled = (query_scaled.astype(BF16).astype(F32) * score_scale).astype(BF16)
    bias_kv = jnp.concatenate([jnp.zeros_like(bias_value), bias_value])
    kv_local = (dot32(tokens_first, full_qkv[width_local:], ((1,), (1,))) + bias_kv).astype(BF16)
    kv_local, output_half = tie(kv_local, output_half)
    kv_all, query_scaled = gather_parts(kv_local, query_scaled)
    output_moved, join_output = gather_late(output_half, 1)
    starts = (ctx_place ^ jnp.asarray(ctx_order(), jnp.int32)) * row_count
    all_count = VectorSum(seq_length.astype(F32), (DP_,)).total()

    logits, weights, context, inverse = attend(
        query_scaled, kv_all, starts, prev_logits, limits, heads_local
    )
    context_turned = rows_turn(context)
    context_turned, output_moved, w_inner, w_outer = tie(
        context_turned, output_moved, w_inner, w_outer
    )
    full_output = join_output(output_moved)
    inner_moved, join_inner = gather_late(w_inner, 0)
    outer_moved, join_outer = gather_late(w_outer, 1)
    context_mine = jnp.concatenate(rows_exchange(jnp.split(context_turned, tp_size, 0)), 1)
    attended = own_first(dot32(context_mine, full_output, ((1,), (0,))))
    first_sum = own_rows(tokens).astype(F32) + attended + bias_output
    normed_first, spread_first, hidden = norm_forward(first_sum, gain_first, shift_first)
    hidden_first = own_first(hidden.astype(BF16))
    hidden_moved = rows_moved(hidden_first)
    full_inner, full_outer = join_inner(inner_moved), join_outer(outer_moved)
    hidden_low = jnp.concatenate([hidden_first] + hidden_moved, 0)
    pre_act = dot32(hidden_low, full_inner, ((1,), (0,))) + bias_inner
    act_low = jax.nn.gelu(pre_act, approximate=False).astype(BF16)
    fed = own_first(rows_sum(dot32(act_low, full_outer, ((1,), (0,)))))
    second_sum = hidden + fed + bias_outer
    normed_second, spread_second, result = norm_forward(second_sum, gain_second, shift_second)
    valid_rows = (own_rows(row_pos) < seq_length).astype(F32)
    deviation = result - own_rows(teacher_states[0]).astype(F32)
    local_squared = jnp.sum(valid_rows[:, None] * deviation * deviation)
    token_total = row_count * lax.axis_size(CTX_) * lax.axis_size(DP_)
    d_out = 2.0 * token_total / all_count * valid_rows[:, None] * deviation
    d_second, grad_gain_second, grad_shift_second = norm_backward(
        d_out, normed_second, spread_second, gain_second
    )
    grad_bias_outer = jnp.sum(d_second, 0)
    d_second_low = rows_gather(own_first(d_second.astype(BF16)))
    d_act = dot32(d_second_low, full_outer, ((1,), (1,)))
    gelu_back = jax.vjp(partial(jax.nn.gelu, approximate=False), pre_act)[1]
    d_pre = gelu_back(d_act)[0]
    grad_bias_inner = jnp.sum(d_pre, 0)
    d_pre_low = d_pre.astype(BF16)
    hidden_part = rows_sum(dot32(d_pre_low, full_inner, ((1,), (1,))))
    outer_sum = WeightSum(dot32(act_low, d_second_low, ((0,), (0,))), 1, True)
    inner_sum = WeightSum(dot32(hidden_low, d_pre_low, ((0,), (0,))), 0)
    d_hidden = d_second + own_first(hidden_part)
    d_first, grad_gain_first, grad_shift_first = norm_backward(
        d_hidden, normed_first, spread_first, gain_first
    )
    grad_bias_output = jnp.sum(d_first, 0)
    d_first_low = own_first(d_first.astype(BF16))
    d_context_mine = dot32(d_first_low, full_output, ((1,), (1,))).astype(BF16)
    d_context = jnp.concatenate(rows_exchange(jnp.split(d_context_mine, tp_size, 1)), 0)
    d_context = rows_turn(d_context)

    packed = (
        pack(
            [
                grad_bias_output,
                grad_bias_outer,
                grad_gain_first,
                grad_shift_first,
                grad_gain_second,
                grad_shift_second,
            ],
            local_squared,
            grad_bias_inner,
            tp_place,
            tp_size,
        )
    )
    early_sum = VectorSum(packed, (DP_, CTX_))
    d_context, outer_sum.moved, inner_sum.moved = tie(
        d_context, outer_sum.moved, inner_sum.moved
    )
    outer_sum.step()
    inner_sum.step()
    both_mine = jnp.concatenate([d_first_low, result.astype(BF16)], 1)
    both_mine, _ = tie(both_mine, d_context)
    both_moved = rows_moved(both_mine)
    d_scores, d_query, d_kept, d_sent = attend_back(
        weights, kv_all, starts, context, d_context, inverse, query_scaled, score_scale
    )
    d_sent, early_sum.moved = tie(d_sent, early_sum.moved)
    early_sum.step()
    d_kv = scatter_parts(d_kept, d_sent)
    d_query_low = d_query.astype(BF16)
    d_kv_low, inner_sum.moved, outer_sum.moved, early_sum.moved, *both_moved = tie(
        d_kv.astype(BF16), inner_sum.moved, outer_sum.moved, early_sum.moved, *both_moved
    )
    d_qkv_low = jnp.concatenate([d_query_low, d_kv_low.T], 1)
    tokens_part = rows_sum(dot32(rows_turn(d_qkv_low), full_qkv, ((1,), (0,))))
    inner_sum.step()
    outer_sum.step()
    early_sum.step()
    qkv_gradient = dot32(d_qkv_low, tokens_first, ((0,), (0,)))
    qkv_sum = WeightSum(qkv_gradient, 1, True)
    both = [both_mine] + both_moved
    d_first_all = jnp.concatenate([block[:, :model_width] for block in both], 0)
    output_gradient = dot32(context_turned, d_first_all, ((0,), (0,)))
    output_sum = WeightSum(output_gradient, 1, True)
    late_vector = jnp.concatenate([jnp.sum(d_query, 0), jnp.sum(d_kv[width_local:], 1)])
    late_sum = VectorSum(late_vector, (DP_, CTX_), True)
    grad_mine = (d_first + own_first(tokens_part)).astype(BF16)
    sums = (early_sum,)
    grad_mine, *moved = tie(grad_mine, *[one.moved for one in sums])
    for one, value in zip(sums, moved):
        one.moved = value
    early = early_sum.total()
    moved = []
    for e in range(1, tp_size):
        moved.append(flipped(early, TP_, e))
    early = [early] + moved
    while len(early) > 1:
        early = [left + right for left, right in zip(early[::2], early[1::2])]
    early = early[0]
    qkv_sum.step()
    output_sum.step()
    late_sum.step()
    output_sum.step()
    qkv_sum.step()
    grad_moved = rows_moved(grad_mine)
    inner_shard, outer_shard = inner_sum.total(), outer_sum.total()
    result_all = rows_place([block[:, model_width:] for block in both]).astype(F32)
    grad_moved[-1], inner_shard, outer_shard, result_all = tie(
        grad_moved[-1], inner_shard, outer_shard, result_all
    )
    grad_inputs = rows_place([grad_mine] + grad_moved).astype(F32)
    output_shard = output_sum.total()
    shard_qkv = qkv_sum.total()
    loss_value = early[6, 0] / (all_count * model_width)
    inner_rows = grad_bias_inner.shape[0] // model_width
    sum_bias_inner = lax.dynamic_slice_in_dim(early, 8 + tp_place * inner_rows, inner_rows, 0).reshape(-1)
    late = late_sum.total()
    return (
        result_all[None],
        logits,
        loss_value,
        grad_inputs[None],
        d_scores,
        shard_qkv[:width_local].T,
        shard_qkv[width_local : 2 * width_local].T,
        shard_qkv[2 * width_local :].T,
        output_shard,
        inner_shard,
        outer_shard,
        late[:width_local],
        late[width_local:],
        early[0],
        sum_bias_inner,
        early[1],
        early[2],
        early[3],
        early[4],
        early[5],
    )


def solution(mesh):
    placed = (
        P(DP_, CTX_, None),
        P(DP_, CTX_, None),
        P(DP_),
        P(DP_, TP_, CTX_, None),
        P(DP_, TP_),
        P(DP_, TP_),
        P(DP_, TP_),
        P(TP_, DP_),
        P(DP_, TP_),
        P(TP_, DP_),
        P(TP_),
        P(TP_),
        P(),
        P(TP_),
        P(),
        P(),
        P(),
        P(),
        P(),
    )
    return jax.shard_map(
        per_device,
        mesh=mesh,
        in_specs=placed,
        out_specs=(
            P(DP_, CTX_, None),
            P(DP_, TP_, CTX_, None),
            P(),
            P(DP_, CTX_, None),
            P(DP_, TP_, CTX_, None),
            P(DP_, TP_),
            P(DP_, TP_),
            P(DP_, TP_),
            P(TP_, DP_),
            P(DP_, TP_),
            P(TP_, DP_),
            P(TP_),
            P(TP_),
            P(),
            P(TP_),
            P(),
            P(),
            P(),
            P(),
            P(),
        ),
        check_vma=False,
    )
```
